512 devices in a mesh: gx: 32 (over x, y), gy: 16 (over z, core).
Axes of the slice: x: 4, y: 8, z: 8, core: 2. Of those that a mesh axis runs over, the one named last changes fastest.
Arguments:
- enthalpy: float32 [128, 256, 2048], P(None, 'gx', 'gy'), may hold values from -6 to 6
- velocity_init: float32 [2, 256, 2048], P(None, 'gx', 'gy'), may hold values from -0.35 to 0.35
- thickness: float32 [256, 2048], P('gx', 'gy'), may hold values from 0.3 to 3
- surface: float32 [256, 2048], P('gx', 'gy'), may hold values from -24 to 24
- friction: float32 [256, 2048], P('gx', 'gy'), may hold values from 0.3 to 10
- kappa: float32 [129], replicated, may hold values from 0.3 to 10
- surface_enthalpy: float32 [256, 2048], P('gx', 'gy'), may hold values from -6 to 6
- geo_flux: float32 [256, 2048], P('gx', 'gy'), may hold values from 0.2 to 1.5
- ice_mask: int32 [256, 2048], P('gx', 'gy'), may hold values 0 or 1
- grounded: int32 [256, 2048], P('gx', 'gy'), may hold values 0 or 1
- boundary_code: int32 [256, 2048], P('gx', 'gy'), may hold values from 0 to 2, as said below
Outputs:
- enthalpy_new: float32 [128, 256, 2048], P(None, 'gx', 'gy')
- velocity: float32 [2, 256, 2048], P(None, 'gx', 'gy')
The draws below stay inside these ranges and needn't reach their ends.
Inputs may be any that keep to these rules, and one draw needn't show every extreme that they name: `boundary_code`: 0 marks a free cell, 1 a cell held at rest, 2 a cell whose velocity stays at its given value.
All inputs are finite; a program needn't handle non-finite values. No bound on the sum of `ice_mask` or of `grounded` on one device may be relied on, other than what follows from the above.
Results may differ from the reference program's by a relative error of at most 0.00018.
Values sent between devices are 32-bit elements; how exact they have to be, the bound alone decides.
No kernel may reach another device: no remote copies, remote signals or barrier semaphores. Data moves between devices by JAX's collectives and lax.ppermute only.
A program may use at most 64 MiB of HBM per device.

```python
import math
import jax
import jax.numpy as jnp
from jax import lax

NZ = 128
SUBSTEPS = 2
PICARD = 2
KRYLOV = 6
NX = 256
NY = 2048


def draw_boundary_code(key, part):
    raw_codes = jax.random.randint(key, (NX, NY), 0, 8)
    return jnp.where(raw_codes == 0, 1, jnp.where(raw_codes == 1, 2, 0)).astype(jnp.int32)


def plant(values, stream_key, low, high):
    shape = values.shape
    place = [jax.random.randint(jax.random.fold_in(stream_key, axis), (), 0, shape[axis]) for axis in range(len(shape))]
    values = values.at[tuple(place)].set(low)
    longest = shape.index(max(shape))
    place[longest] = (place[longest] + 1) % shape[longest]
    return values.at[tuple(place)].set(high)


def shard_levels(rng, shape, cuts, least, largest):
    level, own = 1.0, jax.random.fold_in(rng, 6)
    for axis_at, blocks in cuts:
        draws = jnp.exp(jax.random.uniform(jax.random.fold_in(own, axis_at), (blocks,), jnp.float32, least / len(cuts), largest / len(cuts)))
        level = level * jnp.repeat(draws, shape[axis_at] // blocks).reshape([-1 if axis == axis_at else 1 for axis in range(len(shape))])
    return level


def normal_values(key, extent, scale, bound, shards=(), held_as=jnp.bfloat16):
    drawn = scale * jax.random.normal(key, extent, jnp.float32)
    if shards:
        drawn = drawn * shard_levels(key, extent, shards, -0.22, 0.18)
    return jnp.clip(drawn, -bound, bound).astype(held_as)


def setup_inputs(seed: int = 0) -> dict:
    keys = jax.random.split(jax.random.key(seed), 12)
    enthalpy = normal_values(keys[0], (NZ, NX, NY), 1.0, 6.0, ((1, 32), (2, 16)), jnp.float32)
    velocity_init = jnp.clip(jax.random.uniform(keys[1], (2, NX, NY), jnp.float32, -0.35, 0.35) * shard_levels(keys[1], (2, NX, NY), ((1, 32), (2, 16)), -0.4, 0.0), -0.35, 0.35)
    thickness = jnp.clip(jnp.exp(math.log(3.0) - 2.3025851 * jax.random.uniform(keys[2], (NX, NY), jnp.float32) ** shard_levels(keys[2], (NX, NY), ((0, 32), (1, 16)), -0.2, 0.2)), 0.3, 3.0)
    surface = normal_values(keys[3], (NX, NY), 4.0, 24.0, ((0, 32), (1, 16)), jnp.float32)
    friction = jnp.clip(jnp.exp(math.log(10.0) - 3.506558 * jax.random.uniform(keys[4], (NX, NY), jnp.float32) ** shard_levels(keys[4], (NX, NY), ((0, 32), (1, 16)), -0.2, 0.2)), 0.3, 10.0)
    kappa = jnp.clip(jnp.exp(jax.random.uniform(keys[5], (NZ + 1,), jnp.float32, math.log(0.3), math.log(10.0))), 0.3, 10.0)
    surface_enthalpy = normal_values(keys[6], (NX, NY), 1.0, 6.0, ((0, 32), (1, 16)), jnp.float32)
    geo_flux = jnp.clip(0.2 + 1.3 * jax.random.uniform(keys[7], (NX, NY), jnp.float32) ** shard_levels(keys[7], (NX, NY), ((0, 32), (1, 16)), -0.2, 0.2), 0.2, 1.5)
    ice_mask = plant((jax.random.randint(keys[8], (NX, NY), 0, 5) < 4).astype(jnp.int32), jax.random.fold_in(keys[8], 1), 0, 1)
    grounded = plant((jax.random.randint(keys[9], (NX, NY), 0, 3) < 2).astype(jnp.int32), jax.random.fold_in(keys[9], 1), 0, 1)
    boundary_code = draw_boundary_code(jax.random.fold_in(keys[11], 71), 0)
    return dict(enthalpy=enthalpy, velocity_init=velocity_init, thickness=thickness, surface=surface, friction=friction, kappa=kappa, surface_enthalpy=surface_enthalpy, geo_flux=geo_flux, ice_mask=ice_mask, grounded=grounded, boundary_code=boundary_code)


soften = 0.3
shelf_drag = 0.2
strain_floor = 0.01

def upwind_sweep(values, courant, axis):
    length = values.shape[axis]

    def window(array, start_cut, end_cut):
        return lax.slice_in_dim(array, start_cut, length - end_cut, axis=axis)
    face_speed = 0.5 * (window(courant, 1, 2) + window(courant, 2, 1))
    minus_one = window(values, 0, 3)
    here_cell = window(values, 1, 2)
    plus_one = window(values, 2, 1)
    plus_two = window(values, 3, 0)
    positive = jnp.maximum(face_speed, 0.0)
    negative = jnp.minimum(face_speed, 0.0)
    face_flux = positive * (here_cell + 0.25 * (1.0 - positive) * (plus_one - minus_one))
    face_flux = face_flux + negative * (plus_one - 0.25 * (1.0 + negative) * (plus_two - here_cell))
    count = face_flux.shape[axis]
    return lax.slice_in_dim(face_flux, 1, count, axis=axis) - lax.slice_in_dim(face_flux, 0, count - 1, axis=axis)

def advect(padded, courant_x, courant_y):
    row_count = padded.shape[1]
    col_count = padded.shape[2]
    along_x = upwind_sweep(padded[:, :, 2:col_count - 2], courant_x[None, :, 2:col_count - 2], 1)
    along_y = upwind_sweep(padded[:, 2:row_count - 2, :], courant_y[None, 2:row_count - 2, :], 2)
    return padded[:, 2:row_count - 2, 2:col_count - 2] - along_x - along_y

def column_inverses(kappa):
    levels = kappa.shape[0] - 1
    nothing = jnp.zeros((1,), kappa.dtype)
    lower_band = jnp.concatenate([nothing, -kappa[1:levels]])
    upper_band = jnp.concatenate([-kappa[1:levels], nothing])
    floating = 1.0 + kappa[:levels] + kappa[1:]
    bottom = lax.broadcasted_iota(jnp.int32, (levels,), 0) == levels - 1
    on_bed = jnp.where(bottom, floating - kappa[levels], floating)
    identity = jnp.eye(levels, dtype=kappa.dtype)
    inverse_bed = lax.linalg.tridiagonal_solve(lower_band, on_bed, upper_band, identity)
    inverse_shelf = lax.linalg.tridiagonal_solve(lower_band, floating, upper_band, identity)
    return (inverse_bed, inverse_shelf)

def diffuse(moved, inverse_bed, inverse_shelf, kappa, ice_cols, bed_cols, surface_heat, heat_flux):
    levels = moved.shape[0]
    depth_index = lax.broadcasted_iota(jnp.int32, (levels, 1, 1), 0)
    right_side = moved + jnp.where(depth_index == 0, kappa[0] * surface_heat[None], 0.0)
    right_side = right_side + jnp.where(depth_index == levels - 1, bed_cols[None] * heat_flux[None], 0.0)
    columns = right_side.reshape(levels, -1)
    solved_bed = jnp.dot(inverse_bed, columns, precision=lax.Precision.HIGHEST).reshape(moved.shape)
    solved_shelf = jnp.dot(inverse_shelf, columns, precision=lax.Precision.HIGHEST).reshape(moved.shape)
    solved = jnp.where(bed_cols[None] > 0.5, solved_bed, solved_shelf)
    return jnp.where(ice_cols[None] > 0.5, solved, moved)

def corner_mean(array):
    return 0.25 * (array[:-1, :-1] + array[1:, :-1] + array[:-1, 1:] + array[1:, 1:])

def diff_rows(array):
    return 0.5 * (array[1:, :-1] - array[:-1, :-1] + (array[1:, 1:] - array[:-1, 1:]))

def diff_cols(array):
    return 0.5 * (array[:-1, 1:] - array[:-1, :-1] + (array[1:, 1:] - array[1:, :-1]))

def back_rows(array):
    return 0.5 * (array[:-1, :-1] + array[:-1, 1:] - array[1:, :-1] - array[1:, 1:])

def back_cols(array):
    return 0.5 * (array[:-1, :-1] + array[1:, :-1] - array[:-1, 1:] - array[1:, 1:])

def strains(padded):
    stretch_x = diff_rows(padded[0])
    stretch_y = diff_cols(padded[1])
    shear_rate = 0.5 * (diff_cols(padded[0]) + diff_rows(padded[1]))
    return (stretch_x, stretch_y, shear_rate)

def viscous_weight(rates, thick_corner, stiff_corner):
    stretch_x, stretch_y, shear_rate = rates
    square = stretch_x * stretch_x + stretch_y * stretch_y + stretch_x * stretch_y + shear_rate * shear_rate
    return 0.5 * stiff_corner * thick_corner * jnp.power(square + strain_floor, -1.0 / 3.0)

def stress_image(rates, weight, center, drag_term):
    stretch_x, stretch_y, shear_rate = rates
    stress_x = weight * (4.0 * stretch_x + 2.0 * stretch_y)
    stress_y = weight * (4.0 * stretch_y + 2.0 * stretch_x)
    shear_stress = 2.0 * weight * shear_rate
    first = back_rows(stress_x) + back_cols(shear_stress) + drag_term * center[0]
    second = back_rows(shear_stress) + back_cols(stress_y) + drag_term * center[1]
    return jnp.stack([first, second])

def pad_one(array):
    return jnp.pad(array, ((0, 0), (1, 1), (1, 1)))

def reference(enthalpy, velocity_init, thickness, surface, friction, kappa, surface_enthalpy, geo_flux, ice_mask, grounded, boundary_code):
    ice_cols = ice_mask.astype(jnp.float32)
    bed_cols = grounded.astype(jnp.float32)
    inverse_bed, inverse_shelf = column_inverses(kappa)
    courant = jnp.pad(velocity_init, ((0, 0), (2, 2), (2, 2)))

    def move_level(level_values):
        padded = jnp.pad(level_values, ((2, 2), (2, 2)))[None]
        return advect(padded, courant[0], courant[1])[0]
    current = enthalpy
    for substep in range(SUBSTEPS):
        moved = lax.map(move_level, current)
        current = diffuse(moved, inverse_bed, inverse_shelf, kappa, ice_cols, bed_cols, surface_enthalpy, geo_flux)
    stiffness = jnp.exp(-soften * jnp.mean(current, axis=0))
    statics = pad_one(jnp.stack([thickness, stiffness, surface]))
    thick_corner = corner_mean(statics[0])
    stiff_corner = corner_mean(statics[1])
    heights = statics[2]
    driving = jnp.stack([-thickness * 0.5 * (heights[2:, 1:-1] - heights[:-2, 1:-1]), -thickness * 0.5 * (heights[1:-1, 2:] - heights[1:-1, :-2])])
    free_cells = (boundary_code == 0) & (ice_mask == 1)
    held_cells = free_cells | (boundary_code == 2)
    projector = free_cells.astype(jnp.float32)[None]
    drag_term = jnp.where(grounded == 1, friction, 0.0) + shelf_drag
    velocity = jnp.where(held_cells[None], velocity_init, 0.0)
    for picard_step in range(PICARD):
        rates = strains(pad_one(velocity))
        weight = viscous_weight(rates, thick_corner, stiff_corner)
        residual = projector * (driving - stress_image(rates, weight, velocity, drag_term))
        direction = residual
        change = jnp.zeros_like(velocity)
        norm_now = jnp.sum(residual * residual)
        for krylov_step in range(KRYLOV):
            imaged = projector * stress_image(strains(pad_one(direction)), weight, direction, drag_term)
            step_size = norm_now / jnp.sum(direction * imaged)
            change = change + step_size * direction
            residual = residual - step_size * imaged
            norm_next = jnp.sum(residual * residual)
            direction = residual + norm_next / norm_now * direction
            norm_now = norm_next
        velocity = velocity + change
    return (current, velocity)
```

```python
import functools

import jax
import jax.numpy as jnp
from jax import lax
from jax.experimental import pallas as pl
from jax.experimental.pallas import tpu as pltpu
from jax.sharding import Mesh
from jax.sharding import PartitionSpec as P

SUBSTEPS = 2
PICARD = 2
KRYLOV = 6
TORUS = (4, 8, 8, 2)
GX_GY = ("gx_0", "gx_1", "gy_0", "gy_1")
GX = ("gx_0", "gx_1")
GY = ("gy_0", "gy_1")


soften = 0.3
shelf_drag = 0.2
strain_floor = 0.01

MIDDLE = 17.0
RADIUS = 17.0
PIVOT_FLOOR = 2e-4
OWN = 16
SIDE = 64


def with_halo(shard, sides, width):
    for axis, dim in sides:
        size, length = (lax.axis_size(axis), shard.shape[dim])
        up = [(i, (i + 1) % size) for i in range(size - 1)]
        down = [(j, i) for i, j in up]
        last = lax.slice_in_dim(shard, length - width, length, axis=dim)
        first = lax.slice_in_dim(shard, 0, width, axis=dim)
        before = lax.ppermute(last, axis, up)
        after = lax.ppermute(first, axis, down)
        shard = jnp.concatenate([before, shard, after], axis=dim)
    return shard


def one_axis_at_a_time(shard, axes):
    return functools.reduce(lax.psum, axes, shard)


def with_halo_2(shard, sides, width):
    edges = {}
    for axis, dim in sides:
        size, length = (lax.axis_size(axis), shard.shape[dim])
        up = [(i, (i + 1) % size) for i in range(size - 1)]
        last = lax.slice_in_dim(shard, length - width, length, axis=dim)
        first = lax.slice_in_dim(shard, 0, width, axis=dim)
        edges[dim] = (
            lax.ppermute(last, axis, up),
            lax.ppermute(first, axis, [(b, a) for a, b in up]),
        )
    done = []
    for _, dim in sides:
        low, high = edges[dim]
        around = [(width, width) if d in done else (0, 0) for d in range(shard.ndim)]
        shard = jnp.concatenate([jnp.pad(low, around), shard, jnp.pad(high, around)], axis=dim)
        done.append(dim)
    return shard


def upwind_sweep(values, courant, axis):
    length = values.shape[axis]

    def window(array, start_cut, end_cut):
        return lax.slice_in_dim(array, start_cut, length - end_cut, axis=axis)

    face_speed = 0.5 * (window(courant, 1, 2) + window(courant, 2, 1))
    minus_one = window(values, 0, 3)
    here_cell = window(values, 1, 2)
    plus_one = window(values, 2, 1)
    plus_two = window(values, 3, 0)
    positive = jnp.maximum(face_speed, 0.0)
    negative = jnp.minimum(face_speed, 0.0)
    face_flux = positive * (here_cell + 0.25 * (1.0 - positive) * (plus_one - minus_one))
    face_flux = face_flux + negative * (plus_one - 0.25 * (1.0 + negative) * (plus_two - here_cell))
    count = face_flux.shape[axis]
    return lax.slice_in_dim(face_flux, 1, count, axis=axis) - lax.slice_in_dim(
        face_flux, 0, count - 1, axis=axis
    )


def advect(padded, courant_x, courant_y):
    row_count = padded.shape[1]
    col_count = padded.shape[2]
    along_x = upwind_sweep(
        padded[:, :, 2 : col_count - 2], courant_x[None, :, 2 : col_count - 2], 1
    )
    along_y = upwind_sweep(
        padded[:, 2 : row_count - 2, :], courant_y[None, 2 : row_count - 2, :], 2
    )
    return padded[:, 2 : row_count - 2, 2 : col_count - 2] - along_x - along_y


def diffuse(moved, inverse_bed, inverse_shelf, kappa, ice_cols, bed_cols, surface_heat, heat_flux):
    levels = moved.shape[0]
    depth_index = lax.broadcasted_iota(jnp.int32, (levels, 1, 1), 0)
    right_side = moved + jnp.where(depth_index == 0, kappa[0] * surface_heat[None], 0.0)
    right_side = right_side + jnp.where(
        depth_index == levels - 1, bed_cols[None] * heat_flux[None], 0.0
    )
    columns = right_side.reshape(levels, -1)
    solved_bed = jnp.dot(inverse_bed, columns, precision=lax.Precision.HIGHEST).reshape(moved.shape)
    solved_shelf = jnp.dot(inverse_shelf, columns, precision=lax.Precision.HIGHEST).reshape(
        moved.shape
    )
    solved = jnp.where(bed_cols[None] > 0.5, solved_bed, solved_shelf)
    return jnp.where(ice_cols[None] > 0.5, solved, moved)


def corner_mean(array):
    return 0.25 * (array[:-1, :-1] + array[1:, :-1] + array[:-1, 1:] + array[1:, 1:])


def diff_rows(array):
    return 0.5 * (array[1:, :-1] - array[:-1, :-1] + (array[1:, 1:] - array[:-1, 1:]))


def diff_cols(array):
    return 0.5 * (array[:-1, 1:] - array[:-1, :-1] + (array[1:, 1:] - array[1:, :-1]))


def back_rows(array):
    return 0.5 * (array[:-1, :-1] + array[:-1, 1:] - array[1:, :-1] - array[1:, 1:])


def back_cols(array):
    return 0.5 * (array[:-1, :-1] + array[1:, :-1] - array[:-1, 1:] - array[1:, 1:])


def strains(padded):
    stretch_x = diff_rows(padded[0])
    stretch_y = diff_cols(padded[1])
    shear_rate = 0.5 * (diff_cols(padded[0]) + diff_rows(padded[1]))
    return (stretch_x, stretch_y, shear_rate)


def viscous_weight(rates, thick_corner, stiff_corner):
    stretch_x, stretch_y, shear_rate = rates
    square = (
        stretch_x * stretch_x
        + stretch_y * stretch_y
        + stretch_x * stretch_y
        + shear_rate * shear_rate
    )
    return 0.5 * stiff_corner * thick_corner * jnp.power(square + strain_floor, -1.0 / 3.0)


def stress_image(rates, weight, center, drag_term):
    stretch_x, stretch_y, shear_rate = rates
    stress_x = weight * (4.0 * stretch_x + 2.0 * stretch_y)
    stress_y = weight * (4.0 * stretch_y + 2.0 * stretch_x)
    shear_stress = 2.0 * weight * shear_rate
    first = back_rows(stress_x) + back_cols(shear_stress) + drag_term * center[0]
    second = back_rows(shear_stress) + back_cols(stress_y) + drag_term * center[1]
    return jnp.stack([first, second])


def apply_field(direction, weight, drag_term, projector):
    padded = with_halo(direction, ((GX, 1), (GY, 2)), 1)
    return projector * stress_image(strains(padded), weight, direction, drag_term)


def inverse_kernel(kappa_ref, bed_ref, shelf_ref):
    levels = kappa_ref.shape[1]
    above = kappa_ref[0:8, :]
    below = kappa_ref[8:16, :]
    lane = lax.broadcasted_iota(jnp.int32, (8, levels), 1)
    rows = lax.broadcasted_iota(jnp.int32, (levels, levels), 0)
    cols = lax.broadcasted_iota(jnp.int32, (levels, levels), 1)
    floating = 1.0 + above + below
    on_bed = jnp.where(lane == levels - 1, 1.0 + above, floating)
    for diagonal, out_ref in ((on_bed, bed_ref), (floating, shelf_ref)):
        low = jnp.where(lane == 0, 0.0, -above)
        high = jnp.where(lane == levels - 1, 0.0, -below)
        mid = diagonal
        right = jnp.where(rows == cols, 1.0, 0.0)
        step = 1
        while step < levels:
            back = levels - step
            down = -low / pltpu.roll(mid, step, 1)
            up = -high / pltpu.roll(mid, back, 1)
            mid = mid + down * pltpu.roll(high, step, 1) + up * pltpu.roll(low, back, 1)
            low = down * pltpu.roll(low, step, 1)
            high = up * pltpu.roll(high, back, 1)
            right = (
                right
                + down[0:1] * pltpu.roll(right, step, 1)
                + up[0:1] * pltpu.roll(right, back, 1)
            )
            step *= 2
        out_ref[...] = right / mid[0:1]


def column_inverses(kappa):
    levels = kappa.shape[0] - 1
    above = jnp.broadcast_to(kappa[None, :levels], (8, levels))
    below = jnp.broadcast_to(kappa[None, 1:], (8, levels))
    shape = jax.ShapeDtypeStruct((levels, levels), kappa.dtype)
    return pl.pallas_call(inverse_kernel, out_shape=(shape, shape), name="column_inverses")(
        jnp.concatenate([above, below], axis=0)
    )


def next_row(array):
    return pltpu.roll(array, array.shape[0] - 1, 0)


def next_col(array):
    return pltpu.roll(array, array.shape[1] - 1, 1)


def last_row(array):
    return pltpu.roll(array, 1, 0)


def last_col(array):
    return pltpu.roll(array, 1, 1)


def corner_rates(u, v):
    u_next = next_col(u)
    v_next = next_col(v)
    u_sum, u_diff = (u + u_next, u_next - u)
    v_sum, v_diff = (v + v_next, v_next - v)
    along = next_row(u_sum) - u_sum
    across = v_diff + next_row(v_diff)
    shear = u_diff + next_row(u_diff) + (next_row(v_sum) - v_sum)
    return (along, across, shear)


def stress_back(rates, half_weight):
    along, across, shear = rates
    stress_x = half_weight * (2.0 * along + across)
    stress_y = half_weight * (2.0 * across + along)
    stress_s = 0.5 * half_weight * shear
    x_before = last_col(stress_x)
    y_before = last_col(stress_y)
    s_before = last_col(stress_s)
    x_sum, s_diff = (stress_x + x_before, s_before - stress_s)
    s_sum, y_diff = (stress_s + s_before, y_before - stress_y)
    first = last_row(x_sum + s_diff) + (s_diff - x_sum)
    second = last_row(s_sum + y_diff) + (y_diff - s_sum)
    return (first, second)


def half_weights(rates, corner_product):
    along, across, shear = rates
    square = 0.25 * (along * along + across * across + along * across) + 0.0625 * shear * shear
    return corner_product * jnp.exp(jnp.log(square + strain_floor) * (-1.0 / 3.0))


def krylov_basis(u, v, drag, driving, corner_product, own_row, keep):
    free = drag > 0.0
    rates = corner_rates(u, v)
    half_weight = half_weights(rates, corner_product)
    first, second = stress_back(rates, half_weight)
    r_u = jnp.where(free, driving[0] - first - drag * u, 0.0)
    r_v = jnp.where(free, driving[1] - second - drag * v, 0.0)

    def own(array):
        return array[own_row : own_row + 8, :128]

    basis_u, basis_v = ([r_u], [r_v])
    own_basis, own_image = ([(own(r_u), own(r_v))], [])
    keep(0, r_u, r_v)
    for k in range(KRYLOV):
        b_u, b_v = (basis_u[k], basis_v[k])
        first, second = stress_back(corner_rates(b_u, b_v), half_weight)
        a_u = jnp.where(free, first, 0.0) + drag * b_u
        a_v = jnp.where(free, second, 0.0) + drag * b_v
        own_image.append((own(a_u), own(a_v)))
        if k + 1 < KRYLOV:
            scale = (1.0 if k == 0 else 2.0) / RADIUS
            n_u = scale * a_u - (scale * MIDDLE) * b_u
            n_v = scale * a_v - (scale * MIDDLE) * b_v
            if k > 0:
                n_u = n_u - basis_u[k - 1]
                n_v = n_v - basis_v[k - 1]
            basis_u.append(n_u)
            basis_v.append(n_v)
            own_basis.append((own(n_u), own(n_v)))
            keep(k + 1, n_u, n_v)
    products = []
    for i in range(KRYLOV):
        for j in range(i, KRYLOV):
            products.append(
                own_basis[i][0] * own_image[j][0] + own_basis[i][1] * own_image[j][1]
            )
    for i in range(KRYLOV):
        products.append(own_basis[i][0] * own_basis[0][0] + own_basis[i][1] * own_basis[0][1])
    return products


def write_sums(products, out_ref):
    count = out_ref.shape[0]
    lines = [jnp.sum(p, axis=0, keepdims=True) for p in products]
    lines.append(jnp.zeros((128 - len(lines), 128), jnp.float32))
    table = jnp.concatenate(lines, axis=0)
    out_ref[...] = lax.dot_general(
        jnp.ones((count, 128), jnp.float32),
        table,
        (((1,), (1,)), ((), ())),
        precision=lax.Precision.HIGHEST,
        preferred_element_type=jnp.float32,
    )


def small_solve(parts):
    sums = jnp.sum(parts, axis=0, keepdims=True)
    at = lambda k: sums[:, k : k + 1]
    full = {}
    k = 0
    for i in range(KRYLOV):
        for j in range(i, KRYLOV):
            full[i, j] = at(k)
            k += 1
    norm = [lax.rsqrt(full[i, i]) for i in range(KRYLOV)]
    right = [at(k + i) * norm[i] for i in range(KRYLOV)]
    lower, pivots, least = ({}, [], None)
    scaled = {}
    for j in range(KRYLOV):
        pivot = jnp.ones_like(right[0])
        for m in range(j):
            pivot = pivot - scaled[j, m] * lower[j, m]
        pivots.append(pivot)
        least = pivot if least is None else jnp.minimum(least, pivot)
        inverse = 1.0 / pivot
        for i in range(j + 1, KRYLOV):
            value = full[j, i] * norm[i] * norm[j]
            for m in range(j):
                value = value - scaled[i, m] * lower[j, m]
            scaled[i, j] = value
            lower[i, j] = value * inverse
    forward = []
    for i in range(KRYLOV):
        value = right[i]
        for m in range(i):
            value = value - lower[i, m] * forward[m]
        forward.append(value)
    answer = [None] * KRYLOV
    for i in reversed(range(KRYLOV)):
        value = forward[i] / pivots[i]
        for m in range(i + 1, KRYLOV):
            value = value - lower[m, i] * answer[m]
        answer[i] = value
    return ([a * n for a, n in zip(answer, norm)], least)


def first_picard_kernel(
    place_ref, grid_ref, mine_ref, left_ref, right_ref, basis_ref, fixed_ref, sums_ref
):
    rows = mine_ref.shape[1]
    lane = lax.broadcasted_iota(jnp.int32, (rows, 128), 1)
    row = lax.broadcasted_iota(jnp.int32, (rows, 128), 0) + (place_ref[0] * 8 - OWN)
    row_in = (row >= 0) & (row < grid_ref[0] * 8)
    from_right = lane < SIDE
    col = place_ref[1] + jnp.where(from_right, 1, -1)
    side_in = row_in & (col >= 0) & (col < grid_ref[1])

    def field(k):
        side = jnp.where(from_right, right_ref[k], left_ref[k])
        return jnp.concatenate(
            [jnp.where(row_in, mine_ref[k], 0.0), jnp.where(side_in, side, 0.0)], axis=1
        )

    u, v, drag, thick, stiff, surface = (field(k) for k in range(6))
    t_sum = thick + next_col(thick)
    s_sum = stiff + next_col(stiff)
    corner_product = (1.0 / 64.0) * (t_sum + next_row(t_sum)) * (s_sum + next_row(s_sum))
    driving = (
        -thick * 0.5 * (next_row(surface) - last_row(surface)),
        -thick * 0.5 * (next_col(surface) - last_col(surface)),
    )
    kept = slice(OWN - 8, OWN + 16)

    def keep(k, b_u, b_v):
        basis_ref[2 * k] = b_u[kept]
        basis_ref[2 * k + 1] = b_v[kept]

    for k, value in enumerate((u, v, drag, corner_product, driving[0], driving[1])):
        fixed_ref[k] = value[kept]
    products = krylov_basis(u, v, drag, driving, corner_product, OWN, keep)
    write_sums(products, sums_ref)


def second_picard_kernel(
    parts_ref, basis_ref, fixed_ref, next_ref, velocity_ref, sums_ref, least_ref
):
    answer, least = small_solve(parts_ref[...])
    u, v = (fixed_ref[0], fixed_ref[1])
    for k in range(KRYLOV):
        u = u + answer[k] * basis_ref[2 * k]
        v = v + answer[k] * basis_ref[2 * k + 1]
    velocity_ref[0] = u[8:16, :128]
    velocity_ref[1] = v[8:16, :128]
    least_ref[...] = jnp.broadcast_to(least, least_ref.shape)

    def keep(k, b_u, b_v):
        next_ref[2 * k] = b_u[8:16, :128]
        next_ref[2 * k + 1] = b_v[8:16, :128]

    driving = (fixed_ref[4], fixed_ref[5])
    products = krylov_basis(u, v, fixed_ref[2], driving, fixed_ref[3], 8, keep)
    write_sums(products, sums_ref)


def last_kernel(parts_ref, basis_ref, velocity_ref, least_ref, out_ref, worst_ref):
    answer, least = small_solve(parts_ref[...])
    u, v = (velocity_ref[0], velocity_ref[1])
    for k in range(KRYLOV):
        u = u + answer[k] * basis_ref[2 * k]
        v = v + answer[k] * basis_ref[2 * k + 1]
    out_ref[0] = u
    out_ref[1] = v
    worst_ref[...] = jnp.minimum(least_ref[...], least)


def over_all(sums):
    count = lax.axis_size(GX)
    part = lax.all_to_all(sums, GY, 0, 0, tiled=True)
    part = jnp.broadcast_to(jnp.sum(part, axis=0, keepdims=True), (count, 128))
    return lax.all_to_all(part, GX, 0, 0, tiled=True)


def shifted(array, axis, by):
    size = lax.axis_size(axis)
    return lax.ppermute(array, axis, [(i, (i + by) % size) for i in range(size)])


def momentum(fields):
    f32 = jnp.float32
    below = [shifted(fields, GX, by) for by in (2, 1)]
    above = [shifted(fields, GX, -by) for by in (1, 2)]
    mine = jnp.concatenate(below + [fields] + above, axis=1)
    left = shifted(mine, GY, 1)
    right = shifted(mine, GY, -1)
    gx, gy = (lax.axis_size(GX), lax.axis_size(GY))
    place = jnp.stack([lax.axis_index(GX), lax.axis_index(GY)]).astype(jnp.int32)
    grid = jnp.array([gx, gy], jnp.int32)
    smem = pl.BlockSpec(memory_space=pltpu.SMEM)
    vmem = pl.BlockSpec(memory_space=pltpu.VMEM)
    struct = jax.ShapeDtypeStruct
    basis, fixed, sums = pl.pallas_call(
        first_picard_kernel,
        out_shape=(
            struct((2 * KRYLOV, 24, 256), f32),
            struct((6, 24, 256), f32),
            struct((gy, 128), f32),
        ),
        in_specs=[smem, smem, vmem, vmem, vmem],
        out_specs=(vmem, vmem, vmem),
        name="first_picard",
    )(place, grid, mine, left, right)
    basis, velocity, sums, least = pl.pallas_call(
        second_picard_kernel,
        out_shape=(
            struct((2 * KRYLOV, 8, 128), f32),
            struct((2, 8, 128), f32),
            struct((gy, 128), f32),
            struct((8, 128), f32),
        ),
        name="second_picard",
    )(over_all(sums), basis, fixed)
    return pl.pallas_call(
        last_kernel,
        out_shape=(struct((2, 8, 128), f32), struct((8, 128), f32)),
        name="last_picard",
    )(over_all(sums), basis, velocity, least)


def plain_picard(velocity, thickness, stiffness, surface, drag_term, projector):
    statics = with_halo(jnp.stack([thickness, stiffness, surface]), ((GX, 1), (GY, 2)), 1)
    thick_corner = corner_mean(statics[0])
    stiff_corner = corner_mean(statics[1])
    heights = statics[2]
    driving = jnp.stack(
        [
            -thickness * 0.5 * (heights[2:, 1:-1] - heights[:-2, 1:-1]),
            -thickness * 0.5 * (heights[1:-1, 2:] - heights[1:-1, :-2]),
        ]
    )

    def total(array):
        return one_axis_at_a_time(jnp.sum(array), GX_GY)

    def picard(_, velocity):
        rates = strains(with_halo(velocity, ((GX, 1), (GY, 2)), 1))
        weight = viscous_weight(rates, thick_corner, stiff_corner)
        residual = projector * (driving - stress_image(rates, weight, velocity, drag_term))

        def krylov(_, state):
            change, residual, direction, norm_now = state
            imaged = apply_field(direction, weight, drag_term, projector)
            step_size = norm_now / total(direction * imaged)
            change = change + step_size * direction
            residual = residual - step_size * imaged
            norm_next = total(residual * residual)
            direction = residual + norm_next / norm_now * direction
            return (change, residual, direction, norm_next)

        state = (jnp.zeros_like(velocity), residual, residual, total(residual * residual))
        return velocity + lax.fori_loop(0, KRYLOV, krylov, state)[0]

    return lax.fori_loop(0, PICARD, picard, velocity)


def shards(
    enthalpy,
    velocity_init,
    thickness,
    surface,
    friction,
    kappa,
    surface_enthalpy,
    geo_flux,
    ice_mask,
    grounded,
    boundary_code,
):
    ice_cols = ice_mask.astype(jnp.float32)
    bed_cols = grounded.astype(jnp.float32)
    inverse_bed, inverse_shelf = column_inverses(kappa)
    levels = enthalpy.shape[0]
    stacked = jnp.concatenate([enthalpy, velocity_init], axis=0)
    padded = with_halo_2(stacked, ((GX, 1), (GY, 2)), 2)
    current = padded[:levels]
    courant = padded[levels:]
    for substep in range(SUBSTEPS):
        if substep > 0:
            current = with_halo_2(current, ((GX, 1), (GY, 2)), 2)
        moved = advect(current, courant[0], courant[1])
        current = diffuse(
            moved, inverse_bed, inverse_shelf, kappa, ice_cols, bed_cols, surface_enthalpy, geo_flux
        )
    stiffness = jnp.exp(-soften * jnp.mean(current, axis=0))
    free_cells = (boundary_code == 0) & (ice_mask == 1)
    held_cells = free_cells | (boundary_code == 2)
    projector = free_cells.astype(jnp.float32)
    drag_term = jnp.where(grounded == 1, friction, 0.0) + shelf_drag
    velocity = jnp.where(held_cells[None], velocity_init, 0.0)
    fields = jnp.stack(
        [velocity[0], velocity[1], projector * drag_term, thickness, stiffness, surface]
    )
    quick, worst = momentum(fields)
    velocity = lax.cond(
        worst[0, 0] > PIVOT_FLOOR,
        lambda: quick,
        lambda: plain_picard(
            velocity, thickness, stiffness, surface, drag_term, projector[None]
        ),
    )
    return (current, velocity)


def solution(mesh):
    torus = Mesh(mesh.devices.reshape(TORUS), ("gx_0", "gx_1", "gy_0", "gy_1"))
    placed = (
        P(None, GX, GY),
        P(None, GX, GY),
        P(GX, GY),
        P(GX, GY),
        P(GX, GY),
        P(),
        P(GX, GY),
        P(GX, GY),
        P(GX, GY),
        P(GX, GY),
        P(GX, GY),
    )
    return jax.shard_map(
        shards,
        mesh=torus,
        in_specs=placed,
        out_specs=(P(None, GX, GY), P(None, GX, GY)),
        check_vma=False,
    )
```

```python
import functools

import jax
import jax.numpy as jnp
from jax import lax
from jax.experimental import pallas as pl
from jax.experimental.pallas import tpu as pltpu
from jax.sharding import Mesh
from jax.sharding import PartitionSpec as P

SUBSTEPS = 2
PICARD = 2
KRYLOV = 6
TORUS = (4, 8, 8, 2)
GX_GY = ("gx_0", "gx_1", "gy_0", "gy_1")
GX = ("gx_0", "gx_1")
GY = ("gy_0", "gy_1")


soften = 0.3
shelf_drag = 0.2
strain_floor = 0.01

MIDDLE = 17.0
RADIUS = 17.0
PIVOT_FLOOR = 2e-4
OWN = 16
SIDE = 64


def with_halo(shard, sides, width):
    for axis, dim in sides:
        size, length = (lax.axis_size(axis), shard.shape[dim])
        up = [(i, (i + 1) % size) for i in range(size - 1)]
        down = [(j, i) for i, j in up]
        last = lax.slice_in_dim(shard, length - width, length, axis=dim)
        first = lax.slice_in_dim(shard, 0, width, axis=dim)
        before = lax.ppermute(last, axis, up)
        after = lax.ppermute(first, axis, down)
        shard = jnp.concatenate([before, shard, after], axis=dim)
    return shard


def one_axis_at_a_time(shard, axes):
    return functools.reduce(lax.psum, axes, shard)


def with_halo_2(shard, sides, width):
    edges = {}
    for axis, dim in sides:
        size, length = (lax.axis_size(axis), shard.shape[dim])
        up = [(i, (i + 1) % size) for i in range(size - 1)]
        last = lax.slice_in_dim(shard, length - width, length, axis=dim)
        first = lax.slice_in_dim(shard, 0, width, axis=dim)
        edges[dim] = (
            lax.ppermute(last, axis, up),
            lax.ppermute(first, axis, [(b, a) for a, b in up]),
        )
    done = []
    for _, dim in sides:
        low, high = edges[dim]
        around = [(width, width) if d in done else (0, 0) for d in range(shard.ndim)]
        shard = jnp.concatenate([jnp.pad(low, around), shard, jnp.pad(high, around)], axis=dim)
        done.append(dim)
    return shard


def upwind_sweep(values, courant, axis):
    length = values.shape[axis]

    def window(array, start_cut, end_cut):
        return lax.slice_in_dim(array, start_cut, length - end_cut, axis=axis)

    face_speed = 0.5 * (window(courant, 1, 2) + window(courant, 2, 1))
    minus_one = window(values, 0, 3)
    here_cell = window(values, 1, 2)
    plus_one = window(values, 2, 1)
    plus_two = window(values, 3, 0)
    positive = jnp.maximum(face_speed, 0.0)
    negative = jnp.minimum(face_speed, 0.0)
    face_flux = positive * (here_cell + 0.25 * (1.0 - positive) * (plus_one - minus_one))
    face_flux = face_flux + negative * (plus_one - 0.25 * (1.0 + negative) * (plus_two - here_cell))
    count = face_flux.shape[axis]
    return lax.slice_in_dim(face_flux, 1, count, axis=axis) - lax.slice_in_dim(
        face_flux, 0, count - 1, axis=axis
    )


def advect(padded, courant_x, courant_y):
    row_count = padded.shape[1]
    col_count = padded.shape[2]
    along_x = upwind_sweep(
        padded[:, :, 2 : col_count - 2], courant_x[None, :, 2 : col_count - 2], 1
    )
    along_y = upwind_sweep(
        padded[:, 2 : row_count - 2, :], courant_y[None, 2 : row_count - 2, :], 2
    )
    return padded[:, 2 : row_count - 2, 2 : col_count - 2] - along_x - along_y


def diffuse(moved, inverse_bed, inverse_shelf, kappa, ice_cols, bed_cols, surface_heat, heat_flux):
    levels = moved.shape[0]
    depth_index = lax.broadcasted_iota(jnp.int32, (levels, 1, 1), 0)
    right_side = moved + jnp.where(depth_index == 0, kappa[0] * surface_heat[None], 0.0)
    right_side = right_side + jnp.where(
        depth_index == levels - 1, bed_cols[None] * heat_flux[None], 0.0
    )
    columns = right_side.reshape(levels, -1)
    solved_bed = jnp.dot(inverse_bed, columns, precision=lax.Precision.HIGHEST).reshape(moved.shape)
    solved_shelf = jnp.dot(inverse_shelf, columns, precision=lax.Precision.HIGHEST).reshape(
        moved.shape
    )
    solved = jnp.where(bed_cols[None] > 0.5, solved_bed, solved_shelf)
    return jnp.where(ice_cols[None] > 0.5, solved, moved)


def corner_mean(array):
    return 0.25 * (array[:-1, :-1] + array[1:, :-1] + array[:-1, 1:] + array[1:, 1:])


def diff_rows(array):
    return 0.5 * (array[1:, :-1] - array[:-1, :-1] + (array[1:, 1:] - array[:-1, 1:]))


def diff_cols(array):
    return 0.5 * (array[:-1, 1:] - array[:-1, :-1] + (array[1:, 1:] - array[1:, :-1]))


def back_rows(array):
    return 0.5 * (array[:-1, :-1] + array[:-1, 1:] - array[1:, :-1] - array[1:, 1:])


def back_cols(array):
    return 0.5 * (array[:-1, :-1] + array[1:, :-1] - array[:-1, 1:] - array[1:, 1:])


def strains(padded):
    stretch_x = diff_rows(padded[0])
    stretch_y = diff_cols(padded[1])
    shear_rate = 0.5 * (diff_cols(padded[0]) + diff_rows(padded[1]))
    return (stretch_x, stretch_y, shear_rate)


def viscous_weight(rates, thick_corner, stiff_corner):
    stretch_x, stretch_y, shear_rate = rates
    square = (
        stretch_x * stretch_x
        + stretch_y * stretch_y
        + stretch_x * stretch_y
        + shear_rate * shear_rate
    )
    return 0.5 * stiff_corner * thick_corner * jnp.power(square + strain_floor, -1.0 / 3.0)


def stress_image(rates, weight, center, drag_term):
    stretch_x, stretch_y, shear_rate = rates
    stress_x = weight * (4.0 * stretch_x + 2.0 * stretch_y)
    stress_y = weight * (4.0 * stretch_y + 2.0 * stretch_x)
    shear_stress = 2.0 * weight * shear_rate
    first = back_rows(stress_x) + back_cols(shear_stress) + drag_term * center[0]
    second = back_rows(shear_stress) + back_cols(stress_y) + drag_term * center[1]
    return jnp.stack([first, second])


def apply_field(direction, weight, drag_term, projector):
    padded = with_halo(direction, ((GX, 1), (GY, 2)), 1)
    return projector * stress_image(strains(padded), weight, direction, drag_term)


def inverse_kernel(kappa_ref, bed_ref, shelf_ref):
    levels = kappa_ref.shape[1]
    above = kappa_ref[0:8, :]
    below = kappa_ref[8:16, :]
    lane = lax.broadcasted_iota(jnp.int32, (8, levels), 1)
    rows = lax.broadcasted_iota(jnp.int32, (levels, levels), 0)
    cols = lax.broadcasted_iota(jnp.int32, (levels, levels), 1)
    floating = 1.0 + above + below
    on_bed = jnp.where(lane == levels - 1, 1.0 + above, floating)
    for diagonal, out_ref in ((on_bed, bed_ref), (floating, shelf_ref)):
        low = jnp.where(lane == 0, 0.0, -above)
        high = jnp.where(lane == levels - 1, 0.0, -below)
        mid = diagonal
        right = jnp.where(rows == cols, 1.0, 0.0)
        step = 1
        while step < levels:
            back = levels - step
            down = -low / pltpu.roll(mid, step, 1)
            up = -high / pltpu.roll(mid, back, 1)
            mid = mid + down * pltpu.roll(high, step, 1) + up * pltpu.roll(low, back, 1)
            low = down * pltpu.roll(low, step, 1)
            high = up * pltpu.roll(high, back, 1)
            right = (
                right
                + down[0:1] * pltpu.roll(right, step, 1)
                + up[0:1] * pltpu.roll(right, back, 1)
            )
            step *= 2
        out_ref[...] = right / mid[0:1]


def column_inverses(kappa):
    levels = kappa.shape[0] - 1
    above = jnp.broadcast_to(kappa[None, :levels], (8, levels))
    below = jnp.broadcast_to(kappa[None, 1:], (8, levels))
    shape = jax.ShapeDtypeStruct((levels, levels), kappa.dtype)
    return pl.pallas_call(inverse_kernel, out_shape=(shape, shape), name="column_inverses")(
        jnp.concatenate([above, below], axis=0)
    )


def next_row(array):
    return pltpu.roll(array, array.shape[0] - 1, 0)


def next_col(array):
    return pltpu.roll(array, array.shape[1] - 1, 1)


def last_row(array):
    return pltpu.roll(array, 1, 0)


def last_col(array):
    return pltpu.roll(array, 1, 1)


def corner_rates(u, v):
    u_next = next_col(u)
    v_next = next_col(v)
    u_sum, u_diff = (u + u_next, u_next - u)
    v_sum, v_diff = (v + v_next, v_next - v)
    along = next_row(u_sum) - u_sum
    across = v_diff + next_row(v_diff)
    shear = u_diff + next_row(u_diff) + (next_row(v_sum) - v_sum)
    return (along, across, shear)


def stress_back(rates, half_weight):
    along, across, shear = rates
    stress_x = half_weight * (2.0 * along + across)
    stress_y = half_weight * (2.0 * across + along)
    stress_s = 0.5 * half_weight * shear
    x_before = last_col(stress_x)
    y_before = last_col(stress_y)
    s_before = last_col(stress_s)
    x_sum, s_diff = (stress_x + x_before, s_before - stress_s)
    s_sum, y_diff = (stress_s + s_before, y_before - stress_y)
    first = last_row(x_sum + s_diff) + (s_diff - x_sum)
    second = last_row(s_sum + y_diff) + (y_diff - s_sum)
    return (first, second)


def half_weights(rates, corner_product):
    along, across, shear = rates
    square = 0.25 * (along * along + across * across + along * across) + 0.0625 * shear * shear
    return corner_product * jnp.exp(jnp.log(square + strain_floor) * (-1.0 / 3.0))


def krylov_basis(u, v, drag, driving, corner_product, own_row, keep):
    free = drag > 0.0
    rates = corner_rates(u, v)
    half_weight = half_weights(rates, corner_product)
    first, second = stress_back(rates, half_weight)
    r_u = jnp.where(free, driving[0] - first - drag * u, 0.0)
    r_v = jnp.where(free, driving[1] - second - drag * v, 0.0)

    def own(array):
        return array[own_row : own_row + 8, :128]

    basis_u, basis_v = ([r_u], [r_v])
    own_basis, own_image = ([(own(r_u), own(r_v))], [])
    keep(0, r_u, r_v)
    for k in range(KRYLOV):
        b_u, b_v = (basis_u[k], basis_v[k])
        first, second = stress_back(corner_rates(b_u, b_v), half_weight)
        a_u = jnp.where(free, first, 0.0) + drag * b_u
        a_v = jnp.where(free, second, 0.0) + drag * b_v
        own_image.append((own(a_u), own(a_v)))
        if k + 1 < KRYLOV:
            scale = (1.0 if k == 0 else 2.0) / RADIUS
            n_u = scale * a_u - (scale * MIDDLE) * b_u
            n_v = scale * a_v - (scale * MIDDLE) * b_v
            if k > 0:
                n_u = n_u - basis_u[k - 1]
                n_v = n_v - basis_v[k - 1]
            basis_u.append(n_u)
            basis_v.append(n_v)
            own_basis.append((own(n_u), own(n_v)))
            keep(k + 1, n_u, n_v)
    products = []
    for i in range(KRYLOV):
        for j in range(i, KRYLOV):
            products.append(
                own_basis[i][0] * own_image[j][0] + own_basis[i][1] * own_image[j][1]
            )
    for i in range(KRYLOV):
        products.append(own_basis[i][0] * own_basis[0][0] + own_basis[i][1] * own_basis[0][1])
    return products


def write_sums(products, out_ref):
    count = out_ref.shape[0]
    lines = [jnp.sum(p, axis=0, keepdims=True) for p in products]
    lines.append(jnp.zeros((128 - len(lines), 128), jnp.float32))
    table = jnp.concatenate(lines, axis=0)
    out_ref[...] = lax.dot_general(
        jnp.ones((count, 128), jnp.float32),
        table,
        (((1,), (1,)), ((), ())),
        precision=lax.Precision.HIGHEST,
        preferred_element_type=jnp.float32,
    )


def small_solve(parts):
    sums = jnp.sum(parts, axis=0, keepdims=True)
    at = lambda k: sums[:, k : k + 1]
    full = {}
    k = 0
    for i in range(KRYLOV):
        for j in range(i, KRYLOV):
            full[i, j] = at(k)
            k += 1
    norm = [lax.rsqrt(full[i, i]) for i in range(KRYLOV)]
    right = [at(k + i) * norm[i] for i in range(KRYLOV)]
    lower, pivots, least = ({}, [], None)
    scaled = {}
    for j in range(KRYLOV):
        pivot = jnp.ones_like(right[0])
        for m in range(j):
            pivot = pivot - scaled[j, m] * lower[j, m]
        pivots.append(pivot)
        least = pivot if least is None else jnp.minimum(least, pivot)
        inverse = 1.0 / pivot
        for i in range(j + 1, KRYLOV):
            value = full[j, i] * norm[i] * norm[j]
            for m in range(j):
                value = value - scaled[i, m] * lower[j, m]
            scaled[i, j] = value
            lower[i, j] = value * inverse
    forward = []
    for i in range(KRYLOV):
        value = right[i]
        for m in range(i):
            value = value - lower[i, m] * forward[m]
        forward.append(value)
    answer = [None] * KRYLOV
    for i in reversed(range(KRYLOV)):
        value = forward[i] / pivots[i]
        for m in range(i + 1, KRYLOV):
            value = value - lower[m, i] * answer[m]
        answer[i] = value
    return ([a * n for a, n in zip(answer, norm)], least)


def first_picard_kernel(
    place_ref, grid_ref, mine_ref, left_ref, right_ref, basis_ref, fixed_ref, sums_ref
):
    rows = mine_ref.shape[1]
    lane = lax.broadcasted_iota(jnp.int32, (rows, 128), 1)
    row = lax.broadcasted_iota(jnp.int32, (rows, 128), 0) + (place_ref[0] * 8 - OWN)
    row_in = (row >= 0) & (row < grid_ref[0] * 8)
    from_right = lane < SIDE
    col = place_ref[1] + jnp.where(from_right, 1, -1)
    side_in = row_in & (col >= 0) & (col < grid_ref[1])

    def field(k):
        side = jnp.where(from_right, right_ref[k], left_ref[k])
        return jnp.concatenate(
            [jnp.where(row_in, mine_ref[k], 0.0), jnp.where(side_in, side, 0.0)], axis=1
        )

    u, v, drag, thick, stiff, surface = (field(k) for k in range(6))
    t_sum = thick + next_col(thick)
    s_sum = stiff + next_col(stiff)
    corner_product = (1.0 / 64.0) * (t_sum + next_row(t_sum)) * (s_sum + next_row(s_sum))
    driving = (
        -thick * 0.5 * (next_row(surface) - last_row(surface)),
        -thick * 0.5 * (next_col(surface) - last_col(surface)),
    )
    kept = slice(OWN - 8, OWN + 16)

    def keep(k, b_u, b_v):
        basis_ref[2 * k] = b_u[kept]
        basis_ref[2 * k + 1] = b_v[kept]

    for k, value in enumerate((u, v, drag, corner_product, driving[0], driving[1])):
        fixed_ref[k] = value[kept]
    products = krylov_basis(u, v, drag, driving, corner_product, OWN, keep)
    write_sums(products, sums_ref)


def second_picard_kernel(
    parts_ref, basis_ref, fixed_ref, next_ref, velocity_ref, sums_ref, least_ref
):
    answer, least = small_solve(parts_ref[...])
    u, v = (fixed_ref[0], fixed_ref[1])
    for k in range(KRYLOV):
        u = u + answer[k] * basis_ref[2 * k]
        v = v + answer[k] * basis_ref[2 * k + 1]
    velocity_ref[0] = u[8:16, :128]
    velocity_ref[1] = v[8:16, :128]
    least_ref[...] = jnp.broadcast_to(least, least_ref.shape)

    def keep(k, b_u, b_v):
        next_ref[2 * k] = b_u[8:16, :128]
        next_ref[2 * k + 1] = b_v[8:16, :128]

    driving = (fixed_ref[4], fixed_ref[5])
    products = krylov_basis(u, v, fixed_ref[2], driving, fixed_ref[3], 8, keep)
    write_sums(products, sums_ref)


def last_kernel(parts_ref, basis_ref, velocity_ref, least_ref, out_ref, worst_ref):
    answer, least = small_solve(parts_ref[...])
    u, v = (velocity_ref[0], velocity_ref[1])
    for k in range(KRYLOV):
        u = u + answer[k] * basis_ref[2 * k]
        v = v + answer[k] * basis_ref[2 * k + 1]
    out_ref[0] = u
    out_ref[1] = v
    worst_ref[...] = jnp.minimum(least_ref[...], least)


def over_all(sums):
    count = lax.axis_size(GX)
    part = lax.all_to_all(sums, GY, 0, 0, tiled=True)
    part = jnp.broadcast_to(jnp.sum(part, axis=0, keepdims=True), (count, 128))
    return lax.all_to_all(part, GX, 0, 0, tiled=True)


def shifted(array, axis, by):
    size = lax.axis_size(axis)
    return lax.ppermute(array, axis, [(i, (i + by) % size) for i in range(size)])


def wide_halo(stacked):
    rows, cols = stacked.shape[1:]
    above = shifted(stacked[:, rows - 4 :], GX, 1)
    below = shifted(stacked[:, :4], GX, -1)
    tall = jnp.concatenate([above, stacked, below], axis=1)
    left = shifted(tall[:, 2:-2, cols - 4 :], GY, 1)
    right = shifted(tall[:, 2:-2, :4], GY, -1)
    around = ((0, 0), (2, 2), (0, 0))
    padded = jnp.concatenate([jnp.pad(left, around), tall, jnp.pad(right, around)], axis=2)
    row = lax.broadcasted_iota(jnp.int32, padded.shape[1:], 0) - 4 + lax.axis_index(GX) * rows
    col = lax.broadcasted_iota(jnp.int32, padded.shape[1:], 1) - 4 + lax.axis_index(GY) * cols
    inside = (row >= 0) & (row < rows * lax.axis_size(GX))
    inside = inside & (col >= 0) & (col < cols * lax.axis_size(GY))
    return (jnp.where(inside[None], padded, 0.0), inside)


def momentum(fields):
    f32 = jnp.float32
    below = [shifted(fields, GX, by) for by in (2, 1)]
    above = [shifted(fields, GX, -by) for by in (1, 2)]
    mine = jnp.concatenate(below + [fields] + above, axis=1)
    left = shifted(mine, GY, 1)
    right = shifted(mine, GY, -1)
    gx, gy = (lax.axis_size(GX), lax.axis_size(GY))
    place = jnp.stack([lax.axis_index(GX), lax.axis_index(GY)]).astype(jnp.int32)
    grid = jnp.array([gx, gy], jnp.int32)
    smem = pl.BlockSpec(memory_space=pltpu.SMEM)
    vmem = pl.BlockSpec(memory_space=pltpu.VMEM)
    struct = jax.ShapeDtypeStruct
    basis, fixed, sums = pl.pallas_call(
        first_picard_kernel,
        out_shape=(
            struct((2 * KRYLOV, 24, 256), f32),
            struct((6, 24, 256), f32),
            struct((gy, 128), f32),
        ),
        in_specs=[smem, smem, vmem, vmem, vmem],
        out_specs=(vmem, vmem, vmem),
        name="first_picard",
    )(place, grid, mine, left, right)
    basis, velocity, sums, least = pl.pallas_call(
        second_picard_kernel,
        out_shape=(
            struct((2 * KRYLOV, 8, 128), f32),
            struct((2, 8, 128), f32),
            struct((gy, 128), f32),
            struct((8, 128), f32),
        ),
        name="second_picard",
    )(over_all(sums), basis, fixed)
    return pl.pallas_call(
        last_kernel,
        out_shape=(struct((2, 8, 128), f32), struct((8, 128), f32)),
        name="last_picard",
    )(over_all(sums), basis, velocity, least)


def plain_picard(velocity, thickness, stiffness, surface, drag_term, projector):
    statics = with_halo(jnp.stack([thickness, stiffness, surface]), ((GX, 1), (GY, 2)), 1)
    thick_corner = corner_mean(statics[0])
    stiff_corner = corner_mean(statics[1])
    heights = statics[2]
    driving = jnp.stack(
        [
            -thickness * 0.5 * (heights[2:, 1:-1] - heights[:-2, 1:-1]),
            -thickness * 0.5 * (heights[1:-1, 2:] - heights[1:-1, :-2]),
        ]
    )

    def total(array):
        return one_axis_at_a_time(jnp.sum(array), GX_GY)

    def picard(_, velocity):
        rates = strains(with_halo(velocity, ((GX, 1), (GY, 2)), 1))
        weight = viscous_weight(rates, thick_corner, stiff_corner)
        residual = projector * (driving - stress_image(rates, weight, velocity, drag_term))

        def krylov(_, state):
            change, residual, direction, norm_now = state
            imaged = apply_field(direction, weight, drag_term, projector)
            step_size = norm_now / total(direction * imaged)
            change = change + step_size * direction
            residual = residual - step_size * imaged
            norm_next = total(residual * residual)
            direction = residual + norm_next / norm_now * direction
            return (change, residual, direction, norm_next)

        state = (jnp.zeros_like(velocity), residual, residual, total(residual * residual))
        return velocity + lax.fori_loop(0, KRYLOV, krylov, state)[0]

    return lax.fori_loop(0, PICARD, picard, velocity)


def shards(
    enthalpy,
    velocity_init,
    thickness,
    surface,
    friction,
    kappa,
    surface_enthalpy,
    geo_flux,
    ice_mask,
    grounded,
    boundary_code,
):
    inverse_bed, inverse_shelf = column_inverses(kappa)
    levels = enthalpy.shape[0]
    columns = jnp.stack(
        [ice_mask.astype(jnp.float32), grounded.astype(jnp.float32), surface_enthalpy, geo_flux]
    )
    stacked = jnp.concatenate([enthalpy, velocity_init, columns], axis=0)
    padded, inside = wide_halo(stacked)
    courant = padded[levels : levels + 2]
    ice_cols, bed_cols, heat, flux = padded[levels + 2 :, 2:-2, 2:-2]
    current = advect(padded[:levels], courant[0], courant[1])
    current = diffuse(
        current, inverse_bed, inverse_shelf, kappa, ice_cols, bed_cols, heat, flux
    )
    current = jnp.where(inside[None, 2:-2, 2:-2], current, 0.0)
    courant = courant[:, 2:-2, 2:-2]
    current = advect(current, courant[0], courant[1])
    current = diffuse(
        current,
        inverse_bed,
        inverse_shelf,
        kappa,
        ice_cols[2:-2, 2:-2],
        bed_cols[2:-2, 2:-2],
        surface_enthalpy,
        geo_flux,
    )
    stiffness = jnp.exp(-soften * jnp.mean(current, axis=0))
    free_cells = (boundary_code == 0) & (ice_mask == 1)
    held_cells = free_cells | (boundary_code == 2)
    projector = free_cells.astype(jnp.float32)
    drag_term = jnp.where(grounded == 1, friction, 0.0) + shelf_drag
    velocity = jnp.where(held_cells[None], velocity_init, 0.0)
    fields = jnp.stack(
        [velocity[0], velocity[1], projector * drag_term, thickness, stiffness, surface]
    )
    quick, worst = momentum(fields)
    velocity = lax.cond(
        worst[0, 0] > PIVOT_FLOOR,
        lambda: quick,
        lambda: plain_picard(
            velocity, thickness, stiffness, surface, drag_term, projector[None]
        ),
    )
    return (current, velocity)


def solution(mesh):
    torus = Mesh(mesh.devices.reshape(TORUS), ("gx_0", "gx_1", "gy_0", "gy_1"))
    placed = (
        P(None, GX, GY),
        P(None, GX, GY),
        P(GX, GY),
        P(GX, GY),
        P(GX, GY),
        P(),
        P(GX, GY),
        P(GX, GY),
        P(GX, GY),
        P(GX, GY),
        P(GX, GY),
    )
    return jax.shard_map(
        shards,
        mesh=torus,
        in_specs=placed,
        out_specs=(P(None, GX, GY), P(None, GX, GY)),
        check_vma=False,
    )
```

```python
import functools

import jax
import jax.numpy as jnp
from jax import lax
from jax.experimental import pallas as pl
from jax.experimental.pallas import tpu as pltpu
from jax.sharding import Mesh
from jax.sharding import PartitionSpec as P

PICARD = 2
KRYLOV = 6
TORUS = (4, 8, 8, 2)
GX_GY = ("gx_0", "gx_1", "gy_0", "gy_1")
GX = ("gx_0", "gx_1")
GY = ("gy_0", "gy_1")


soften = 0.3
shelf_drag = 0.2
strain_floor = 0.01

MIDDLE = 17.0
RADIUS = 17.0
PIVOT_FLOOR = 2e-4
OWN = 16
SIDE = 64


def with_halo(shard, sides, width):
    for axis, dim in sides:
        size, length = (lax.axis_size(axis), shard.shape[dim])
        up = [(i, (i + 1) % size) for i in range(size - 1)]
        down = [(j, i) for i, j in up]
        last = lax.slice_in_dim(shard, length - width, length, axis=dim)
        first = lax.slice_in_dim(shard, 0, width, axis=dim)
        before = lax.ppermute(last, axis, up)
        after = lax.ppermute(first, axis, down)
        shard = jnp.concatenate([before, shard, after], axis=dim)
    return shard


def one_axis_at_a_time(shard, axes):
    return functools.reduce(lax.psum, axes, shard)


def corner_mean(array):
    return 0.25 * (array[:-1, :-1] + array[1:, :-1] + array[:-1, 1:] + array[1:, 1:])


def diff_rows(array):
    return 0.5 * (array[1:, :-1] - array[:-1, :-1] + (array[1:, 1:] - array[:-1, 1:]))


def diff_cols(array):
    return 0.5 * (array[:-1, 1:] - array[:-1, :-1] + (array[1:, 1:] - array[1:, :-1]))


def back_rows(array):
    return 0.5 * (array[:-1, :-1] + array[:-1, 1:] - array[1:, :-1] - array[1:, 1:])


def back_cols(array):
    return 0.5 * (array[:-1, :-1] + array[1:, :-1] - array[:-1, 1:] - array[1:, 1:])


def strains(padded):
    stretch_x = diff_rows(padded[0])
    stretch_y = diff_cols(padded[1])
    shear_rate = 0.5 * (diff_cols(padded[0]) + diff_rows(padded[1]))
    return (stretch_x, stretch_y, shear_rate)


def viscous_weight(rates, thick_corner, stiff_corner):
    stretch_x, stretch_y, shear_rate = rates
    square = (
        stretch_x * stretch_x
        + stretch_y * stretch_y
        + stretch_x * stretch_y
        + shear_rate * shear_rate
    )
    return 0.5 * stiff_corner * thick_corner * jnp.power(square + strain_floor, -1.0 / 3.0)


def stress_image(rates, weight, center, drag_term):
    stretch_x, stretch_y, shear_rate = rates
    stress_x = weight * (4.0 * stretch_x + 2.0 * stretch_y)
    stress_y = weight * (4.0 * stretch_y + 2.0 * stretch_x)
    shear_stress = 2.0 * weight * shear_rate
    first = back_rows(stress_x) + back_cols(shear_stress) + drag_term * center[0]
    second = back_rows(shear_stress) + back_cols(stress_y) + drag_term * center[1]
    return jnp.stack([first, second])


def apply_field(direction, weight, drag_term, projector):
    padded = with_halo(direction, ((GX, 1), (GY, 2)), 1)
    return projector * stress_image(strains(padded), weight, direction, drag_term)


def inverse_kernel(kappa_ref, out_ref):
    levels = kappa_ref.shape[1]
    above = kappa_ref[0:8, :]
    below = kappa_ref[8:16, :]
    lane = lax.broadcasted_iota(jnp.int32, (8, levels), 1)
    rows = lax.broadcasted_iota(jnp.int32, (levels, levels), 0)
    cols = lax.broadcasted_iota(jnp.int32, (levels, levels), 1)
    floating = 1.0 + above + below
    on_bed = jnp.where(lane == levels - 1, 1.0 + above, floating)
    for k, diagonal in enumerate((on_bed, floating)):
        low = jnp.where(lane == 0, 0.0, -above)
        high = jnp.where(lane == levels - 1, 0.0, -below)
        mid = diagonal
        right = jnp.where(rows == cols, 1.0, 0.0)
        step = 1
        while step < levels:
            back = levels - step
            down = -low / pltpu.roll(mid, step, 1)
            up = -high / pltpu.roll(mid, back, 1)
            mid = mid + down * pltpu.roll(high, step, 1) + up * pltpu.roll(low, back, 1)
            low = down * pltpu.roll(low, step, 1)
            high = up * pltpu.roll(high, back, 1)
            right = (
                right
                + down[0:1] * pltpu.roll(right, step, 1)
                + up[0:1] * pltpu.roll(right, back, 1)
            )
            step *= 2
        out_ref[k * levels : (k + 1) * levels] = right / mid[0:1]


def column_inverses(kappa):
    levels = kappa.shape[0] - 1
    above = jnp.broadcast_to(kappa[None, :levels], (8, levels))
    below = jnp.broadcast_to(kappa[None, 1:], (8, levels))
    return pl.pallas_call(
        inverse_kernel,
        out_shape=jax.ShapeDtypeStruct((2 * levels, levels), kappa.dtype),
        name="column_inverses",
    )(jnp.concatenate([above, below], axis=0))


def next_row(array):
    return pltpu.roll(array, array.shape[0] - 1, 0)


def next_col(array):
    return pltpu.roll(array, array.shape[1] - 1, 1)


def last_row(array):
    return pltpu.roll(array, 1, 0)


def last_col(array):
    return pltpu.roll(array, 1, 1)


def corner_rates(u, v):
    u_next = next_col(u)
    v_next = next_col(v)
    u_sum, u_diff = (u + u_next, u_next - u)
    v_sum, v_diff = (v + v_next, v_next - v)
    along = next_row(u_sum) - u_sum
    across = v_diff + next_row(v_diff)
    shear = u_diff + next_row(u_diff) + (next_row(v_sum) - v_sum)
    return (along, across, shear)


def stress_back(rates, half_weight):
    along, across, shear = rates
    stress_x = half_weight * (2.0 * along + across)
    stress_y = half_weight * (2.0 * across + along)
    stress_s = 0.5 * half_weight * shear
    x_before = last_col(stress_x)
    y_before = last_col(stress_y)
    s_before = last_col(stress_s)
    x_sum, s_diff = (stress_x + x_before, s_before - stress_s)
    s_sum, y_diff = (stress_s + s_before, y_before - stress_y)
    first = last_row(x_sum + s_diff) + (s_diff - x_sum)
    second = last_row(s_sum + y_diff) + (y_diff - s_sum)
    return (first, second)


def half_weights(rates, corner_product):
    along, across, shear = rates
    square = 0.25 * (along * along + across * across + along * across) + 0.0625 * shear * shear
    return corner_product * jnp.exp(jnp.log(square + strain_floor) * (-1.0 / 3.0))


def krylov_basis(u, v, drag, driving, corner_product, own_row, keep):
    free = drag > 0.0
    rates = corner_rates(u, v)
    half_weight = half_weights(rates, corner_product)
    first, second = stress_back(rates, half_weight)
    r_u = jnp.where(free, driving[0] - first - drag * u, 0.0)
    r_v = jnp.where(free, driving[1] - second - drag * v, 0.0)

    def own(array):
        return array[own_row : own_row + 8, :128]

    basis_u, basis_v = ([r_u], [r_v])
    own_basis, own_image = ([(own(r_u), own(r_v))], [])
    keep(0, r_u, r_v)
    for k in range(KRYLOV):
        b_u, b_v = (basis_u[k], basis_v[k])
        first, second = stress_back(corner_rates(b_u, b_v), half_weight)
        a_u = jnp.where(free, first, 0.0) + drag * b_u
        a_v = jnp.where(free, second, 0.0) + drag * b_v
        own_image.append((own(a_u), own(a_v)))
        if k + 1 < KRYLOV:
            scale = (1.0 if k == 0 else 2.0) / RADIUS
            n_u = scale * a_u - (scale * MIDDLE) * b_u
            n_v = scale * a_v - (scale * MIDDLE) * b_v
            if k > 0:
                n_u = n_u - basis_u[k - 1]
                n_v = n_v - basis_v[k - 1]
            basis_u.append(n_u)
            basis_v.append(n_v)
            own_basis.append((own(n_u), own(n_v)))
            keep(k + 1, n_u, n_v)
    products = []
    for i in range(KRYLOV):
        for j in range(i, KRYLOV):
            products.append(
                own_basis[i][0] * own_image[j][0] + own_basis[i][1] * own_image[j][1]
            )
    for i in range(KRYLOV):
        products.append(own_basis[i][0] * own_basis[0][0] + own_basis[i][1] * own_basis[0][1])
    return products


def write_sums(products, out_ref):
    count = out_ref.shape[0]
    lines = [jnp.sum(p, axis=0, keepdims=True) for p in products]
    lines.append(jnp.zeros((128 - len(lines), 128), jnp.float32))
    table = jnp.concatenate(lines, axis=0)
    out_ref[...] = lax.dot_general(
        jnp.ones((count, 128), jnp.float32),
        table,
        (((1,), (1,)), ((), ())),
        precision=lax.Precision.HIGHEST,
        preferred_element_type=jnp.float32,
    )


def small_solve(parts):
    sums = jnp.sum(parts, axis=0, keepdims=True)
    at = lambda k: sums[:, k : k + 1]
    full = {}
    k = 0
    for i in range(KRYLOV):
        for j in range(i, KRYLOV):
            full[i, j] = at(k)
            k += 1
    norm = [lax.rsqrt(full[i, i]) for i in range(KRYLOV)]
    right = [at(k + i) * norm[i] for i in range(KRYLOV)]
    lower, pivots, least = ({}, [], None)
    scaled = {}
    for j in range(KRYLOV):
        pivot = jnp.ones_like(right[0])
        for m in range(j):
            pivot = pivot - scaled[j, m] * lower[j, m]
        pivots.append(pivot)
        least = pivot if least is None else jnp.minimum(least, pivot)
        inverse = 1.0 / pivot
        for i in range(j + 1, KRYLOV):
            value = full[j, i] * norm[i] * norm[j]
            for m in range(j):
                value = value - scaled[i, m] * lower[j, m]
            scaled[i, j] = value
            lower[i, j] = value * inverse
    forward = []
    for i in range(KRYLOV):
        value = right[i]
        for m in range(i):
            value = value - lower[i, m] * forward[m]
        forward.append(value)
    answer = [None] * KRYLOV
    for i in reversed(range(KRYLOV)):
        value = forward[i] / pivots[i]
        for m in range(i + 1, KRYLOV):
            value = value - lower[m, i] * answer[m]
        answer[i] = value
    return ([a * n for a, n in zip(answer, norm)], least)


def first_picard_kernel(
    place_ref, grid_ref, mine_ref, left_ref, right_ref, basis_ref, fixed_ref, sums_ref
):
    rows = mine_ref.shape[1]
    lane = lax.broadcasted_iota(jnp.int32, (rows, 128), 1)
    row = lax.broadcasted_iota(jnp.int32, (rows, 128), 0) + (place_ref[0] * 8 - OWN)
    row_in = (row >= 0) & (row < grid_ref[0] * 8)
    from_right = lane < SIDE
    col = place_ref[1] + jnp.where(from_right, 1, -1)
    side_in = row_in & (col >= 0) & (col < grid_ref[1])

    def field(k):
        side = jnp.where(from_right, right_ref[k], left_ref[k])
        return jnp.concatenate(
            [jnp.where(row_in, mine_ref[k], 0.0), jnp.where(side_in, side, 0.0)], axis=1
        )

    u, v, drag, thick, stiff, surface = (field(k) for k in range(6))
    t_sum = thick + next_col(thick)
    s_sum = stiff + next_col(stiff)
    corner_product = (1.0 / 64.0) * (t_sum + next_row(t_sum)) * (s_sum + next_row(s_sum))
    driving = (
        -thick * 0.5 * (next_row(surface) - last_row(surface)),
        -thick * 0.5 * (next_col(surface) - last_col(surface)),
    )
    kept = slice(OWN - 8, OWN + 16)

    def keep(k, b_u, b_v):
        basis_ref[2 * k] = b_u[kept]
        basis_ref[2 * k + 1] = b_v[kept]

    for k, value in enumerate((u, v, drag, corner_product, driving[0], driving[1])):
        fixed_ref[k] = value[kept]
    products = krylov_basis(u, v, drag, driving, corner_product, OWN, keep)
    write_sums(products, sums_ref)


def second_picard_kernel(
    parts_ref, basis_ref, fixed_ref, next_ref, velocity_ref, sums_ref, least_ref
):
    answer, least = small_solve(parts_ref[...])
    u, v = (fixed_ref[0], fixed_ref[1])
    for k in range(KRYLOV):
        u = u + answer[k] * basis_ref[2 * k]
        v = v + answer[k] * basis_ref[2 * k + 1]
    velocity_ref[0] = u[8:16, :128]
    velocity_ref[1] = v[8:16, :128]
    least_ref[...] = jnp.broadcast_to(least, least_ref.shape)

    def keep(k, b_u, b_v):
        next_ref[2 * k] = b_u[8:16, :128]
        next_ref[2 * k + 1] = b_v[8:16, :128]

    driving = (fixed_ref[4], fixed_ref[5])
    products = krylov_basis(u, v, fixed_ref[2], driving, fixed_ref[3], 8, keep)
    write_sums(products, sums_ref)


def last_kernel(parts_ref, basis_ref, velocity_ref, least_ref, out_ref, worst_ref):
    answer, least = small_solve(parts_ref[...])
    u, v = (velocity_ref[0], velocity_ref[1])
    for k in range(KRYLOV):
        u = u + answer[k] * basis_ref[2 * k]
        v = v + answer[k] * basis_ref[2 * k + 1]
    out_ref[0] = u
    out_ref[1] = v
    worst_ref[...] = jnp.minimum(least_ref[...], least)


def over_all(sums):
    count = lax.axis_size(GX)
    part = lax.all_to_all(sums, GY, 0, 0, tiled=True)
    part = jnp.broadcast_to(jnp.sum(part, axis=0, keepdims=True), (count, 128))
    return lax.all_to_all(part, GX, 0, 0, tiled=True)


def shifted(array, axis, by):
    size = lax.axis_size(axis)
    return lax.ppermute(array, axis, [(i, (i + by) % size) for i in range(size)])


def momentum(fields, place, grid):
    f32 = jnp.float32
    below = [shifted(fields, GX, by) for by in (2, 1)]
    above = [shifted(fields, GX, -by) for by in (1, 2)]
    mine = jnp.concatenate(below + [fields] + above, axis=1)
    left = shifted(mine, GY, 1)
    right = shifted(mine, GY, -1)
    gy = lax.axis_size(GY)
    smem = pl.BlockSpec(memory_space=pltpu.SMEM)
    vmem = pl.BlockSpec(memory_space=pltpu.VMEM)
    struct = jax.ShapeDtypeStruct
    basis, fixed, sums = pl.pallas_call(
        first_picard_kernel,
        out_shape=(
            struct((2 * KRYLOV, 24, 256), f32),
            struct((6, 24, 256), f32),
            struct((gy, 128), f32),
        ),
        in_specs=[smem, smem, vmem, vmem, vmem],
        out_specs=(vmem, vmem, vmem),
        name="first_picard",
    )(place, grid, mine, left, right)
    basis, velocity, sums, least = pl.pallas_call(
        second_picard_kernel,
        out_shape=(
            struct((2 * KRYLOV, 8, 128), f32),
            struct((2, 8, 128), f32),
            struct((gy, 128), f32),
            struct((8, 128), f32),
        ),
        name="second_picard",
    )(over_all(sums), basis, fixed)
    return pl.pallas_call(
        last_kernel,
        out_shape=(struct((2, 8, 128), f32), struct((8, 128), f32)),
        name="last_picard",
    )(over_all(sums), basis, velocity, least)


def plain_picard(velocity, thickness, stiffness, surface, drag_term, projector):
    statics = with_halo(jnp.stack([thickness, stiffness, surface]), ((GX, 1), (GY, 2)), 1)
    thick_corner = corner_mean(statics[0])
    stiff_corner = corner_mean(statics[1])
    heights = statics[2]
    driving = jnp.stack(
        [
            -thickness * 0.5 * (heights[2:, 1:-1] - heights[:-2, 1:-1]),
            -thickness * 0.5 * (heights[1:-1, 2:] - heights[1:-1, :-2]),
        ]
    )

    def total(array):
        return one_axis_at_a_time(jnp.sum(array), GX_GY)

    def picard(_, velocity):
        rates = strains(with_halo(velocity, ((GX, 1), (GY, 2)), 1))
        weight = viscous_weight(rates, thick_corner, stiff_corner)
        residual = projector * (driving - stress_image(rates, weight, velocity, drag_term))

        def krylov(_, state):
            change, residual, direction, norm_now = state
            imaged = apply_field(direction, weight, drag_term, projector)
            step_size = norm_now / total(direction * imaged)
            change = change + step_size * direction
            residual = residual - step_size * imaged
            norm_next = total(residual * residual)
            direction = residual + norm_next / norm_now * direction
            return (change, residual, direction, norm_next)

        state = (jnp.zeros_like(velocity), residual, residual, total(residual * residual))
        return velocity + lax.fori_loop(0, KRYLOV, krylov, state)[0]

    return lax.fori_loop(0, PICARD, picard, velocity)


def column_tiles(planes):
    shape = (32, 1024)
    line = lax.broadcasted_iota(jnp.int32, shape, 0)
    spot = lax.broadcasted_iota(jnp.int32, shape, 1)
    within = line & 15
    column = jnp.where(line < 16, 0, 126) + (within & 1)
    pick = jnp.where(spot == (within >> 1) * 128 + column, 1.0, 0.0)
    tiles = lax.dot_general(
        pick,
        jnp.concatenate(planes, axis=1),
        (((1,), (1,)), ((), ())),
        precision=lax.Precision.HIGHEST,
        preferred_element_type=jnp.float32,
    )
    return (tiles[:16], tiles[16:])


def pack_kernel(enthalpy_ref, speed_ref, low_ref, high_ref, left_ref, right_ref):
    planes = [enthalpy_ref[pl.ds(x, 128, stride=8), :] for x in range(8)]
    low_ref[0:128] = planes[0]
    low_ref[128:256] = planes[1]
    low_ref[256:264] = speed_ref[0]
    high_ref[0:128] = planes[6]
    high_ref[128:256] = planes[7]
    high_ref[256:264] = speed_ref[0]
    first, last = column_tiles(planes)
    left_ref[0:16] = first
    left_ref[16:24] = speed_ref[1]
    right_ref[0:16] = last
    right_ref[16:24] = speed_ref[1]


def line_weights(low_face, high_face):
    p_high, m_high = (jnp.maximum(high_face, 0.0), jnp.minimum(high_face, 0.0))
    p_low, m_low = (jnp.maximum(low_face, 0.0), jnp.minimum(low_face, 0.0))
    q_high, n_high = (0.25 * p_high * (1.0 - p_high), 0.25 * m_high * (1.0 + m_high))
    q_low, n_low = (0.25 * p_low * (1.0 - p_low), 0.25 * m_low * (1.0 + m_low))
    return (
        -q_low,
        q_high + (p_low + n_low),
        (q_low + m_low) - (p_high + n_high),
        -(q_high + m_high) - n_low,
        n_high,
    )


def cell_weights(speed_ref, before_x, after_x, before_y, after_y):
    c_x, c_y = (speed_ref[0], speed_ref[1])
    row = lax.broadcasted_iota(jnp.int32, (8, 128), 0)
    lane = lax.broadcasted_iota(jnp.int32, (8, 128), 1)
    x_before = jnp.where(row == 0, pltpu.roll(before_x, 1, 0), pltpu.roll(c_x, 1, 0))
    x_after = jnp.where(row == 7, pltpu.roll(after_x, 7, 0), pltpu.roll(c_x, 7, 0))
    y_before = jnp.where(lane == 0, pltpu.roll(before_y, 1, 1), pltpu.roll(c_y, 1, 1))
    y_after = jnp.where(lane == 127, pltpu.roll(after_y, 127, 1), pltpu.roll(c_y, 127, 1))
    along_x = line_weights(0.5 * (x_before + c_x), 0.5 * (c_x + x_after))
    along_y = line_weights(0.5 * (y_before + c_y), 0.5 * (c_y + y_after))
    center = 1.0 + along_x[2] + along_y[2]
    return (center,) + along_x[:2] + along_x[3:] + along_y[:2] + along_y[3:]


def edge_products(weights, before_y, after_y):
    line = lax.broadcasted_iota(jnp.int32, (32, 128), 0)
    lane = lax.broadcasted_iota(jnp.int32, (32, 128), 1)
    back_2, back_1, ahead_1, ahead_2 = weights[5:]
    spread = []
    for x in range(8):
        b_2, b_1, a_1, a_2 = (w[x : x + 1] for w in (back_2, back_1, ahead_1, ahead_2))
        far = (line == 2 * x) & (lane == 0)
        far = far | ((line == 2 * x + 1) & (lane == 1))
        value = jnp.where(far, b_2, 0.0)
        value = jnp.where((line == 2 * x + 1) & (lane == 0), b_1, value)
        far = (line == 16 + 2 * x) & (lane == 126)
        far = far | ((line == 17 + 2 * x) & (lane == 127))
        value = jnp.where(far, a_2, value)
        value = jnp.where((line == 16 + 2 * x) & (lane == 127), a_1, value)
        spread.append(value)
    return lax.dot_general(
        jnp.concatenate([before_y, after_y], axis=0),
        jnp.concatenate(spread, axis=1),
        (((0,), (0,)), ((), ())),
        precision=lax.Precision.HIGHEST,
        preferred_element_type=jnp.float32,
    )


def substep(planes, weights, edges, inverses, first_kappa, ice, bed, surface_heat, heat_flux):
    lane = lax.broadcasted_iota(jnp.int32, (8, 128), 1)
    center, x_b2, x_b1, x_a1, x_a2, y_b2, y_b1, y_a1, y_a2 = weights
    y_b2 = jnp.where(lane < 2, 0.0, y_b2)
    y_b1 = jnp.where(lane < 1, 0.0, y_b1)
    y_a1 = jnp.where(lane > 126, 0.0, y_a1)
    y_a2 = jnp.where(lane > 125, 0.0, y_a2)
    level = lax.broadcasted_iota(jnp.int32, (128, 128), 0)
    done = []
    for x in range(0, 8, 2):
        moved, sides = ([], [])
        for r in (x, x + 1):
            at = lambda w: w[r : r + 1]
            e = planes[r + 2]
            value = at(center) * e + edges[:, r * 128 : r * 128 + 128]
            value = value + at(x_b2) * planes[r] + at(x_b1) * planes[r + 1]
            value = value + at(x_a1) * planes[r + 3] + at(x_a2) * planes[r + 4]
            value = value + at(y_b2) * pltpu.roll(e, 2, 1) + at(y_b1) * pltpu.roll(e, 1, 1)
            value = value + at(y_a1) * pltpu.roll(e, 127, 1) + at(y_a2) * pltpu.roll(e, 126, 1)
            moved.append(value)
            top = first_kappa * at(surface_heat)
            bottom = at(bed) * at(heat_flux)
            sides.append(
                value + jnp.where(level == 0, top, jnp.where(level == 127, bottom, 0.0))
            )
        solved = jnp.dot(
            inverses,
            jnp.concatenate(sides, axis=1),
            precision=lax.Precision.HIGHEST,
            preferred_element_type=jnp.float32,
        )
        for k, r in enumerate((x, x + 1)):
            mine = slice(k * 128, k * 128 + 128)
            choice = jnp.where(bed[r : r + 1] > 0.5, solved[:128, mine], solved[128:, mine])
            done.append(jnp.where(ice[r : r + 1] > 0.5, choice, moved[k]))
    return done


def first_substep_kernel(
    place_ref,
    grid_ref,
    kappa_ref,
    enthalpy_ref,
    speed_ref,
    below_ref,
    above_ref,
    left_ref,
    right_ref,
    inverses_ref,
    ice_ref,
    grounded_ref,
    surface_ref,
    flux_ref,
    out_ref,
    low_ref,
    high_ref,
    first_ref,
    last_ref,
    weights_ref,
):
    has_below, has_above, has_left, has_right = sides_inside(place_ref, grid_ref)
    below = jnp.where(has_below, below_ref[...], 0.0)
    above = jnp.where(has_above, above_ref[...], 0.0)
    left = jnp.where(has_left, left_ref[...], 0.0)
    right = jnp.where(has_right, right_ref[...], 0.0)
    weights = cell_weights(speed_ref, below[256:], above[256:], left[16:], right[16:])
    for k in range(9):
        weights_ref[k] = weights[k]
    edges = edge_products(weights, left[:16], right[:16])
    planes = [below[:128], below[128:256]]
    planes += [enthalpy_ref[pl.ds(x, 128, stride=8), :] for x in range(8)]
    planes += [above[:128], above[128:256]]
    done = substep(
        planes,
        weights,
        edges,
        inverses_ref[...],
        kappa_ref[0],
        ice_ref[...].astype(jnp.float32),
        grounded_ref[...].astype(jnp.float32),
        surface_ref[...],
        flux_ref[...],
    )
    for x in range(8):
        out_ref[x] = done[x]
    low_ref[0:128] = done[0]
    low_ref[128:256] = done[1]
    high_ref[0:128] = done[6]
    high_ref[128:256] = done[7]
    first_ref[...], last_ref[...] = column_tiles(done)


def sides_inside(place_ref, grid_ref):
    return (
        place_ref[0] > 0,
        place_ref[0] < grid_ref[0] - 1,
        place_ref[1] > 0,
        place_ref[1] < grid_ref[1] - 1,
    )


def second_substep_kernel(
    place_ref,
    grid_ref,
    kappa_ref,
    enthalpy_ref,
    below_ref,
    above_ref,
    left_ref,
    right_ref,
    weights_ref,
    inverses_ref,
    ice_ref,
    grounded_ref,
    surface_ref,
    flux_ref,
    speed_ref,
    thick_ref,
    height_ref,
    friction_ref,
    code_ref,
    out_ref,
    fields_ref,
):
    has_below, has_above, has_left, has_right = sides_inside(place_ref, grid_ref)
    below = jnp.where(has_below, below_ref[...], 0.0)
    above = jnp.where(has_above, above_ref[...], 0.0)
    left = jnp.where(has_left, left_ref[...], 0.0)
    right = jnp.where(has_right, right_ref[...], 0.0)
    weights = tuple(weights_ref[k] for k in range(9))
    edges = edge_products(weights, left, right)
    planes = [below[:128], below[128:256]]
    planes += [enthalpy_ref[x] for x in range(8)]
    planes += [above[:128], above[128:256]]
    ice = ice_ref[...]
    grounded = grounded_ref[...]
    done = substep(
        planes,
        weights,
        edges,
        inverses_ref[...],
        kappa_ref[0],
        ice.astype(jnp.float32),
        grounded.astype(jnp.float32),
        surface_ref[...],
        flux_ref[...],
    )
    means = []
    for x in range(8):
        out_ref[pl.ds(x, 128, stride=8), :] = done[x]
        means.append(jnp.sum(done[x], axis=0, keepdims=True))
    free = (code_ref[...] == 0) & (ice == 1)
    held = free | (code_ref[...] == 2)
    drag = jnp.where(grounded == 1, friction_ref[...], 0.0) + shelf_drag
    fields_ref[0] = jnp.where(held, speed_ref[0], 0.0)
    fields_ref[1] = jnp.where(held, speed_ref[1], 0.0)
    fields_ref[2] = jnp.where(free, drag, 0.0)
    fields_ref[3] = thick_ref[...]
    fields_ref[4] = jnp.exp(jnp.concatenate(means, axis=0) * (-soften / 128.0))
    fields_ref[5] = height_ref[...]


def exchanged(low, high, left, right):
    return (
        shifted(high, GX, 1),
        shifted(low, GX, -1),
        shifted(right, GY, 1),
        shifted(left, GY, -1),
    )


def shards(
    enthalpy,
    velocity_init,
    thickness,
    surface,
    friction,
    kappa,
    surface_enthalpy,
    geo_flux,
    ice_mask,
    grounded,
    boundary_code,
):
    f32 = jnp.float32
    struct = jax.ShapeDtypeStruct
    smem = pl.BlockSpec(memory_space=pltpu.SMEM)
    vmem = pl.BlockSpec(memory_space=pltpu.VMEM)
    place = jnp.stack([lax.axis_index(GX), lax.axis_index(GY)]).astype(jnp.int32)
    grid = jnp.array([lax.axis_size(GX), lax.axis_size(GY)], jnp.int32)
    flat = enthalpy.reshape(1024, 128)
    packed = pl.pallas_call(
        pack_kernel,
        out_shape=(struct((264, 128), f32),) * 2 + (struct((24, 128), f32),) * 2,
        name="pack",
    )(flat, velocity_init)
    around = exchanged(*packed)
    inverses = column_inverses(kappa)
    current, *packed, weights = pl.pallas_call(
        first_substep_kernel,
        out_shape=(struct((8, 128, 128), f32),)
        + (struct((256, 128), f32),) * 2
        + (struct((16, 128), f32),) * 2
        + (struct((9, 8, 128), f32),),
        in_specs=[smem] * 3 + [vmem] * 11,
        out_specs=(vmem,) * 6,
        name="first_substep",
    )(
        place,
        grid,
        kappa,
        flat,
        velocity_init,
        *around,
        inverses,
        ice_mask,
        grounded,
        surface_enthalpy,
        geo_flux,
    )
    around = exchanged(*packed)
    current, fields = pl.pallas_call(
        second_substep_kernel,
        out_shape=(struct((1024, 128), f32), struct((6, 8, 128), f32)),
        in_specs=[smem] * 3 + [vmem] * 16,
        out_specs=(vmem, vmem),
        name="second_substep",
    )(
        place,
        grid,
        kappa,
        current,
        *around,
        weights,
        inverses,
        ice_mask,
        grounded,
        surface_enthalpy,
        geo_flux,
        velocity_init,
        thickness,
        surface,
        friction,
        boundary_code,
    )
    quick, worst = momentum(fields, place, grid)

    def plain():
        free = ((boundary_code == 0) & (ice_mask == 1)).astype(f32)[None]
        drag_term = jnp.where(grounded == 1, friction, 0.0) + shelf_drag
        return plain_picard(fields[:2], thickness, fields[4], surface, drag_term, free)

    velocity = lax.cond(worst[0, 0] > PIVOT_FLOOR, lambda: quick, plain)
    return (current.reshape(enthalpy.shape), velocity)


def solution(mesh):
    torus = Mesh(mesh.devices.reshape(TORUS), ("gx_0", "gx_1", "gy_0", "gy_1"))
    placed = (
        P(None, GX, GY),
        P(None, GX, GY),
        P(GX, GY),
        P(GX, GY),
        P(GX, GY),
        P(),
        P(GX, GY),
        P(GX, GY),
        P(GX, GY),
        P(GX, GY),
        P(GX, GY),
    )
    return jax.shard_map(
        shards,
        mesh=torus,
        in_specs=placed,
        out_specs=(P(None, GX, GY), P(None, GX, GY)),
        check_vma=False,
    )
```

```python
import functools

import jax
import jax.numpy as jnp
from jax import lax
from jax.experimental import pallas as pl
from jax.experimental.pallas import tpu as pltpu
from jax.sharding import Mesh
from jax.sharding import PartitionSpec as P

PICARD = 2
KRYLOV = 6
TORUS = (4, 8, 8, 2)
GX_GY = ("gx_0", "gx_1", "gy_0", "gy_1")
GX = ("gx_0", "gx_1")
GY = ("gy_0", "gy_1")


soften = 0.3
shelf_drag = 0.2
strain_floor = 0.01

MIDDLE = 17.0
RADIUS = 17.0
PIVOT_FLOOR = 2e-4
OWN = 16
SIDE = 64


def with_halo(shard, sides, width):
    for axis, dim in sides:
        size, length = (lax.axis_size(axis), shard.shape[dim])
        up = [(i, (i + 1) % size) for i in range(size - 1)]
        down = [(j, i) for i, j in up]
        last = lax.slice_in_dim(shard, length - width, length, axis=dim)
        first = lax.slice_in_dim(shard, 0, width, axis=dim)
        before = lax.ppermute(last, axis, up)
        after = lax.ppermute(first, axis, down)
        shard = jnp.concatenate([before, shard, after], axis=dim)
    return shard


def one_axis_at_a_time(shard, axes):
    return functools.reduce(lax.psum, axes, shard)


def corner_mean(array):
    return 0.25 * (array[:-1, :-1] + array[1:, :-1] + array[:-1, 1:] + array[1:, 1:])


def diff_rows(array):
    return 0.5 * (array[1:, :-1] - array[:-1, :-1] + (array[1:, 1:] - array[:-1, 1:]))


def diff_cols(array):
    return 0.5 * (array[:-1, 1:] - array[:-1, :-1] + (array[1:, 1:] - array[1:, :-1]))


def back_rows(array):
    return 0.5 * (array[:-1, :-1] + array[:-1, 1:] - array[1:, :-1] - array[1:, 1:])


def back_cols(array):
    return 0.5 * (array[:-1, :-1] + array[1:, :-1] - array[:-1, 1:] - array[1:, 1:])


def strains(padded):
    stretch_x = diff_rows(padded[0])
    stretch_y = diff_cols(padded[1])
    shear_rate = 0.5 * (diff_cols(padded[0]) + diff_rows(padded[1]))
    return (stretch_x, stretch_y, shear_rate)


def viscous_weight(rates, thick_corner, stiff_corner):
    stretch_x, stretch_y, shear_rate = rates
    square = (
        stretch_x * stretch_x
        + stretch_y * stretch_y
        + stretch_x * stretch_y
        + shear_rate * shear_rate
    )
    return 0.5 * stiff_corner * thick_corner * jnp.power(square + strain_floor, -1.0 / 3.0)


def stress_image(rates, weight, center, drag_term):
    stretch_x, stretch_y, shear_rate = rates
    stress_x = weight * (4.0 * stretch_x + 2.0 * stretch_y)
    stress_y = weight * (4.0 * stretch_y + 2.0 * stretch_x)
    shear_stress = 2.0 * weight * shear_rate
    first = back_rows(stress_x) + back_cols(shear_stress) + drag_term * center[0]
    second = back_rows(shear_stress) + back_cols(stress_y) + drag_term * center[1]
    return jnp.stack([first, second])


def apply_field(direction, weight, drag_term, projector):
    padded = with_halo(direction, ((GX, 1), (GY, 2)), 1)
    return projector * stress_image(strains(padded), weight, direction, drag_term)


def inverse_kernel(kappa_ref, out_ref):
    levels = out_ref.shape[1]
    above = jnp.broadcast_to(kappa_ref[:, :levels], (8, levels))
    below = jnp.broadcast_to(kappa_ref[:, 1:], (8, levels))
    lane = lax.broadcasted_iota(jnp.int32, (8, levels), 1)
    rows = lax.broadcasted_iota(jnp.int32, (levels, levels), 0)
    cols = lax.broadcasted_iota(jnp.int32, (levels, levels), 1)
    floating = 1.0 + above + below
    on_bed = jnp.where(lane == levels - 1, 1.0 + above, floating)
    for k, diagonal in enumerate((on_bed, floating)):
        low = jnp.where(lane == 0, 0.0, -above)
        high = jnp.where(lane == levels - 1, 0.0, -below)
        mid = diagonal
        right = jnp.where(rows == cols, 1.0, 0.0)
        step = 1
        while step < levels:
            back = levels - step
            down = -low / pltpu.roll(mid, step, 1)
            up = -high / pltpu.roll(mid, back, 1)
            mid = mid + down * pltpu.roll(high, step, 1) + up * pltpu.roll(low, back, 1)
            low = down * pltpu.roll(low, step, 1)
            high = up * pltpu.roll(high, back, 1)
            right = (
                right
                + down[0:1] * pltpu.roll(right, step, 1)
                + up[0:1] * pltpu.roll(right, back, 1)
            )
            step *= 2
        out_ref[k * levels : (k + 1) * levels] = right * (1.0 / mid)[0:1]


def column_inverses(kappa):
    levels = kappa.shape[0] - 1
    return pl.pallas_call(
        inverse_kernel,
        out_shape=jax.ShapeDtypeStruct((2 * levels, levels), kappa.dtype),
        name="column_inverses",
    )(kappa[None])


def next_row(array):
    return pltpu.roll(array, array.shape[0] - 1, 0)


def next_col(array):
    return pltpu.roll(array, array.shape[1] - 1, 1)


def last_row(array):
    return pltpu.roll(array, 1, 0)


def last_col(array):
    return pltpu.roll(array, 1, 1)


def corner_rates(u, v):
    u_next = next_col(u)
    v_next = next_col(v)
    u_sum, u_diff = (u + u_next, u_next - u)
    v_sum, v_diff = (v + v_next, v_next - v)
    along = next_row(u_sum) - u_sum
    across = v_diff + next_row(v_diff)
    shear = u_diff + next_row(u_diff) + (next_row(v_sum) - v_sum)
    return (along, across, shear)


def stress_back(rates, half_weight):
    along, across, shear = rates
    stress_x = half_weight * (2.0 * along + across)
    stress_y = half_weight * (2.0 * across + along)
    stress_s = 0.5 * half_weight * shear
    x_before = last_col(stress_x)
    y_before = last_col(stress_y)
    s_before = last_col(stress_s)
    x_sum, s_diff = (stress_x + x_before, s_before - stress_s)
    s_sum, y_diff = (stress_s + s_before, y_before - stress_y)
    first = last_row(x_sum + s_diff) + (s_diff - x_sum)
    second = last_row(s_sum + y_diff) + (y_diff - s_sum)
    return (first, second)


def half_weights(rates, corner_product):
    along, across, shear = rates
    square = 0.25 * (along * along + across * across + along * across) + 0.0625 * shear * shear
    return corner_product * jnp.exp(jnp.log(square + strain_floor) * (-1.0 / 3.0))


def krylov_basis(u, v, drag, driving, corner_product, own_row, keep):
    free = drag > 0.0
    rates = corner_rates(u, v)
    half_weight = half_weights(rates, corner_product)
    first, second = stress_back(rates, half_weight)
    r_u = jnp.where(free, driving[0] - first - drag * u, 0.0)
    r_v = jnp.where(free, driving[1] - second - drag * v, 0.0)

    def own(array):
        return array[own_row : own_row + 8, :128]

    basis_u, basis_v = ([r_u], [r_v])
    own_basis, own_image = ([(own(r_u), own(r_v))], [])
    keep(0, r_u, r_v)
    for k in range(KRYLOV):
        b_u, b_v = (basis_u[k], basis_v[k])
        first, second = stress_back(corner_rates(b_u, b_v), half_weight)
        a_u = jnp.where(free, first, 0.0) + drag * b_u
        a_v = jnp.where(free, second, 0.0) + drag * b_v
        own_image.append((own(a_u), own(a_v)))
        if k + 1 < KRYLOV:
            scale = (1.0 if k == 0 else 2.0) / RADIUS
            n_u = scale * a_u - (scale * MIDDLE) * b_u
            n_v = scale * a_v - (scale * MIDDLE) * b_v
            if k > 0:
                n_u = n_u - basis_u[k - 1]
                n_v = n_v - basis_v[k - 1]
            basis_u.append(n_u)
            basis_v.append(n_v)
            own_basis.append((own(n_u), own(n_v)))
            keep(k + 1, n_u, n_v)
    products = []
    for i in range(KRYLOV):
        for j in range(i, KRYLOV):
            products.append(
                own_basis[i][0] * own_image[j][0] + own_basis[i][1] * own_image[j][1]
            )
    for i in range(KRYLOV):
        products.append(own_basis[i][0] * own_basis[0][0] + own_basis[i][1] * own_basis[0][1])
    return products


def write_sums(products, out_ref):
    count = out_ref.shape[0]
    lines = [jnp.sum(p, axis=0, keepdims=True) for p in products]
    lines.append(jnp.zeros((128 - len(lines), 128), jnp.float32))
    table = jnp.concatenate(lines, axis=0)
    out_ref[...] = lax.dot_general(
        jnp.ones((count, 128), jnp.float32),
        table,
        (((1,), (1,)), ((), ())),
        precision=lax.Precision.HIGHEST,
        preferred_element_type=jnp.float32,
    )


def small_solve(parts):
    sums = jnp.broadcast_to(jnp.sum(parts, axis=0, keepdims=True), (8, 128))
    at = lambda k: jnp.broadcast_to(sums[:, k : k + 1], (8, 128))
    system = {}
    k = 0
    for i in range(KRYLOV):
        for j in range(i, KRYLOV):
            system[i, j] = at(k)
            k += 1
    start = [system[i, i] for i in range(KRYLOV)]
    right = [at(k + i) for i in range(KRYLOV)]
    least = None
    for p in range(KRYLOV):
        relative = system[p, p] / start[p]
        least = relative if least is None else jnp.minimum(least, relative)
        inverse = 1.0 / system[p, p]
        for i in range(p + 1, KRYLOV):
            factor = system[p, i] * inverse
            for j in range(i, KRYLOV):
                system[i, j] = system[i, j] - factor * system[p, j]
            right[i] = right[i] - factor * right[p]
        system[p, p] = inverse
    answer = [None] * KRYLOV
    for i in reversed(range(KRYLOV)):
        value = right[i]
        for m in range(i + 1, KRYLOV):
            value = value - system[i, m] * answer[m]
        answer[i] = value * system[i, i]
    return (answer, least)


def where_am_i():
    place = []
    for axes in (GX, GY):
        major, minor = axes
        length = lax.axis_size(minor)
        place.append((lax.axis_index(major) * length + lax.axis_index(minor)))
    return (place[0], place[1], lax.axis_size(GX), lax.axis_size(GY))


def first_picard_kernel(statics_ref, left_ref, right_ref, stiff_ref, basis_ref, fixed_ref, sums_ref):
    gx, gy, gx_size, gy_size = where_am_i()
    rows = 40
    lane = lax.broadcasted_iota(jnp.int32, (rows, 128), 1)
    row = lax.broadcasted_iota(jnp.int32, (rows, 128), 0) + (gx * 8 - OWN)
    row_in = (row >= 0) & (row < gx_size * 8)
    from_right = lane < SIDE
    col = gy + jnp.where(from_right, 1, -1)
    side_in = row_in & (col >= 0) & (col < gy_size)

    def field(k):
        part = slice(k * rows, k * rows + rows)
        side = jnp.where(from_right, right_ref[part], left_ref[part])
        return jnp.concatenate(
            [jnp.where(row_in, statics_ref[part], 0.0), jnp.where(side_in, side, 0.0)], axis=1
        )

    u, v, drag, thick, surface = (field(k) for k in range(5))
    blocks = [stiff_ref[jnp.clip(gx + k, 0, gx_size - 1)] for k in range(-2, 3)]
    stiff = jnp.concatenate(blocks, axis=0)
    stiff = jnp.where(jnp.concatenate([row_in, side_in], axis=1), stiff, 0.0)
    t_sum = thick + next_col(thick)
    s_sum = stiff + next_col(stiff)
    corner_product = (1.0 / 64.0) * (t_sum + next_row(t_sum)) * (s_sum + next_row(s_sum))
    driving = (
        -thick * 0.5 * (next_row(surface) - last_row(surface)),
        -thick * 0.5 * (next_col(surface) - last_col(surface)),
    )
    kept = slice(OWN - 8, OWN + 16)

    def keep(k, b_u, b_v):
        basis_ref[2 * k] = b_u[kept]
        basis_ref[2 * k + 1] = b_v[kept]

    for k, value in enumerate((u, v, drag, corner_product, driving[0], driving[1])):
        fixed_ref[k] = value[kept]
    products = krylov_basis(u, v, drag, driving, corner_product, OWN, keep)
    write_sums(products, sums_ref)


def second_picard_kernel(
    parts_ref, basis_ref, fixed_ref, next_ref, velocity_ref, sums_ref, least_ref
):
    answer, least = small_solve(parts_ref[...])
    u, v = (fixed_ref[0], fixed_ref[1])
    for k in range(KRYLOV):
        scale = jnp.tile(answer[k], (3, 2))
        u = u + scale * basis_ref[2 * k]
        v = v + scale * basis_ref[2 * k + 1]
    velocity_ref[0] = u[8:16, :128]
    velocity_ref[1] = v[8:16, :128]
    least_ref[...] = least

    def keep(k, b_u, b_v):
        next_ref[2 * k] = b_u[8:16, :128]
        next_ref[2 * k + 1] = b_v[8:16, :128]

    driving = (fixed_ref[4], fixed_ref[5])
    products = krylov_basis(u, v, fixed_ref[2], driving, fixed_ref[3], 8, keep)
    write_sums(products, sums_ref)


def last_kernel(parts_ref, basis_ref, velocity_ref, least_ref, out_ref, worst_ref):
    answer, least = small_solve(parts_ref[...])
    u, v = (velocity_ref[0], velocity_ref[1])
    for k in range(KRYLOV):
        u = u + answer[k] * basis_ref[2 * k]
        v = v + answer[k] * basis_ref[2 * k + 1]
    out_ref[0] = u
    out_ref[1] = v
    worst_ref[0, 0] = jnp.min(jnp.minimum(least_ref[...], least))


def over_all(sums):
    count = lax.axis_size(GX)
    part = lax.all_to_all(sums, GY, 0, 0, tiled=True)
    part = jnp.broadcast_to(jnp.sum(part, axis=0, keepdims=True), (count, 128))
    return lax.all_to_all(part, GX, 0, 0, tiled=True)


def shifted(array, axis, by):
    size = lax.axis_size(axis)
    return lax.ppermute(array, axis, [(i, (i + by) % size) for i in range(size)])


def momentum(statics):
    f32 = jnp.float32
    struct = jax.ShapeDtypeStruct
    smem = pl.BlockSpec(memory_space=pltpu.SMEM)
    vmem = pl.BlockSpec(memory_space=pltpu.VMEM)
    gx, gy = (lax.axis_size(GX), lax.axis_size(GY))
    left = shifted(statics, GY, 1)
    right = shifted(statics, GY, -1)
    lane = lax.broadcasted_iota(jnp.int32, (8, 128), 1)
    side = jnp.where(lane < SIDE, right[200:], left[200:])
    strip = jnp.concatenate([statics[200:], side], axis=1)
    strip = lax.all_to_all(jnp.broadcast_to(strip[None], (gx, 8, 256)), GX, 0, 0, tiled=True)
    basis, fixed, sums = pl.pallas_call(
        first_picard_kernel,
        out_shape=(
            struct((2 * KRYLOV, 24, 256), f32),
            struct((6, 24, 256), f32),
            struct((gy, 128), f32),
        ),
        name="first_picard",
    )(statics, left, right, strip)
    basis, velocity, sums, least = pl.pallas_call(
        second_picard_kernel,
        out_shape=(
            struct((2 * KRYLOV, 8, 128), f32),
            struct((2, 8, 128), f32),
            struct((gy, 128), f32),
            struct((8, 128), f32),
        ),
        name="second_picard",
    )(over_all(sums), basis, fixed)
    return pl.pallas_call(
        last_kernel,
        out_shape=(struct((2, 8, 128), f32), struct((1, 1), f32)),
        out_specs=(vmem, smem),
        name="last_picard",
    )(over_all(sums), basis, velocity, least)


def plain_picard(velocity, thickness, stiffness, surface, drag_term, projector):
    statics = with_halo(jnp.stack([thickness, stiffness, surface]), ((GX, 1), (GY, 2)), 1)
    thick_corner = corner_mean(statics[0])
    stiff_corner = corner_mean(statics[1])
    heights = statics[2]
    driving = jnp.stack(
        [
            -thickness * 0.5 * (heights[2:, 1:-1] - heights[:-2, 1:-1]),
            -thickness * 0.5 * (heights[1:-1, 2:] - heights[1:-1, :-2]),
        ]
    )

    def total(array):
        return one_axis_at_a_time(jnp.sum(array), GX_GY)

    def picard(_, velocity):
        rates = strains(with_halo(velocity, ((GX, 1), (GY, 2)), 1))
        weight = viscous_weight(rates, thick_corner, stiff_corner)
        residual = projector * (driving - stress_image(rates, weight, velocity, drag_term))

        def krylov(_, state):
            change, residual, direction, norm_now = state
            imaged = apply_field(direction, weight, drag_term, projector)
            step_size = norm_now / total(direction * imaged)
            change = change + step_size * direction
            residual = residual - step_size * imaged
            norm_next = total(residual * residual)
            direction = residual + norm_next / norm_now * direction
            return (change, residual, direction, norm_next)

        state = (jnp.zeros_like(velocity), residual, residual, total(residual * residual))
        return velocity + lax.fori_loop(0, KRYLOV, krylov, state)[0]

    return lax.fori_loop(0, PICARD, picard, velocity)


def column_tiles(planes):
    shape = (32, 1024)
    line = lax.broadcasted_iota(jnp.int32, shape, 0)
    spot = lax.broadcasted_iota(jnp.int32, shape, 1)
    within = line & 15
    column = jnp.where(line < 16, 0, 126) + (within & 1)
    pick = jnp.where(spot == (within >> 1) * 128 + column, 1.0, 0.0)
    tiles = lax.dot_general(
        pick,
        jnp.concatenate(planes, axis=1),
        (((1,), (1,)), ((), ())),
        precision=lax.Precision.HIGHEST,
        preferred_element_type=jnp.float32,
    )
    return (tiles[:16], tiles[16:])


def pack_kernel(
    enthalpy_ref,
    speed_ref,
    thick_ref,
    height_ref,
    friction_ref,
    ice_ref,
    grounded_ref,
    code_ref,
    low_ref,
    high_ref,
    left_ref,
    right_ref,
):
    planes = [enthalpy_ref[pl.ds(x, 128, stride=8), :] for x in range(8)]
    free = (code_ref[...] == 0) & (ice_ref[...] == 1)
    held = free | (code_ref[...] == 2)
    drag = jnp.where(grounded_ref[...] == 1, friction_ref[...], 0.0) + shelf_drag
    statics = (
        jnp.where(held, speed_ref[0], 0.0),
        jnp.where(held, speed_ref[1], 0.0),
        jnp.where(free, drag, 0.0),
        thick_ref[...],
        height_ref[...],
        speed_ref[0],
    )
    for out_ref, pair in ((low_ref, (0, 1)), (high_ref, (6, 7))):
        out_ref[0:128] = planes[pair[0]]
        out_ref[128:256] = planes[pair[1]]
        for k, value in enumerate(statics):
            out_ref[256 + 8 * k : 264 + 8 * k] = value
    first, last = column_tiles(planes)
    left_ref[0:16] = first
    left_ref[16:24] = speed_ref[1]
    right_ref[0:16] = last
    right_ref[16:24] = speed_ref[1]


def line_weights(low_face, high_face):
    p_high, m_high = (jnp.maximum(high_face, 0.0), jnp.minimum(high_face, 0.0))
    p_low, m_low = (jnp.maximum(low_face, 0.0), jnp.minimum(low_face, 0.0))
    q_high, n_high = (0.25 * p_high * (1.0 - p_high), 0.25 * m_high * (1.0 + m_high))
    q_low, n_low = (0.25 * p_low * (1.0 - p_low), 0.25 * m_low * (1.0 + m_low))
    return (
        -q_low,
        q_high + (p_low + n_low),
        (q_low + m_low) - (p_high + n_high),
        -(q_high + m_high) - n_low,
        n_high,
    )


def cell_weights(speed_ref, before_x, after_x, before_y, after_y):
    c_x, c_y = (speed_ref[0], speed_ref[1])
    row = lax.broadcasted_iota(jnp.int32, (8, 128), 0)
    lane = lax.broadcasted_iota(jnp.int32, (8, 128), 1)
    x_before = jnp.where(row == 0, pltpu.roll(before_x, 1, 0), pltpu.roll(c_x, 1, 0))
    x_after = jnp.where(row == 7, pltpu.roll(after_x, 7, 0), pltpu.roll(c_x, 7, 0))
    y_before = jnp.where(lane == 0, pltpu.roll(before_y, 1, 1), pltpu.roll(c_y, 1, 1))
    y_after = jnp.where(lane == 127, pltpu.roll(after_y, 127, 1), pltpu.roll(c_y, 127, 1))
    along_x = line_weights(0.5 * (x_before + c_x), 0.5 * (c_x + x_after))
    along_y = line_weights(0.5 * (y_before + c_y), 0.5 * (c_y + y_after))
    center = 1.0 + along_x[2] + along_y[2]
    return (center,) + along_x[:2] + along_x[3:] + along_y[:2] + along_y[3:]


def edge_products(weights, before_y, after_y):
    line = lax.broadcasted_iota(jnp.int32, (32, 128), 0)
    lane = lax.broadcasted_iota(jnp.int32, (32, 128), 1)
    back_2, back_1, ahead_1, ahead_2 = weights[5:]
    spread = []
    for x in range(8):
        b_2, b_1, a_1, a_2 = (w[x : x + 1] for w in (back_2, back_1, ahead_1, ahead_2))
        far = (line == 2 * x) & (lane == 0)
        far = far | ((line == 2 * x + 1) & (lane == 1))
        value = jnp.where(far, b_2, 0.0)
        value = jnp.where((line == 2 * x + 1) & (lane == 0), b_1, value)
        far = (line == 16 + 2 * x) & (lane == 126)
        far = far | ((line == 17 + 2 * x) & (lane == 127))
        value = jnp.where(far, a_2, value)
        value = jnp.where((line == 16 + 2 * x) & (lane == 127), a_1, value)
        spread.append(value)
    return lax.dot_general(
        jnp.concatenate([before_y, after_y], axis=0),
        jnp.concatenate(spread, axis=1),
        (((0,), (0,)), ((), ())),
        precision=lax.Precision.HIGHEST,
        preferred_element_type=jnp.float32,
    )


def substep(planes, weights, edges, inverses, first_kappa, ice, bed, surface_heat, heat_flux):
    lane = lax.broadcasted_iota(jnp.int32, (8, 128), 1)
    center, x_b2, x_b1, x_a1, x_a2, y_b2, y_b1, y_a1, y_a2 = weights
    y_b2 = jnp.where(lane < 2, 0.0, y_b2)
    y_b1 = jnp.where(lane < 1, 0.0, y_b1)
    y_a1 = jnp.where(lane > 126, 0.0, y_a1)
    y_a2 = jnp.where(lane > 125, 0.0, y_a2)
    level = lax.broadcasted_iota(jnp.int32, (128, 128), 0)
    done = []
    for x in range(0, 8, 2):
        moved, sides = ([], [])
        for r in (x, x + 1):
            at = lambda w: w[r : r + 1]
            e = planes[r + 2]
            value = at(center) * e + edges[:, r * 128 : r * 128 + 128]
            value = value + at(x_b2) * planes[r] + at(x_b1) * planes[r + 1]
            value = value + at(x_a1) * planes[r + 3] + at(x_a2) * planes[r + 4]
            value = value + at(y_b2) * pltpu.roll(e, 2, 1) + at(y_b1) * pltpu.roll(e, 1, 1)
            value = value + at(y_a1) * pltpu.roll(e, 127, 1) + at(y_a2) * pltpu.roll(e, 126, 1)
            moved.append(value)
            top = first_kappa * at(surface_heat)
            bottom = at(bed) * at(heat_flux)
            sides.append(
                value + jnp.where(level == 0, top, jnp.where(level == 127, bottom, 0.0))
            )
        solved = jnp.dot(
            inverses,
            jnp.concatenate(sides, axis=1),
            precision=lax.Precision.HIGHEST,
            preferred_element_type=jnp.float32,
        )
        for k, r in enumerate((x, x + 1)):
            mine = slice(k * 128, k * 128 + 128)
            choice = jnp.where(bed[r : r + 1] > 0.5, solved[:128, mine], solved[128:, mine])
            done.append(jnp.where(ice[r : r + 1] > 0.5, choice, moved[k]))
    return done


def inside(below_ref, above_ref, left_ref, right_ref):
    gx, gy, gx_size, gy_size = where_am_i()
    return (
        jnp.where(gx > 0, below_ref[...], 0.0),
        jnp.where(gx < gx_size - 1, above_ref[...], 0.0),
        jnp.where(gy > 0, left_ref[...], 0.0),
        jnp.where(gy < gy_size - 1, right_ref[...], 0.0),
    )


def first_substep_kernel(
    kappa_ref,
    enthalpy_ref,
    speed_ref,
    below_ref,
    above_ref,
    left_ref,
    right_ref,
    inverses_ref,
    ice_ref,
    grounded_ref,
    surface_ref,
    flux_ref,
    out_ref,
    low_ref,
    high_ref,
    first_ref,
    last_ref,
    weights_ref,
):
    below, above, left, right = inside(below_ref, above_ref, left_ref, right_ref)
    weights = cell_weights(speed_ref, below[296:], above[296:], left[16:], right[16:])
    for k in range(9):
        weights_ref[k] = weights[k]
    edges = edge_products(weights, left[:16], right[:16])
    planes = [below[:128], below[128:256]]
    planes += [enthalpy_ref[pl.ds(x, 128, stride=8), :] for x in range(8)]
    planes += [above[:128], above[128:256]]
    done = substep(
        planes,
        weights,
        edges,
        inverses_ref[...],
        kappa_ref[0],
        ice_ref[...].astype(jnp.float32),
        grounded_ref[...].astype(jnp.float32),
        surface_ref[...],
        flux_ref[...],
    )
    for x in range(8):
        out_ref[x] = done[x]
    low_ref[0:128] = done[0]
    low_ref[128:256] = done[1]
    low_ref[256:296] = above[256:296]
    high_ref[0:128] = done[6]
    high_ref[128:256] = done[7]
    high_ref[256:296] = below[256:296]
    first_ref[...], last_ref[...] = column_tiles(done)


def second_substep_kernel(
    kappa_ref,
    enthalpy_ref,
    below_ref,
    above_ref,
    left_ref,
    right_ref,
    weights_ref,
    inverses_ref,
    ice_ref,
    grounded_ref,
    surface_ref,
    flux_ref,
    near_below_ref,
    near_above_ref,
    mine_ref,
    out_ref,
    statics_ref,
):
    below, above, left, right = inside(below_ref, above_ref, left_ref, right_ref)
    weights = tuple(weights_ref[k] for k in range(9))
    edges = edge_products(weights, left, right)
    planes = [below[:128], below[128:256]]
    planes += [enthalpy_ref[x] for x in range(8)]
    planes += [above[:128], above[128:256]]
    done = substep(
        planes,
        weights,
        edges,
        inverses_ref[...],
        kappa_ref[0],
        ice_ref[...].astype(jnp.float32),
        grounded_ref[...].astype(jnp.float32),
        surface_ref[...],
        flux_ref[...],
    )
    means = []
    for x in range(8):
        out_ref[pl.ds(x, 128, stride=8), :] = done[x]
        means.append(jnp.sum(done[x], axis=0, keepdims=True))
    blocks = (below_ref, near_below_ref, mine_ref, near_above_ref, above_ref)
    for k in range(5):
        for b, block_ref in enumerate(blocks):
            row = 40 * k + 8 * b
            statics_ref[row : row + 8] = block_ref[256 + 8 * k : 264 + 8 * k]
    statics_ref[200:208] = jnp.exp(jnp.concatenate(means, axis=0) * (-soften / 128.0))


def exchanged(low, high, left, right):
    return (
        shifted(high, GX, 1),
        shifted(low, GX, -1),
        shifted(right, GY, 1),
        shifted(left, GY, -1),
    )


def shards(
    enthalpy,
    velocity_init,
    thickness,
    surface,
    friction,
    kappa,
    surface_enthalpy,
    geo_flux,
    ice_mask,
    grounded,
    boundary_code,
):
    f32 = jnp.float32
    struct = jax.ShapeDtypeStruct
    smem = pl.BlockSpec(memory_space=pltpu.SMEM)
    vmem = pl.BlockSpec(memory_space=pltpu.VMEM)
    flat = enthalpy.reshape(1024, 128)
    packed = pl.pallas_call(
        pack_kernel,
        out_shape=(struct((304, 128), f32),) * 2 + (struct((24, 128), f32),) * 2,
        name="pack",
    )(flat, velocity_init, thickness, surface, friction, ice_mask, grounded, boundary_code)
    mine = packed[0]
    near = exchanged(*packed)
    inverses = column_inverses(kappa)
    columns = (ice_mask, grounded, surface_enthalpy, geo_flux)
    current, *packed, weights = pl.pallas_call(
        first_substep_kernel,
        out_shape=(struct((8, 128, 128), f32),)
        + (struct((296, 128), f32),) * 2
        + (struct((16, 128), f32),) * 2
        + (struct((9, 8, 128), f32),),
        in_specs=[smem] + [vmem] * 11,
        out_specs=(vmem,) * 6,
        name="first_substep",
    )(kappa, flat, velocity_init, *near, inverses, *columns)
    around = exchanged(*packed)
    current, statics = pl.pallas_call(
        second_substep_kernel,
        out_shape=(struct((1024, 128), f32), struct((208, 128), f32)),
        in_specs=[smem] + [vmem] * 14,
        out_specs=(vmem, vmem),
        name="second_substep",
    )(kappa, current, *around, weights, inverses, *columns, near[0], near[1], mine)
    quick, worst = momentum(statics)

    def plain():
        free_cells = (boundary_code == 0) & (ice_mask == 1)
        held_cells = free_cells | (boundary_code == 2)
        projector = free_cells.astype(f32)[None]
        drag_term = jnp.where(grounded == 1, friction, 0.0) + shelf_drag
        velocity = jnp.where(held_cells[None], velocity_init, 0.0)
        return plain_picard(
            velocity, thickness, statics[200:], surface, drag_term, projector
        )

    velocity = lax.cond(worst[0, 0] > PIVOT_FLOOR, lambda: quick, plain)
    return (current.reshape(enthalpy.shape), velocity)


def solution(mesh):
    torus = Mesh(mesh.devices.reshape(TORUS), ("gx_0", "gx_1", "gy_0", "gy_1"))
    placed = (
        P(None, GX, GY),
        P(None, GX, GY),
        P(GX, GY),
        P(GX, GY),
        P(GX, GY),
        P(),
        P(GX, GY),
        P(GX, GY),
        P(GX, GY),
        P(GX, GY),
        P(GX, GY),
    )
    return jax.shard_map(
        shards,
        mesh=torus,
        in_specs=placed,
        out_specs=(P(None, GX, GY), P(None, GX, GY)),
        check_vma=False,
    )
```

```python
import functools

import jax
import jax.numpy as jnp
from jax import lax
from jax.experimental import pallas as pl
from jax.experimental.pallas import tpu as pltpu
from jax.sharding import Mesh
from jax.sharding import PartitionSpec as P

PICARD = 2
KRYLOV = 6
TORUS = (4, 8, 8, 2)
GX_GY = ("gx_0", "gx_1", "gy_0", "gy_1")
GX = ("gx_0", "gx_1")
GY = ("gy_0", "gy_1")


soften = 0.3
shelf_drag = 0.2
strain_floor = 0.01

MIDDLE = 17.0
RADIUS = 17.0
PIVOT_FLOOR = 2e-4
OWN = 16
SIDE = 64


def with_halo(shard, sides, width):
    for axis, dim in sides:
        size, length = (lax.axis_size(axis), shard.shape[dim])
        up = [(i, (i + 1) % size) for i in range(size - 1)]
        down = [(j, i) for i, j in up]
        last = lax.slice_in_dim(shard, length - width, length, axis=dim)
        first = lax.slice_in_dim(shard, 0, width, axis=dim)
        before = lax.ppermute(last, axis, up)
        after = lax.ppermute(first, axis, down)
        shard = jnp.concatenate([before, shard, after], axis=dim)
    return shard


def one_axis_at_a_time(shard, axes):
    return functools.reduce(lax.psum, axes, shard)


def corner_mean(array):
    return 0.25 * (array[:-1, :-1] + array[1:, :-1] + array[:-1, 1:] + array[1:, 1:])


def diff_rows(array):
    return 0.5 * (array[1:, :-1] - array[:-1, :-1] + (array[1:, 1:] - array[:-1, 1:]))


def diff_cols(array):
    return 0.5 * (array[:-1, 1:] - array[:-1, :-1] + (array[1:, 1:] - array[1:, :-1]))


def back_rows(array):
    return 0.5 * (array[:-1, :-1] + array[:-1, 1:] - array[1:, :-1] - array[1:, 1:])


def back_cols(array):
    return 0.5 * (array[:-1, :-1] + array[1:, :-1] - array[:-1, 1:] - array[1:, 1:])


def strains(padded):
    stretch_x = diff_rows(padded[0])
    stretch_y = diff_cols(padded[1])
    shear_rate = 0.5 * (diff_cols(padded[0]) + diff_rows(padded[1]))
    return (stretch_x, stretch_y, shear_rate)


def viscous_weight(rates, thick_corner, stiff_corner):
    stretch_x, stretch_y, shear_rate = rates
    square = (
        stretch_x * stretch_x
        + stretch_y * stretch_y
        + stretch_x * stretch_y
        + shear_rate * shear_rate
    )
    return 0.5 * stiff_corner * thick_corner * jnp.power(square + strain_floor, -1.0 / 3.0)


def stress_image(rates, weight, center, drag_term):
    stretch_x, stretch_y, shear_rate = rates
    stress_x = weight * (4.0 * stretch_x + 2.0 * stretch_y)
    stress_y = weight * (4.0 * stretch_y + 2.0 * stretch_x)
    shear_stress = 2.0 * weight * shear_rate
    first = back_rows(stress_x) + back_cols(shear_stress) + drag_term * center[0]
    second = back_rows(shear_stress) + back_cols(stress_y) + drag_term * center[1]
    return jnp.stack([first, second])


def apply_field(direction, weight, drag_term, projector):
    padded = with_halo(direction, ((GX, 1), (GY, 2)), 1)
    return projector * stress_image(strains(padded), weight, direction, drag_term)


def inverse_kernel(kappa_ref, out_ref):
    levels = out_ref.shape[1]
    above = jnp.broadcast_to(kappa_ref[:, :levels], (8, levels))
    below = jnp.broadcast_to(kappa_ref[:, 1:], (8, levels))
    lane = lax.broadcasted_iota(jnp.int32, (8, levels), 1)
    rows = lax.broadcasted_iota(jnp.int32, (levels, levels), 0)
    cols = lax.broadcasted_iota(jnp.int32, (levels, levels), 1)
    floating = 1.0 + above + below
    on_bed = jnp.where(lane == levels - 1, 1.0 + above, floating)
    for k, diagonal in enumerate((on_bed, floating)):
        low = jnp.where(lane == 0, 0.0, -above)
        high = jnp.where(lane == levels - 1, 0.0, -below)
        mid = diagonal
        right = jnp.where(rows == cols, 1.0, 0.0)
        step = 1
        while step < levels:
            back = levels - step
            down = -low / pltpu.roll(mid, step, 1)
            up = -high / pltpu.roll(mid, back, 1)
            mid = mid + down * pltpu.roll(high, step, 1) + up * pltpu.roll(low, back, 1)
            low = down * pltpu.roll(low, step, 1)
            high = up * pltpu.roll(high, back, 1)
            right = (
                right
                + down[0:1] * pltpu.roll(right, step, 1)
                + up[0:1] * pltpu.roll(right, back, 1)
            )
            step *= 2
        out_ref[k * levels : (k + 1) * levels] = right * (1.0 / mid)[0:1]


def column_inverses(kappa):
    levels = kappa.shape[0] - 1
    return pl.pallas_call(
        inverse_kernel,
        out_shape=kept(2 * levels, levels),
        name="column_inverses",
    )(kappa[None])


def on_chip(array):
    return pltpu.with_memory_space_constraint(array, pltpu.VMEM)


def kept(*shape):
    return pltpu.VMEM(shape, jnp.float32)


def next_row(array):
    return pltpu.roll(array, array.shape[0] - 1, 0)


def next_col(array):
    return pltpu.roll(array, array.shape[1] - 1, 1)


def last_row(array):
    return pltpu.roll(array, 1, 0)


def last_col(array):
    return pltpu.roll(array, 1, 1)


def corner_rates(u, v):
    u_next = next_col(u)
    v_next = next_col(v)
    u_sum, u_diff = (u + u_next, u_next - u)
    v_sum, v_diff = (v + v_next, v_next - v)
    along = next_row(u_sum) - u_sum
    across = v_diff + next_row(v_diff)
    shear = u_diff + next_row(u_diff) + (next_row(v_sum) - v_sum)
    return (along, across, shear)


def stress_back(rates, half_weight):
    along, across, shear = rates
    stress_x = half_weight * (2.0 * along + across)
    stress_y = half_weight * (2.0 * across + along)
    stress_s = 0.5 * half_weight * shear
    x_before = last_col(stress_x)
    y_before = last_col(stress_y)
    s_before = last_col(stress_s)
    x_sum, s_diff = (stress_x + x_before, s_before - stress_s)
    s_sum, y_diff = (stress_s + s_before, y_before - stress_y)
    first = last_row(x_sum + s_diff) + (s_diff - x_sum)
    second = last_row(s_sum + y_diff) + (y_diff - s_sum)
    return (first, second)


def half_weights(rates, corner_product):
    along, across, shear = rates
    square = 0.25 * (along * along + across * across + along * across) + 0.0625 * shear * shear
    return corner_product * jnp.exp(jnp.log(square + strain_floor) * (-1.0 / 3.0))


def krylov_basis(u, v, drag, driving, corner_product, own_row, keep):
    free = drag > 0.0
    rates = corner_rates(u, v)
    half_weight = half_weights(rates, corner_product)
    first, second = stress_back(rates, half_weight)
    r_u = jnp.where(free, driving[0] - first - drag * u, 0.0)
    r_v = jnp.where(free, driving[1] - second - drag * v, 0.0)

    def own(array):
        return array[own_row : own_row + 8, :128]

    basis_u, basis_v = ([r_u], [r_v])
    own_basis, own_image = ([(own(r_u), own(r_v))], [])
    keep(0, r_u, r_v)
    for k in range(KRYLOV):
        b_u, b_v = (basis_u[k], basis_v[k])
        first, second = stress_back(corner_rates(b_u, b_v), half_weight)
        a_u = jnp.where(free, first, 0.0) + drag * b_u
        a_v = jnp.where(free, second, 0.0) + drag * b_v
        own_image.append((own(a_u), own(a_v)))
        if k + 1 < KRYLOV:
            scale = (1.0 if k == 0 else 2.0) / RADIUS
            n_u = scale * a_u - (scale * MIDDLE) * b_u
            n_v = scale * a_v - (scale * MIDDLE) * b_v
            if k > 0:
                n_u = n_u - basis_u[k - 1]
                n_v = n_v - basis_v[k - 1]
            basis_u.append(n_u)
            basis_v.append(n_v)
            own_basis.append((own(n_u), own(n_v)))
            keep(k + 1, n_u, n_v)
    products = []
    for i in range(KRYLOV):
        for j in range(i, KRYLOV):
            products.append(
                own_basis[i][0] * own_image[j][0] + own_basis[i][1] * own_image[j][1]
            )
    for i in range(KRYLOV):
        products.append(own_basis[i][0] * own_basis[0][0] + own_basis[i][1] * own_basis[0][1])
    return products


def write_sums(products, out_ref):
    count = out_ref.shape[0]
    lines = [jnp.sum(p, axis=0, keepdims=True) for p in products]
    lines.append(jnp.zeros((128 - len(lines), 128), jnp.float32))
    table = jnp.concatenate(lines, axis=0)
    out_ref[...] = lax.dot_general(
        jnp.ones((count, 128), jnp.float32),
        table,
        (((1,), (1,)), ((), ())),
        precision=lax.Precision.HIGHEST,
        preferred_element_type=jnp.float32,
    )


def small_solve(parts):
    sums = jnp.broadcast_to(jnp.sum(parts, axis=0, keepdims=True), (8, 128))
    at = lambda k: jnp.broadcast_to(sums[:, k : k + 1], (8, 128))
    system = {}
    k = 0
    for i in range(KRYLOV):
        for j in range(i, KRYLOV):
            system[i, j] = at(k)
            k += 1
    start = [system[i, i] for i in range(KRYLOV)]
    right = [at(k + i) for i in range(KRYLOV)]
    least = None
    for p in range(KRYLOV):
        relative = system[p, p] / start[p]
        least = relative if least is None else jnp.minimum(least, relative)
        inverse = 1.0 / system[p, p]
        for i in range(p + 1, KRYLOV):
            factor = system[p, i] * inverse
            for j in range(i, KRYLOV):
                system[i, j] = system[i, j] - factor * system[p, j]
            right[i] = right[i] - factor * right[p]
        system[p, p] = inverse
    answer = [None] * KRYLOV
    for i in reversed(range(KRYLOV)):
        value = right[i]
        for m in range(i + 1, KRYLOV):
            value = value - system[i, m] * answer[m]
        answer[i] = value * system[i, i]
    return (answer, least)


def where_am_i():
    place = []
    for axes in (GX, GY):
        major, minor = axes
        length = lax.axis_size(minor)
        place.append((lax.axis_index(major) * length + lax.axis_index(minor)))
    return (place[0], place[1], lax.axis_size(GX), lax.axis_size(GY))


def first_picard_kernel(statics_ref, left_ref, right_ref, stiff_ref, basis_ref, fixed_ref, sums_ref):
    gx, gy, gx_size, gy_size = where_am_i()
    rows = 40
    lane = lax.broadcasted_iota(jnp.int32, (rows, 128), 1)
    row = lax.broadcasted_iota(jnp.int32, (rows, 128), 0) + (gx * 8 - OWN)
    row_in = (row >= 0) & (row < gx_size * 8)
    from_right = lane < SIDE
    col = gy + jnp.where(from_right, 1, -1)
    side_in = row_in & (col >= 0) & (col < gy_size)

    def field(k):
        part = slice(k * rows, k * rows + rows)
        side = jnp.where(from_right, right_ref[part], left_ref[part])
        return jnp.concatenate(
            [jnp.where(row_in, statics_ref[part], 0.0), jnp.where(side_in, side, 0.0)], axis=1
        )

    u, v, drag, thick, surface = (field(k) for k in range(5))
    blocks = [stiff_ref[jnp.clip(gx + k, 0, gx_size - 1)] for k in range(-2, 3)]
    stiff = jnp.concatenate(blocks, axis=0)
    stiff = jnp.where(jnp.concatenate([row_in, side_in], axis=1), stiff, 0.0)
    t_sum = thick + next_col(thick)
    s_sum = stiff + next_col(stiff)
    corner_product = (1.0 / 64.0) * (t_sum + next_row(t_sum)) * (s_sum + next_row(s_sum))
    driving = (
        -thick * 0.5 * (next_row(surface) - last_row(surface)),
        -thick * 0.5 * (next_col(surface) - last_col(surface)),
    )
    kept = slice(OWN - 8, OWN + 16)

    def keep(k, b_u, b_v):
        basis_ref[2 * k] = b_u[kept]
        basis_ref[2 * k + 1] = b_v[kept]

    for k, value in enumerate((u, v, drag, corner_product, driving[0], driving[1])):
        fixed_ref[k] = value[kept]
    products = krylov_basis(u, v, drag, driving, corner_product, OWN, keep)
    write_sums(products, sums_ref)


def second_picard_kernel(
    parts_ref, basis_ref, fixed_ref, next_ref, velocity_ref, sums_ref, least_ref
):
    answer, least = small_solve(parts_ref[...])
    u, v = (fixed_ref[0], fixed_ref[1])
    for k in range(KRYLOV):
        scale = jnp.tile(answer[k], (3, 2))
        u = u + scale * basis_ref[2 * k]
        v = v + scale * basis_ref[2 * k + 1]
    velocity_ref[0] = u[8:16, :128]
    velocity_ref[1] = v[8:16, :128]
    least_ref[...] = least

    def keep(k, b_u, b_v):
        next_ref[2 * k] = b_u[8:16, :128]
        next_ref[2 * k + 1] = b_v[8:16, :128]

    driving = (fixed_ref[4], fixed_ref[5])
    products = krylov_basis(u, v, fixed_ref[2], driving, fixed_ref[3], 8, keep)
    write_sums(products, sums_ref)


def last_kernel(parts_ref, basis_ref, velocity_ref, least_ref, out_ref, worst_ref):
    answer, least = small_solve(parts_ref[...])
    u, v = (velocity_ref[0], velocity_ref[1])
    for k in range(KRYLOV):
        u = u + answer[k] * basis_ref[2 * k]
        v = v + answer[k] * basis_ref[2 * k + 1]
    out_ref[0] = u
    out_ref[1] = v
    worst_ref[0, 0] = jnp.min(jnp.minimum(least_ref[...], least))


def over_all(sums):
    count = lax.axis_size(GX)
    part = lax.all_to_all(sums, GY, 0, 0, tiled=True)
    part = jnp.broadcast_to(jnp.sum(part, axis=0, keepdims=True), (count, 128))
    return lax.all_to_all(part, GX, 0, 0, tiled=True)


def shifted(array, axis, by):
    size = lax.axis_size(axis)
    return lax.ppermute(array, axis, [(i, (i + by) % size) for i in range(size)])


def momentum(statics):
    smem = pl.BlockSpec(memory_space=pltpu.SMEM)
    vmem = pl.BlockSpec(memory_space=pltpu.VMEM)
    gx, gy = (lax.axis_size(GX), lax.axis_size(GY))
    left = shifted(statics, GY, 1)
    right = shifted(statics, GY, -1)
    lane = lax.broadcasted_iota(jnp.int32, (8, 128), 1)
    side = jnp.where(lane < SIDE, right[200:], left[200:])
    strip = jnp.concatenate([statics[200:], side], axis=1)
    strip = lax.all_to_all(jnp.broadcast_to(strip[None], (gx, 8, 256)), GX, 0, 0, tiled=True)
    basis, fixed, sums = pl.pallas_call(
        first_picard_kernel,
        out_shape=(
            kept(2 * KRYLOV, 24, 256),
            kept(6, 24, 256),
            kept(gy, 128),
        ),
        name="first_picard",
    )(*map(on_chip, (statics, left, right, strip)))
    basis, velocity, sums, least = pl.pallas_call(
        second_picard_kernel,
        out_shape=(
            kept(2 * KRYLOV, 8, 128),
            kept(2, 8, 128),
            kept(gy, 128),
            kept(8, 128),
        ),
        name="second_picard",
    )(*map(on_chip, (over_all(sums), basis, fixed)))
    return pl.pallas_call(
        last_kernel,
        out_shape=(
            jax.ShapeDtypeStruct((2, 8, 128), jnp.float32),
            jax.ShapeDtypeStruct((1, 1), jnp.float32),
        ),
        out_specs=(vmem, smem),
        name="last_picard",
    )(*map(on_chip, (over_all(sums), basis, velocity, least)))


def plain_picard(velocity, thickness, stiffness, surface, drag_term, projector):
    statics = with_halo(jnp.stack([thickness, stiffness, surface]), ((GX, 1), (GY, 2)), 1)
    thick_corner = corner_mean(statics[0])
    stiff_corner = corner_mean(statics[1])
    heights = statics[2]
    driving = jnp.stack(
        [
            -thickness * 0.5 * (heights[2:, 1:-1] - heights[:-2, 1:-1]),
            -thickness * 0.5 * (heights[1:-1, 2:] - heights[1:-1, :-2]),
        ]
    )

    def total(array):
        return one_axis_at_a_time(jnp.sum(array), GX_GY)

    def picard(_, velocity):
        rates = strains(with_halo(velocity, ((GX, 1), (GY, 2)), 1))
        weight = viscous_weight(rates, thick_corner, stiff_corner)
        residual = projector * (driving - stress_image(rates, weight, velocity, drag_term))

        def krylov(_, state):
            change, residual, direction, norm_now = state
            imaged = apply_field(direction, weight, drag_term, projector)
            step_size = norm_now / total(direction * imaged)
            change = change + step_size * direction
            residual = residual - step_size * imaged
            norm_next = total(residual * residual)
            direction = residual + norm_next / norm_now * direction
            return (change, residual, direction, norm_next)

        state = (jnp.zeros_like(velocity), residual, residual, total(residual * residual))
        return velocity + lax.fori_loop(0, KRYLOV, krylov, state)[0]

    return lax.fori_loop(0, PICARD, picard, velocity)


def column_tiles(planes):
    shape = (32, 1024)
    line = lax.broadcasted_iota(jnp.int32, shape, 0)
    spot = lax.broadcasted_iota(jnp.int32, shape, 1)
    within = line & 15
    column = jnp.where(line < 16, 0, 126) + (within & 1)
    pick = jnp.where(spot == (within >> 1) * 128 + column, 1.0, 0.0)
    tiles = lax.dot_general(
        pick,
        jnp.concatenate(planes, axis=1),
        (((1,), (1,)), ((), ())),
        precision=lax.Precision.HIGHEST,
        preferred_element_type=jnp.float32,
    )
    return (tiles[:16], tiles[16:])


def pack_kernel(
    enthalpy_ref,
    speed_ref,
    thick_ref,
    height_ref,
    friction_ref,
    ice_ref,
    grounded_ref,
    code_ref,
    low_ref,
    high_ref,
    left_ref,
    right_ref,
):
    planes = [enthalpy_ref[pl.ds(x, 128, stride=8), :] for x in range(8)]
    free = (code_ref[...] == 0) & (ice_ref[...] == 1)
    held = free | (code_ref[...] == 2)
    drag = jnp.where(grounded_ref[...] == 1, friction_ref[...], 0.0) + shelf_drag
    statics = (
        jnp.where(held, speed_ref[0], 0.0),
        jnp.where(held, speed_ref[1], 0.0),
        jnp.where(free, drag, 0.0),
        thick_ref[...],
        height_ref[...],
        speed_ref[0],
    )
    for out_ref, pair in ((low_ref, (0, 1)), (high_ref, (6, 7))):
        out_ref[0:128] = planes[pair[0]]
        out_ref[128:256] = planes[pair[1]]
        for k, value in enumerate(statics):
            out_ref[256 + 8 * k : 264 + 8 * k] = value
    first, last = column_tiles(planes)
    left_ref[0:16] = first
    left_ref[16:24] = speed_ref[1]
    right_ref[0:16] = last
    right_ref[16:24] = speed_ref[1]


def line_weights(low_face, high_face):
    p_high, m_high = (jnp.maximum(high_face, 0.0), jnp.minimum(high_face, 0.0))
    p_low, m_low = (jnp.maximum(low_face, 0.0), jnp.minimum(low_face, 0.0))
    q_high, n_high = (0.25 * p_high * (1.0 - p_high), 0.25 * m_high * (1.0 + m_high))
    q_low, n_low = (0.25 * p_low * (1.0 - p_low), 0.25 * m_low * (1.0 + m_low))
    return (
        -q_low,
        q_high + (p_low + n_low),
        (q_low + m_low) - (p_high + n_high),
        -(q_high + m_high) - n_low,
        n_high,
    )


def cell_weights(speed_ref, before_x, after_x, before_y, after_y):
    c_x, c_y = (speed_ref[0], speed_ref[1])
    row = lax.broadcasted_iota(jnp.int32, (8, 128), 0)
    lane = lax.broadcasted_iota(jnp.int32, (8, 128), 1)
    x_before = jnp.where(row == 0, pltpu.roll(before_x, 1, 0), pltpu.roll(c_x, 1, 0))
    x_after = jnp.where(row == 7, pltpu.roll(after_x, 7, 0), pltpu.roll(c_x, 7, 0))
    y_before = jnp.where(lane == 0, pltpu.roll(before_y, 1, 1), pltpu.roll(c_y, 1, 1))
    y_after = jnp.where(lane == 127, pltpu.roll(after_y, 127, 1), pltpu.roll(c_y, 127, 1))
    along_x = line_weights(0.5 * (x_before + c_x), 0.5 * (c_x + x_after))
    along_y = line_weights(0.5 * (y_before + c_y), 0.5 * (c_y + y_after))
    center = 1.0 + along_x[2] + along_y[2]
    return (center,) + along_x[:2] + along_x[3:] + along_y[:2] + along_y[3:]


def edge_products(weights, before_y, after_y):
    line = lax.broadcasted_iota(jnp.int32, (32, 128), 0)
    lane = lax.broadcasted_iota(jnp.int32, (32, 128), 1)
    back_2, back_1, ahead_1, ahead_2 = weights[5:]
    spread = []
    for x in range(8):
        b_2, b_1, a_1, a_2 = (w[x : x + 1] for w in (back_2, back_1, ahead_1, ahead_2))
        far = (line == 2 * x) & (lane == 0)
        far = far | ((line == 2 * x + 1) & (lane == 1))
        value = jnp.where(far, b_2, 0.0)
        value = jnp.where((line == 2 * x + 1) & (lane == 0), b_1, value)
        far = (line == 16 + 2 * x) & (lane == 126)
        far = far | ((line == 17 + 2 * x) & (lane == 127))
        value = jnp.where(far, a_2, value)
        value = jnp.where((line == 16 + 2 * x) & (lane == 127), a_1, value)
        spread.append(value)
    return lax.dot_general(
        jnp.concatenate([before_y, after_y], axis=0),
        jnp.concatenate(spread, axis=1),
        (((0,), (0,)), ((), ())),
        precision=lax.Precision.HIGHEST,
        preferred_element_type=jnp.float32,
    )


def substep(planes, weights, edges, inverses, first_kappa, ice, bed, surface_heat, heat_flux):
    lane = lax.broadcasted_iota(jnp.int32, (8, 128), 1)
    center, x_b2, x_b1, x_a1, x_a2, y_b2, y_b1, y_a1, y_a2 = weights
    y_b2 = jnp.where(lane < 2, 0.0, y_b2)
    y_b1 = jnp.where(lane < 1, 0.0, y_b1)
    y_a1 = jnp.where(lane > 126, 0.0, y_a1)
    y_a2 = jnp.where(lane > 125, 0.0, y_a2)
    level = lax.broadcasted_iota(jnp.int32, (128, 128), 0)
    done = []
    for x in range(0, 8, 2):
        moved, sides = ([], [])
        for r in (x, x + 1):
            at = lambda w: w[r : r + 1]
            e = planes[r + 2]
            value = at(center) * e + edges[:, r * 128 : r * 128 + 128]
            value = value + at(x_b2) * planes[r] + at(x_b1) * planes[r + 1]
            value = value + at(x_a1) * planes[r + 3] + at(x_a2) * planes[r + 4]
            value = value + at(y_b2) * pltpu.roll(e, 2, 1) + at(y_b1) * pltpu.roll(e, 1, 1)
            value = value + at(y_a1) * pltpu.roll(e, 127, 1) + at(y_a2) * pltpu.roll(e, 126, 1)
            moved.append(value)
            top = first_kappa * at(surface_heat)
            bottom = at(bed) * at(heat_flux)
            sides.append(
                value + jnp.where(level == 0, top, jnp.where(level == 127, bottom, 0.0))
            )
        solved = jnp.dot(
            inverses,
            jnp.concatenate(sides, axis=1),
            precision=lax.Precision.HIGHEST,
            preferred_element_type=jnp.float32,
        )
        for k, r in enumerate((x, x + 1)):
            mine = slice(k * 128, k * 128 + 128)
            choice = jnp.where(bed[r : r + 1] > 0.5, solved[:128, mine], solved[128:, mine])
            done.append(jnp.where(ice[r : r + 1] > 0.5, choice, moved[k]))
    return done


def inside(below_ref, above_ref, left_ref, right_ref):
    gx, gy, gx_size, gy_size = where_am_i()
    return (
        jnp.where(gx > 0, below_ref[...], 0.0),
        jnp.where(gx < gx_size - 1, above_ref[...], 0.0),
        jnp.where(gy > 0, left_ref[...], 0.0),
        jnp.where(gy < gy_size - 1, right_ref[...], 0.0),
    )


def first_substep_kernel(
    kappa_ref,
    enthalpy_ref,
    speed_ref,
    below_ref,
    above_ref,
    left_ref,
    right_ref,
    inverses_ref,
    ice_ref,
    grounded_ref,
    surface_ref,
    flux_ref,
    out_ref,
    low_ref,
    high_ref,
    first_ref,
    last_ref,
    weights_ref,
):
    below, above, left, right = inside(below_ref, above_ref, left_ref, right_ref)
    weights = cell_weights(speed_ref, below[296:], above[296:], left[16:], right[16:])
    for k in range(9):
        weights_ref[k] = weights[k]
    edges = edge_products(weights, left[:16], right[:16])
    planes = [below[:128], below[128:256]]
    planes += [enthalpy_ref[pl.ds(x, 128, stride=8), :] for x in range(8)]
    planes += [above[:128], above[128:256]]
    done = substep(
        planes,
        weights,
        edges,
        inverses_ref[...],
        kappa_ref[0],
        ice_ref[...].astype(jnp.float32),
        grounded_ref[...].astype(jnp.float32),
        surface_ref[...],
        flux_ref[...],
    )
    for x in range(8):
        out_ref[x] = done[x]
    low_ref[0:128] = done[0]
    low_ref[128:256] = done[1]
    low_ref[256:296] = above[256:296]
    high_ref[0:128] = done[6]
    high_ref[128:256] = done[7]
    high_ref[256:296] = below[256:296]
    first_ref[...], last_ref[...] = column_tiles(done)


def second_substep_kernel(
    kappa_ref,
    enthalpy_ref,
    below_ref,
    above_ref,
    left_ref,
    right_ref,
    weights_ref,
    inverses_ref,
    ice_ref,
    grounded_ref,
    surface_ref,
    flux_ref,
    near_below_ref,
    near_above_ref,
    mine_ref,
    out_ref,
    statics_ref,
    stiff_ref,
):
    below, above, left, right = inside(below_ref, above_ref, left_ref, right_ref)
    weights = tuple(weights_ref[k] for k in range(9))
    edges = edge_products(weights, left, right)
    planes = [below[:128], below[128:256]]
    planes += [enthalpy_ref[x] for x in range(8)]
    planes += [above[:128], above[128:256]]
    done = substep(
        planes,
        weights,
        edges,
        inverses_ref[...],
        kappa_ref[0],
        ice_ref[...].astype(jnp.float32),
        grounded_ref[...].astype(jnp.float32),
        surface_ref[...],
        flux_ref[...],
    )
    means = []
    for x in range(8):
        out_ref[pl.ds(x, 128, stride=8), :] = done[x]
        means.append(jnp.sum(done[x], axis=0, keepdims=True))
    blocks = (below_ref, near_below_ref, mine_ref, near_above_ref, above_ref)
    for k in range(5):
        for b, block_ref in enumerate(blocks):
            row = 40 * k + 8 * b
            statics_ref[row : row + 8] = block_ref[256 + 8 * k : 264 + 8 * k]
    stiffness = jnp.exp(jnp.concatenate(means, axis=0) * (-soften / 128.0))
    statics_ref[200:208] = stiffness
    stiff_ref[...] = stiffness


def exchanged(low, high, left, right):
    return (
        shifted(high, GX, 1),
        shifted(low, GX, -1),
        shifted(right, GY, 1),
        shifted(left, GY, -1),
    )


def shards(
    enthalpy,
    velocity_init,
    thickness,
    surface,
    friction,
    kappa,
    surface_enthalpy,
    geo_flux,
    ice_mask,
    grounded,
    boundary_code,
):
    f32 = jnp.float32
    smem = pl.BlockSpec(memory_space=pltpu.SMEM)
    vmem = pl.BlockSpec(memory_space=pltpu.VMEM)
    flat = enthalpy.reshape(1024, 128)
    packed = pl.pallas_call(
        pack_kernel,
        out_shape=(kept(304, 128),) * 2 + (kept(24, 128),) * 2,
        name="pack",
    )(flat, velocity_init, thickness, surface, friction, ice_mask, grounded, boundary_code)
    mine = packed[0]
    near = tuple(map(on_chip, exchanged(*packed)))
    inverses = on_chip(column_inverses(kappa))
    columns = (ice_mask, grounded, surface_enthalpy, geo_flux)
    current, *packed, weights = pl.pallas_call(
        first_substep_kernel,
        out_shape=(kept(8, 128, 128),)
        + (kept(296, 128),) * 2
        + (kept(16, 128),) * 2
        + (kept(9, 8, 128),),
        in_specs=[smem] + [vmem] * 11,
        out_specs=(vmem,) * 6,
        name="first_substep",
    )(kappa, flat, velocity_init, *near, inverses, *columns)
    around = tuple(map(on_chip, exchanged(*packed)))
    current, statics, stiffness = pl.pallas_call(
        second_substep_kernel,
        out_shape=(
            jax.ShapeDtypeStruct((1024, 128), f32),
            kept(208, 128),
            jax.ShapeDtypeStruct((8, 128), f32),
        ),
        in_specs=[smem] + [vmem] * 14,
        out_specs=(vmem, vmem, vmem),
        name="second_substep",
    )(
        kappa,
        on_chip(current),
        *around,
        on_chip(weights),
        inverses,
        *columns,
        near[0],
        near[1],
        on_chip(mine),
    )
    quick, worst = momentum(statics)

    def plain():
        free_cells = (boundary_code == 0) & (ice_mask == 1)
        held_cells = free_cells | (boundary_code == 2)
        projector = free_cells.astype(f32)[None]
        drag_term = jnp.where(grounded == 1, friction, 0.0) + shelf_drag
        velocity = jnp.where(held_cells[None], velocity_init, 0.0)
        return plain_picard(
            velocity, thickness, stiffness, surface, drag_term, projector
        )

    velocity = lax.cond(worst[0, 0] > PIVOT_FLOOR, lambda: quick, plain)
    return (current.reshape(enthalpy.shape), velocity)


def solution(mesh):
    torus = Mesh(mesh.devices.reshape(TORUS), ("gx_0", "gx_1", "gy_0", "gy_1"))
    placed = (
        P(None, GX, GY),
        P(None, GX, GY),
        P(GX, GY),
        P(GX, GY),
        P(GX, GY),
        P(),
        P(GX, GY),
        P(GX, GY),
        P(GX, GY),
        P(GX, GY),
        P(GX, GY),
    )
    return jax.shard_map(
        shards,
        mesh=torus,
        in_specs=placed,
        out_specs=(P(None, GX, GY), P(None, GX, GY)),
        check_vma=False,
    )
```

```python
import functools

import jax
import jax.numpy as jnp
from jax import lax
from jax.experimental import pallas as pl
from jax.experimental.pallas import tpu as pltpu
from jax.sharding import Mesh
from jax.sharding import PartitionSpec as P

PICARD = 2
KRYLOV = 6
TORUS = (4, 8, 8, 2)
GX_GY = ("gx_0", "gx_1", "gy_0", "gy_1")
GX = ("gx_0", "gx_1")
GY = ("gy_0", "gy_1")


soften = 0.3
shelf_drag = 0.2
strain_floor = 0.01

MIDDLE = 17.0
RADIUS = 17.0
PIVOT_FLOOR = 2e-4
OWN = 16
SIDE = 64


def with_halo(shard, sides, width):
    for axis, dim in sides:
        size, length = (lax.axis_size(axis), shard.shape[dim])
        up = [(i, (i + 1) % size) for i in range(size - 1)]
        down = [(j, i) for i, j in up]
        last = lax.slice_in_dim(shard, length - width, length, axis=dim)
        first = lax.slice_in_dim(shard, 0, width, axis=dim)
        before = lax.ppermute(last, axis, up)
        after = lax.ppermute(first, axis, down)
        shard = jnp.concatenate([before, shard, after], axis=dim)
    return shard


def one_axis_at_a_time(shard, axes):
    return functools.reduce(lax.psum, axes, shard)


def corner_mean(array):
    return 0.25 * (array[:-1, :-1] + array[1:, :-1] + array[:-1, 1:] + array[1:, 1:])


def diff_rows(array):
    return 0.5 * (array[1:, :-1] - array[:-1, :-1] + (array[1:, 1:] - array[:-1, 1:]))


def diff_cols(array):
    return 0.5 * (array[:-1, 1:] - array[:-1, :-1] + (array[1:, 1:] - array[1:, :-1]))


def back_rows(array):
    return 0.5 * (array[:-1, :-1] + array[:-1, 1:] - array[1:, :-1] - array[1:, 1:])


def back_cols(array):
    return 0.5 * (array[:-1, :-1] + array[1:, :-1] - array[:-1, 1:] - array[1:, 1:])


def strains(padded):
    stretch_x = diff_rows(padded[0])
    stretch_y = diff_cols(padded[1])
    shear_rate = 0.5 * (diff_cols(padded[0]) + diff_rows(padded[1]))
    return (stretch_x, stretch_y, shear_rate)


def viscous_weight(rates, thick_corner, stiff_corner):
    stretch_x, stretch_y, shear_rate = rates
    square = (
        stretch_x * stretch_x
        + stretch_y * stretch_y
        + stretch_x * stretch_y
        + shear_rate * shear_rate
    )
    return 0.5 * stiff_corner * thick_corner * jnp.power(square + strain_floor, -1.0 / 3.0)


def stress_image(rates, weight, center, drag_term):
    stretch_x, stretch_y, shear_rate = rates
    stress_x = weight * (4.0 * stretch_x + 2.0 * stretch_y)
    stress_y = weight * (4.0 * stretch_y + 2.0 * stretch_x)
    shear_stress = 2.0 * weight * shear_rate
    first = back_rows(stress_x) + back_cols(shear_stress) + drag_term * center[0]
    second = back_rows(shear_stress) + back_cols(stress_y) + drag_term * center[1]
    return jnp.stack([first, second])


def apply_field(direction, weight, drag_term, projector):
    padded = with_halo(direction, ((GX, 1), (GY, 2)), 1)
    return projector * stress_image(strains(padded), weight, direction, drag_term)


def inverse_kernel(kappa_ref, out_ref):
    levels = out_ref.shape[1]
    above = jnp.broadcast_to(kappa_ref[:, :levels], (8, levels))
    below = jnp.broadcast_to(kappa_ref[:, 1:], (8, levels))
    lane = lax.broadcasted_iota(jnp.int32, (8, levels), 1)
    rows = lax.broadcasted_iota(jnp.int32, (levels, levels), 0)
    cols = lax.broadcasted_iota(jnp.int32, (levels, levels), 1)
    floating = 1.0 + above + below
    on_bed = jnp.where(lane == levels - 1, 1.0 + above, floating)
    for k, diagonal in enumerate((on_bed, floating)):
        low = jnp.where(lane == 0, 0.0, -above)
        high = jnp.where(lane == levels - 1, 0.0, -below)
        mid = diagonal
        right = jnp.where(rows == cols, 1.0, 0.0)
        step = 1
        while step < levels:
            back = levels - step
            down = -low / pltpu.roll(mid, step, 1)
            up = -high / pltpu.roll(mid, back, 1)
            mid = mid + down * pltpu.roll(high, step, 1) + up * pltpu.roll(low, back, 1)
            low = down * pltpu.roll(low, step, 1)
            high = up * pltpu.roll(high, back, 1)
            right = (
                right
                + down[0:1] * pltpu.roll(right, step, 1)
                + up[0:1] * pltpu.roll(right, back, 1)
            )
            step *= 2
        out_ref[k * levels : (k + 1) * levels] = right * (1.0 / mid)[0:1]


def column_inverses(kappa):
    levels = kappa.shape[0] - 1
    return pl.pallas_call(
        inverse_kernel,
        out_shape=kept(2 * levels, levels),
        name="column_inverses",
    )(kappa[None])


def on_chip(array):
    return pltpu.with_memory_space_constraint(array, pltpu.VMEM)


def kept(*shape):
    return pltpu.VMEM(shape, jnp.float32)


def next_row(array):
    return pltpu.roll(array, array.shape[0] - 1, 0)


def next_col(array):
    return pltpu.roll(array, array.shape[1] - 1, 1)


def last_row(array):
    return pltpu.roll(array, 1, 0)


def last_col(array):
    return pltpu.roll(array, 1, 1)


def corner_rates(u, v):
    u_next = next_col(u)
    v_next = next_col(v)
    u_sum, u_diff = (u + u_next, u_next - u)
    v_sum, v_diff = (v + v_next, v_next - v)
    along = next_row(u_sum) - u_sum
    across = v_diff + next_row(v_diff)
    shear = u_diff + next_row(u_diff) + (next_row(v_sum) - v_sum)
    return (along, across, shear)


def stress_back(rates, half_weight):
    along, across, shear = rates
    stress_x = half_weight * (2.0 * along + across)
    stress_y = half_weight * (2.0 * across + along)
    stress_s = 0.5 * half_weight * shear
    x_before = last_col(stress_x)
    y_before = last_col(stress_y)
    s_before = last_col(stress_s)
    x_sum, s_diff = (stress_x + x_before, s_before - stress_s)
    s_sum, y_diff = (stress_s + s_before, y_before - stress_y)
    first = last_row(x_sum + s_diff) + (s_diff - x_sum)
    second = last_row(s_sum + y_diff) + (y_diff - s_sum)
    return (first, second)


def half_weights(rates, corner_product):
    along, across, shear = rates
    square = 0.25 * (along * along + across * across + along * across) + 0.0625 * shear * shear
    return corner_product * jnp.exp(jnp.log(square + strain_floor) * (-1.0 / 3.0))


def krylov_basis(u, v, drag, driving, corner_product, own_row, keep):
    free = drag > 0.0
    rates = corner_rates(u, v)
    half_weight = half_weights(rates, corner_product)
    first, second = stress_back(rates, half_weight)
    r_u = jnp.where(free, driving[0] - first - drag * u, 0.0)
    r_v = jnp.where(free, driving[1] - second - drag * v, 0.0)

    def own(array):
        return array[own_row : own_row + 8, :128]

    basis_u, basis_v = ([r_u], [r_v])
    own_basis, own_image = ([(own(r_u), own(r_v))], [])
    keep(0, r_u, r_v)
    for k in range(KRYLOV):
        b_u, b_v = (basis_u[k], basis_v[k])
        first, second = stress_back(corner_rates(b_u, b_v), half_weight)
        a_u = jnp.where(free, first, 0.0) + drag * b_u
        a_v = jnp.where(free, second, 0.0) + drag * b_v
        own_image.append((own(a_u), own(a_v)))
        if k + 1 < KRYLOV:
            scale = (1.0 if k == 0 else 2.0) / RADIUS
            n_u = scale * a_u - (scale * MIDDLE) * b_u
            n_v = scale * a_v - (scale * MIDDLE) * b_v
            if k > 0:
                n_u = n_u - basis_u[k - 1]
                n_v = n_v - basis_v[k - 1]
            basis_u.append(n_u)
            basis_v.append(n_v)
            own_basis.append((own(n_u), own(n_v)))
            keep(k + 1, n_u, n_v)
    products = []
    for i in range(KRYLOV):
        for j in range(i, KRYLOV):
            products.append(
                own_basis[i][0] * own_image[j][0] + own_basis[i][1] * own_image[j][1]
            )
    for i in range(KRYLOV):
        products.append(own_basis[i][0] * own_basis[0][0] + own_basis[i][1] * own_basis[0][1])
    return products


def write_sums(products, out_ref):
    count = out_ref.shape[0]
    lines = [jnp.sum(p, axis=0, keepdims=True) for p in products]
    lines.append(jnp.zeros((128 - len(lines), 128), jnp.float32))
    table = jnp.concatenate(lines, axis=0)
    out_ref[...] = lax.dot_general(
        jnp.ones((count, 128), jnp.float32),
        table,
        (((1,), (1,)), ((), ())),
        precision=lax.Precision.HIGHEST,
        preferred_element_type=jnp.float32,
    )


def small_solve(parts):
    sums = jnp.broadcast_to(jnp.sum(parts, axis=0, keepdims=True), (8, 128))
    at = lambda k: jnp.broadcast_to(sums[:, k : k + 1], (8, 128))
    system = {}
    k = 0
    for i in range(KRYLOV):
        for j in range(i, KRYLOV):
            system[i, j] = at(k)
            k += 1
    start = [system[i, i] for i in range(KRYLOV)]
    right = [at(k + i) for i in range(KRYLOV)]
    least = None
    for p in range(KRYLOV):
        relative = system[p, p] / start[p]
        least = relative if least is None else jnp.minimum(least, relative)
        inverse = 1.0 / system[p, p]
        for i in range(p + 1, KRYLOV):
            factor = system[p, i] * inverse
            for j in range(i, KRYLOV):
                system[i, j] = system[i, j] - factor * system[p, j]
            right[i] = right[i] - factor * right[p]
        system[p, p] = inverse
    answer = [None] * KRYLOV
    for i in reversed(range(KRYLOV)):
        value = right[i]
        for m in range(i + 1, KRYLOV):
            value = value - system[i, m] * answer[m]
        answer[i] = value * system[i, i]
    return (answer, least)


def where_am_i():
    place = []
    for axes in (GX, GY):
        major, minor = axes
        length = lax.axis_size(minor)
        place.append((lax.axis_index(major) * length + lax.axis_index(minor)))
    return (place[0], place[1], lax.axis_size(GX), lax.axis_size(GY))


def first_picard_kernel(
    mine_ref,
    left_ref,
    right_ref,
    stiff_ref,
    below_ref,
    above_ref,
    basis_ref,
    fixed_ref,
    sums_ref,
):
    row_in, side_in = inside_grid(40, -OWN)
    fields = (mine_ref, left_ref, right_ref)
    u, v, drag, thick, surface = (
        wide_field(*fields, 16 + 40 * k, row_in, side_in) for k in range(5)
    )
    stiff = jnp.concatenate([below_ref[...], stiff_ref[0:8], above_ref[...]], axis=0)
    stiff = jnp.where(jnp.concatenate([row_in, side_in], axis=1), stiff, 0.0)
    t_sum = thick + next_col(thick)
    s_sum = stiff + next_col(stiff)
    corner_product = (1.0 / 64.0) * (t_sum + next_row(t_sum)) * (s_sum + next_row(s_sum))
    driving = (
        -thick * 0.5 * (next_row(surface) - last_row(surface)),
        -thick * 0.5 * (next_col(surface) - last_col(surface)),
    )
    kept = slice(OWN - 8, OWN + 16)

    def keep(k, b_u, b_v):
        basis_ref[2 * k] = b_u[kept]
        basis_ref[2 * k + 1] = b_v[kept]

    for k, value in enumerate((u, v, drag, corner_product, driving[0], driving[1])):
        fixed_ref[k] = value[kept]
    products = krylov_basis(u, v, drag, driving, corner_product, OWN, keep)
    write_sums(products, sums_ref)


def second_picard_kernel(
    parts_ref, basis_ref, fixed_ref, next_ref, velocity_ref, sums_ref, least_ref
):
    answer, least = small_solve(parts_ref[...])
    u, v = (fixed_ref[0], fixed_ref[1])
    for k in range(KRYLOV):
        scale = jnp.tile(answer[k], (3, 2))
        u = u + scale * basis_ref[2 * k]
        v = v + scale * basis_ref[2 * k + 1]
    velocity_ref[0] = u[8:16, :128]
    velocity_ref[1] = v[8:16, :128]
    least_ref[...] = least

    def keep(k, b_u, b_v):
        next_ref[2 * k] = b_u[8:16, :128]
        next_ref[2 * k + 1] = b_v[8:16, :128]

    driving = (fixed_ref[4], fixed_ref[5])
    products = krylov_basis(u, v, fixed_ref[2], driving, fixed_ref[3], 8, keep)
    write_sums(products, sums_ref)


def last_kernel(parts_ref, basis_ref, velocity_ref, least_ref, out_ref, worst_ref):
    answer, least = small_solve(parts_ref[...])
    u, v = (velocity_ref[0], velocity_ref[1])
    for k in range(KRYLOV):
        u = u + answer[k] * basis_ref[2 * k]
        v = v + answer[k] * basis_ref[2 * k + 1]
    out_ref[0] = u
    out_ref[1] = v
    worst_ref[0, 0] = jnp.min(jnp.minimum(least_ref[...], least))


def over_all(sums):
    count = lax.axis_size(GX)
    part = lax.all_to_all(sums, GY, 0, 0, tiled=True)
    part = jnp.broadcast_to(jnp.sum(part, axis=0, keepdims=True), (count, 128))
    return lax.all_to_all(part, GX, 0, 0, tiled=True)


def shifted(array, axis, by):
    size = lax.axis_size(axis)
    return lax.ppermute(array, axis, [(i, (i + by) % size) for i in range(size)])


def momentum(mine, sides, low, stiff):
    smem = pl.BlockSpec(memory_space=pltpu.SMEM)
    vmem = pl.BlockSpec(memory_space=pltpu.VMEM)
    gy = lax.axis_size(GY)
    basis, fixed, sums = pl.pallas_call(
        first_picard_kernel,
        out_shape=(
            kept(2 * KRYLOV, 24, 256),
            kept(6, 24, 256),
            kept(gy, 128),
        ),
        name="first_picard",
    )(mine, *sides, low, *stiff)
    basis, velocity, sums, least = pl.pallas_call(
        second_picard_kernel,
        out_shape=(
            kept(2 * KRYLOV, 8, 128),
            kept(2, 8, 128),
            kept(gy, 128),
            kept(8, 128),
        ),
        name="second_picard",
    )(*map(on_chip, (over_all(sums), basis, fixed)))
    return pl.pallas_call(
        last_kernel,
        out_shape=(
            jax.ShapeDtypeStruct((2, 8, 128), jnp.float32),
            jax.ShapeDtypeStruct((1, 1), jnp.float32),
        ),
        out_specs=(vmem, smem),
        name="last_picard",
    )(*map(on_chip, (over_all(sums), basis, velocity, least)))


def plain_picard(velocity, thickness, stiffness, surface, drag_term, projector):
    statics = with_halo(jnp.stack([thickness, stiffness, surface]), ((GX, 1), (GY, 2)), 1)
    thick_corner = corner_mean(statics[0])
    stiff_corner = corner_mean(statics[1])
    heights = statics[2]
    driving = jnp.stack(
        [
            -thickness * 0.5 * (heights[2:, 1:-1] - heights[:-2, 1:-1]),
            -thickness * 0.5 * (heights[1:-1, 2:] - heights[1:-1, :-2]),
        ]
    )

    def total(array):
        return one_axis_at_a_time(jnp.sum(array), GX_GY)

    def picard(_, velocity):
        rates = strains(with_halo(velocity, ((GX, 1), (GY, 2)), 1))
        weight = viscous_weight(rates, thick_corner, stiff_corner)
        residual = projector * (driving - stress_image(rates, weight, velocity, drag_term))

        def krylov(_, state):
            change, residual, direction, norm_now = state
            imaged = apply_field(direction, weight, drag_term, projector)
            step_size = norm_now / total(direction * imaged)
            change = change + step_size * direction
            residual = residual - step_size * imaged
            norm_next = total(residual * residual)
            direction = residual + norm_next / norm_now * direction
            return (change, residual, direction, norm_next)

        state = (jnp.zeros_like(velocity), residual, residual, total(residual * residual))
        return velocity + lax.fori_loop(0, KRYLOV, krylov, state)[0]

    return lax.fori_loop(0, PICARD, picard, velocity)


def column_tiles(planes):
    shape = (32, 1024)
    line = lax.broadcasted_iota(jnp.int32, shape, 0)
    spot = lax.broadcasted_iota(jnp.int32, shape, 1)
    within = line & 15
    column = jnp.where(line < 16, 0, 126) + (within & 1)
    pick = jnp.where(spot == (within >> 1) * 128 + column, 1.0, 0.0)
    tiles = lax.dot_general(
        pick,
        jnp.concatenate(planes, axis=1),
        (((1,), (1,)), ((), ())),
        precision=lax.Precision.HIGHEST,
        preferred_element_type=jnp.float32,
    )
    return (tiles[:16], tiles[16:])


def pack_kernel(
    enthalpy_ref,
    speed_ref,
    thick_ref,
    height_ref,
    friction_ref,
    ice_ref,
    grounded_ref,
    code_ref,
    surface_ref,
    flux_ref,
    low_ref,
    high_ref,
    left_ref,
    right_ref,
):
    planes = [enthalpy_ref[pl.ds(x, 128, stride=8), :] for x in range(8)]
    free = (code_ref[...] == 0) & (ice_ref[...] == 1)
    held = free | (code_ref[...] == 2)
    drag = jnp.where(grounded_ref[...] == 1, friction_ref[...], 0.0) + shelf_drag
    statics = (
        jnp.where(held, speed_ref[0], 0.0),
        jnp.where(held, speed_ref[1], 0.0),
        jnp.where(free, drag, 0.0),
        thick_ref[...],
        height_ref[...],
        speed_ref[0],
        speed_ref[1],
        ice_ref[...].astype(jnp.float32),
        grounded_ref[...].astype(jnp.float32),
        surface_ref[...],
        flux_ref[...],
    )
    for out_ref, pair in ((low_ref, (0, 1)), (high_ref, (6, 7))):
        out_ref[0:128] = planes[pair[0]]
        out_ref[128:256] = planes[pair[1]]
        for k, value in enumerate(statics):
            out_ref[256 + 8 * k : 264 + 8 * k] = value
    first, last = column_tiles(planes)
    left_ref[0:16] = first
    left_ref[16:24] = speed_ref[1]
    right_ref[0:16] = last
    right_ref[16:24] = speed_ref[1]


def line_weights(low_face, high_face):
    p_high, m_high = (jnp.maximum(high_face, 0.0), jnp.minimum(high_face, 0.0))
    p_low, m_low = (jnp.maximum(low_face, 0.0), jnp.minimum(low_face, 0.0))
    q_high, n_high = (0.25 * p_high * (1.0 - p_high), 0.25 * m_high * (1.0 + m_high))
    q_low, n_low = (0.25 * p_low * (1.0 - p_low), 0.25 * m_low * (1.0 + m_low))
    return (
        -q_low,
        q_high + (p_low + n_low),
        (q_low + m_low) - (p_high + n_high),
        -(q_high + m_high) - n_low,
        n_high,
    )


def cell_weights(speed_ref, before_x, after_x, before_y, after_y):
    c_x, c_y = (speed_ref[0], speed_ref[1])
    row = lax.broadcasted_iota(jnp.int32, (8, 128), 0)
    lane = lax.broadcasted_iota(jnp.int32, (8, 128), 1)
    x_before = jnp.where(row == 0, pltpu.roll(before_x, 1, 0), pltpu.roll(c_x, 1, 0))
    x_after = jnp.where(row == 7, pltpu.roll(after_x, 7, 0), pltpu.roll(c_x, 7, 0))
    y_before = jnp.where(lane == 0, pltpu.roll(before_y, 1, 1), pltpu.roll(c_y, 1, 1))
    y_after = jnp.where(lane == 127, pltpu.roll(after_y, 127, 1), pltpu.roll(c_y, 127, 1))
    along_x = line_weights(0.5 * (x_before + c_x), 0.5 * (c_x + x_after))
    along_y = line_weights(0.5 * (y_before + c_y), 0.5 * (c_y + y_after))
    center = 1.0 + along_x[2] + along_y[2]
    return (center,) + along_x[:2] + along_x[3:] + along_y[:2] + along_y[3:]


def edge_products(weights, before_y, after_y):
    line = lax.broadcasted_iota(jnp.int32, (32, 128), 0)
    lane = lax.broadcasted_iota(jnp.int32, (32, 128), 1)
    back_2, back_1, ahead_1, ahead_2 = weights[5:]
    spread = []
    for x in range(8):
        b_2, b_1, a_1, a_2 = (w[x : x + 1] for w in (back_2, back_1, ahead_1, ahead_2))
        far = (line == 2 * x) & (lane == 0)
        far = far | ((line == 2 * x + 1) & (lane == 1))
        value = jnp.where(far, b_2, 0.0)
        value = jnp.where((line == 2 * x + 1) & (lane == 0), b_1, value)
        far = (line == 16 + 2 * x) & (lane == 126)
        far = far | ((line == 17 + 2 * x) & (lane == 127))
        value = jnp.where(far, a_2, value)
        value = jnp.where((line == 16 + 2 * x) & (lane == 127), a_1, value)
        spread.append(value)
    return lax.dot_general(
        jnp.concatenate([before_y, after_y], axis=0),
        jnp.concatenate(spread, axis=1),
        (((0,), (0,)), ((), ())),
        precision=lax.Precision.HIGHEST,
        preferred_element_type=jnp.float32,
    )


def substep(planes, weights, edges, inverses, first_kappa, ice, bed, surface_heat, heat_flux):
    lane = lax.broadcasted_iota(jnp.int32, (8, 128), 1)
    center, x_b2, x_b1, x_a1, x_a2, y_b2, y_b1, y_a1, y_a2 = weights
    y_b2 = jnp.where(lane < 2, 0.0, y_b2)
    y_b1 = jnp.where(lane < 1, 0.0, y_b1)
    y_a1 = jnp.where(lane > 126, 0.0, y_a1)
    y_a2 = jnp.where(lane > 125, 0.0, y_a2)
    level = lax.broadcasted_iota(jnp.int32, (128, 128), 0)
    done = []
    for x in range(0, 8, 2):
        moved, sides = ([], [])
        for r in (x, x + 1):
            at = lambda w: w[r : r + 1]
            e = planes[r + 2]
            value = at(center) * e + edges[:, r * 128 : r * 128 + 128]
            value = value + at(x_b2) * planes[r] + at(x_b1) * planes[r + 1]
            value = value + at(x_a1) * planes[r + 3] + at(x_a2) * planes[r + 4]
            value = value + at(y_b2) * pltpu.roll(e, 2, 1) + at(y_b1) * pltpu.roll(e, 1, 1)
            value = value + at(y_a1) * pltpu.roll(e, 127, 1) + at(y_a2) * pltpu.roll(e, 126, 1)
            moved.append(value)
            top = first_kappa * at(surface_heat)
            bottom = at(bed) * at(heat_flux)
            sides.append(
                value + jnp.where(level == 0, top, jnp.where(level == 127, bottom, 0.0))
            )
        solved = jnp.dot(
            inverses,
            jnp.concatenate(sides, axis=1),
            precision=lax.Precision.HIGHEST,
            preferred_element_type=jnp.float32,
        )
        for k, r in enumerate((x, x + 1)):
            mine = slice(k * 128, k * 128 + 128)
            choice = jnp.where(bed[r : r + 1] > 0.5, solved[:128, mine], solved[128:, mine])
            done.append(jnp.where(ice[r : r + 1] > 0.5, choice, moved[k]))
    return done


def inside(below_ref, above_ref, left_ref, right_ref):
    gx, gy, gx_size, gy_size = where_am_i()
    return (
        jnp.where(gx > 0, below_ref[...], 0.0),
        jnp.where(gx < gx_size - 1, above_ref[...], 0.0),
        jnp.where(gy > 0, left_ref[...], 0.0),
        jnp.where(gy < gy_size - 1, right_ref[...], 0.0),
    )


def sum_weights(inverses_ref):
    bed = jnp.sum(inverses_ref[0:128], axis=0, keepdims=True) * (1.0 / 128.0)
    shelf = jnp.sum(inverses_ref[128:256], axis=0, keepdims=True) * (1.0 / 128.0)
    return (bed, shelf, jnp.full((1, 128), 1.0 / 128.0, jnp.float32))


def level_sums(planes, inverses_ref):
    parts = sum_weights(inverses_ref)
    sums = jnp.dot(
        jnp.concatenate(parts + (jnp.zeros((5, 128), jnp.float32),), axis=0),
        jnp.concatenate(planes, axis=1),
        precision=lax.Precision.HIGHEST,
        preferred_element_type=jnp.float32,
    )
    rows = [sums[k : k + 1, x * 128 : x * 128 + 128] for k in range(3) for x in range(8)]
    return jnp.concatenate(rows, axis=0)


def gather_kernel(
    near_below_ref,
    near_above_ref,
    mine_ref,
    below_ref,
    above_ref,
    sums_ref,
    first_ref,
    last_ref,
    left_ref,
    right_ref,
):
    left_ref[0:16] = first_ref[...]
    right_ref[0:16] = last_ref[...]
    blocks = (below_ref, near_below_ref, mine_ref, near_above_ref, above_ref)
    pieces = []
    for k in range(5):
        pieces += [block_ref[256 + 8 * k : 264 + 8 * k] for block_ref in blocks]
    for k in range(3):
        part = slice(296 + 8 * k, 304 + 8 * k)
        pieces += [block_ref[part] for block_ref in (below_ref, sums_ref, above_ref)]
    for k in range(6):
        part = slice(296 + 8 * k, 304 + 8 * k)
        pieces += [block_ref[part] for block_ref in (near_below_ref, mine_ref, near_above_ref)]
    for out_ref in (left_ref, right_ref):
        for k, piece in enumerate(pieces):
            out_ref[16 + 8 * k : 24 + 8 * k] = piece


def inside_grid(rows, first_row):
    gx, gy, gx_size, gy_size = where_am_i()
    lane = lax.broadcasted_iota(jnp.int32, (rows, 128), 1)
    row = lax.broadcasted_iota(jnp.int32, (rows, 128), 0) + (gx * 8 + first_row)
    row_in = (row >= 0) & (row < gx_size * 8)
    col = gy + jnp.where(lane < SIDE, 1, -1)
    return (row_in, row_in & (col >= 0) & (col < gy_size))


def wide_field(mine_ref, left_ref, right_ref, start, row_in, side_in):
    rows = row_in.shape[0]
    part = slice(start, start + rows)
    lane = lax.broadcasted_iota(jnp.int32, (rows, 128), 1)
    side = jnp.where(lane < SIDE, right_ref[part], left_ref[part])
    return jnp.concatenate(
        [jnp.where(row_in, mine_ref[part], 0.0), jnp.where(side_in, side, 0.0)], axis=1
    )


def stiffness_kernel(
    kappa_ref, mine_ref, left_ref, right_ref, inverses_ref, low_ref, high_ref, own_ref
):
    where_in = inside_grid(24, -8)
    take = lambda start: wide_field(mine_ref, left_ref, right_ref, start, *where_in)
    sums = [take(216 + 24 * k) for k in range(3)]
    c_x, c_y, ice, bed, heat, flux = (take(288 + 24 * k) for k in range(6))
    along_x = line_weights(0.5 * (last_row(c_x) + c_x), 0.5 * (c_x + next_row(c_x)))
    along_y = line_weights(0.5 * (last_col(c_y) + c_y), 0.5 * (c_y + next_col(c_y)))
    moved = []
    for e in sums:
        value = (1.0 + along_x[2] + along_y[2]) * e
        for axis, line in ((0, along_x), (1, along_y)):
            size = e.shape[axis]
            value = value + line[0] * pltpu.roll(e, 2, axis)
            value = value + line[1] * pltpu.roll(e, 1, axis)
            value = value + line[3] * pltpu.roll(e, size - 1, axis)
            value = value + line[4] * pltpu.roll(e, size - 2, axis)
        moved.append(value)
    on_bed, on_shelf, _ = sum_weights(inverses_ref)
    top = kappa_ref[0] * heat
    grounded = moved[0] + on_bed[:, 0:1] * top + on_bed[:, 127:128] * flux
    floating = moved[1] + on_shelf[:, 0:1] * top
    mean = jnp.where(ice > 0.5, jnp.where(bed > 0.5, grounded, floating), moved[2])
    stiffness = jnp.exp(mean * -soften)
    low_ref[...] = stiffness[8:24]
    high_ref[...] = stiffness[0:16]
    own_ref[...] = stiffness[8:16, :128]


def first_substep_kernel(
    kappa_ref,
    enthalpy_ref,
    speed_ref,
    below_ref,
    above_ref,
    left_ref,
    right_ref,
    inverses_ref,
    ice_ref,
    grounded_ref,
    surface_ref,
    flux_ref,
    out_ref,
    low_ref,
    high_ref,
    first_ref,
    last_ref,
    weights_ref,
):
    below, above, left, right = inside(below_ref, above_ref, left_ref, right_ref)
    weights = cell_weights(speed_ref, below[296:304], above[296:304], left[16:], right[16:])
    for k in range(9):
        weights_ref[k] = weights[k]
    edges = edge_products(weights, left[:16], right[:16])
    planes = [below[:128], below[128:256]]
    planes += [enthalpy_ref[pl.ds(x, 128, stride=8), :] for x in range(8)]
    planes += [above[:128], above[128:256]]
    done = substep(
        planes,
        weights,
        edges,
        inverses_ref[...],
        kappa_ref[0],
        ice_ref[...].astype(jnp.float32),
        grounded_ref[...].astype(jnp.float32),
        surface_ref[...],
        flux_ref[...],
    )
    for x in range(8):
        out_ref[x] = done[x]
    low_ref[0:128] = done[0]
    low_ref[128:256] = done[1]
    low_ref[256:296] = above[256:296]
    sums = level_sums(done, inverses_ref)
    low_ref[296:320] = sums
    high_ref[296:320] = sums
    high_ref[0:128] = done[6]
    high_ref[128:256] = done[7]
    high_ref[256:296] = below[256:296]
    first_ref[...], last_ref[...] = column_tiles(done)


def second_substep_kernel(
    kappa_ref,
    enthalpy_ref,
    below_ref,
    above_ref,
    left_ref,
    right_ref,
    weights_ref,
    inverses_ref,
    ice_ref,
    grounded_ref,
    surface_ref,
    flux_ref,
    out_ref,
):
    sides = (below_ref.at[0:256], above_ref.at[0:256], left_ref.at[0:16], right_ref.at[0:16])
    below, above, left, right = inside(*sides)
    weights = tuple(weights_ref[k] for k in range(9))
    edges = edge_products(weights, left, right)
    planes = [below[:128], below[128:256]]
    planes += [enthalpy_ref[x] for x in range(8)]
    planes += [above[:128], above[128:256]]
    done = substep(
        planes,
        weights,
        edges,
        inverses_ref[...],
        kappa_ref[0],
        ice_ref[...].astype(jnp.float32),
        grounded_ref[...].astype(jnp.float32),
        surface_ref[...],
        flux_ref[...],
    )
    for x in range(8):
        out_ref[pl.ds(x, 128, stride=8), :] = done[x]


def beside(low, high, axis):
    return (on_chip(shifted(high, axis, 1)), on_chip(shifted(low, axis, -1)))


def shards(
    enthalpy,
    velocity_init,
    thickness,
    surface,
    friction,
    kappa,
    surface_enthalpy,
    geo_flux,
    ice_mask,
    grounded,
    boundary_code,
):
    f32 = jnp.float32
    smem = pl.BlockSpec(memory_space=pltpu.SMEM)
    vmem = pl.BlockSpec(memory_space=pltpu.VMEM)
    flat = enthalpy.reshape(1024, 128)
    columns = (ice_mask, grounded, surface_enthalpy, geo_flux)
    mine, high, first, last = pl.pallas_call(
        pack_kernel,
        out_shape=(kept(344, 128), kept(344, 128), kept(24, 128), kept(24, 128)),
        name="pack",
    )(
        flat,
        velocity_init,
        thickness,
        surface,
        friction,
        ice_mask,
        grounded,
        boundary_code,
        surface_enthalpy,
        geo_flux,
    )
    near = beside(mine, high, GX)
    near_sides = beside(first, last, GY)
    inverses = on_chip(column_inverses(kappa))
    current, low, high, first, last, weights = pl.pallas_call(
        first_substep_kernel,
        out_shape=(
            kept(8, 128, 128),
            kept(320, 128),
            kept(320, 128),
            kept(16, 128),
            kept(16, 128),
            kept(9, 8, 128),
        ),
        in_specs=[smem] + [vmem] * 11,
        out_specs=(vmem,) * 6,
        name="first_substep",
    )(kappa, flat, velocity_init, *near, *near_sides, inverses, *columns)
    far = beside(low, high, GX)
    mine, last = pl.pallas_call(
        gather_kernel,
        out_shape=(kept(432, 128), kept(432, 128)),
        name="gather",
    )(*near, on_chip(mine), *far, *map(on_chip, (low, first, last)))
    mine = on_chip(mine)
    sides = beside(mine, last, GY)
    low, high, stiffness = pl.pallas_call(
        stiffness_kernel,
        out_shape=(kept(16, 256), kept(16, 256), jax.ShapeDtypeStruct((8, 128), f32)),
        in_specs=[smem] + [vmem] * 4,
        out_specs=(vmem,) * 3,
        name="stiffness",
    )(kappa, mine, *sides, inverses)
    stiff = beside(low, high, GX)
    current = pl.pallas_call(
        second_substep_kernel,
        out_shape=jax.ShapeDtypeStruct((1024, 128), f32),
        in_specs=[smem] + [vmem] * 11,
        out_specs=vmem,
        name="second_substep",
    )(kappa, on_chip(current), *far, *sides, on_chip(weights), inverses, *columns)
    quick, worst = momentum(mine, sides, on_chip(low), stiff)

    def plain():
        free_cells = (boundary_code == 0) & (ice_mask == 1)
        held_cells = free_cells | (boundary_code == 2)
        projector = free_cells.astype(f32)[None]
        drag_term = jnp.where(grounded == 1, friction, 0.0) + shelf_drag
        velocity = jnp.where(held_cells[None], velocity_init, 0.0)
        return plain_picard(
            velocity, thickness, stiffness, surface, drag_term, projector
        )

    velocity = lax.cond(worst[0, 0] > PIVOT_FLOOR, lambda: quick, plain)
    return (current.reshape(enthalpy.shape), velocity)


def solution(mesh):
    torus = Mesh(mesh.devices.reshape(TORUS), ("gx_0", "gx_1", "gy_0", "gy_1"))
    placed = (
        P(None, GX, GY),
        P(None, GX, GY),
        P(GX, GY),
        P(GX, GY),
        P(GX, GY),
        P(),
        P(GX, GY),
        P(GX, GY),
        P(GX, GY),
        P(GX, GY),
        P(GX, GY),
    )
    return jax.shard_map(
        shards,
        mesh=torus,
        in_specs=placed,
        out_specs=(P(None, GX, GY), P(None, GX, GY)),
        check_vma=False,
    )
```

```python
import functools

import jax
import jax.numpy as jnp
from jax import lax
from jax.experimental import pallas as pl
from jax.experimental.pallas import tpu as pltpu
from jax.sharding import Mesh
from jax.sharding import PartitionSpec as P

PICARD = 2
KRYLOV = 6
TORUS = (4, 8, 8, 2)
GX_GY = ("gx_0", "gx_1", "gy_0", "gy_1")
GX = ("gx_0", "gx_1")
GY = ("gy_0", "gy_1")


soften = 0.3
shelf_drag = 0.2
strain_floor = 0.01

MIDDLE = 17.0
RADIUS = 17.0
PIVOT_FLOOR = 2e-4
OWN = 16
SIDE = 64


def with_halo(shard, sides, width):
    for axis, dim in sides:
        size, length = (lax.axis_size(axis), shard.shape[dim])
        up = [(i, (i + 1) % size) for i in range(size - 1)]
        down = [(j, i) for i, j in up]
        last = lax.slice_in_dim(shard, length - width, length, axis=dim)
        first = lax.slice_in_dim(shard, 0, width, axis=dim)
        before = lax.ppermute(last, axis, up)
        after = lax.ppermute(first, axis, down)
        shard = jnp.concatenate([before, shard, after], axis=dim)
    return shard


def one_axis_at_a_time(shard, axes):
    return functools.reduce(lax.psum, axes, shard)


def corner_mean(array):
    return 0.25 * (array[:-1, :-1] + array[1:, :-1] + array[:-1, 1:] + array[1:, 1:])


def diff_rows(array):
    return 0.5 * (array[1:, :-1] - array[:-1, :-1] + (array[1:, 1:] - array[:-1, 1:]))


def diff_cols(array):
    return 0.5 * (array[:-1, 1:] - array[:-1, :-1] + (array[1:, 1:] - array[1:, :-1]))


def back_rows(array):
    return 0.5 * (array[:-1, :-1] + array[:-1, 1:] - array[1:, :-1] - array[1:, 1:])


def back_cols(array):
    return 0.5 * (array[:-1, :-1] + array[1:, :-1] - array[:-1, 1:] - array[1:, 1:])


def strains(padded):
    stretch_x = diff_rows(padded[0])
    stretch_y = diff_cols(padded[1])
    shear_rate = 0.5 * (diff_cols(padded[0]) + diff_rows(padded[1]))
    return (stretch_x, stretch_y, shear_rate)


def viscous_weight(rates, thick_corner, stiff_corner):
    stretch_x, stretch_y, shear_rate = rates
    square = (
        stretch_x * stretch_x
        + stretch_y * stretch_y
        + stretch_x * stretch_y
        + shear_rate * shear_rate
    )
    return 0.5 * stiff_corner * thick_corner * jnp.power(square + strain_floor, -1.0 / 3.0)


def stress_image(rates, weight, center, drag_term):
    stretch_x, stretch_y, shear_rate = rates
    stress_x = weight * (4.0 * stretch_x + 2.0 * stretch_y)
    stress_y = weight * (4.0 * stretch_y + 2.0 * stretch_x)
    shear_stress = 2.0 * weight * shear_rate
    first = back_rows(stress_x) + back_cols(shear_stress) + drag_term * center[0]
    second = back_rows(shear_stress) + back_cols(stress_y) + drag_term * center[1]
    return jnp.stack([first, second])


def apply_field(direction, weight, drag_term, projector):
    padded = with_halo(direction, ((GX, 1), (GY, 2)), 1)
    return projector * stress_image(strains(padded), weight, direction, drag_term)


def inverse_kernel(kappa_ref, out_ref):
    levels = out_ref.shape[1]
    above = jnp.broadcast_to(kappa_ref[:, :levels], (8, levels))
    below = jnp.broadcast_to(kappa_ref[:, 1:], (8, levels))
    lane = lax.broadcasted_iota(jnp.int32, (8, levels), 1)
    rows = lax.broadcasted_iota(jnp.int32, (levels, levels), 0)
    cols = lax.broadcasted_iota(jnp.int32, (levels, levels), 1)
    floating = 1.0 + above + below
    on_bed = jnp.where(lane == levels - 1, 1.0 + above, floating)
    for k, diagonal in enumerate((on_bed, floating)):
        low = jnp.where(lane == 0, 0.0, -above)
        high = jnp.where(lane == levels - 1, 0.0, -below)
        mid = diagonal
        right = jnp.where(rows == cols, 1.0, 0.0)
        step = 1
        while step < levels:
            back = levels - step
            down = -low / pltpu.roll(mid, step, 1)
            up = -high / pltpu.roll(mid, back, 1)
            mid = mid + down * pltpu.roll(high, step, 1) + up * pltpu.roll(low, back, 1)
            low = down * pltpu.roll(low, step, 1)
            high = up * pltpu.roll(high, back, 1)
            right = (
                right
                + down[0:1] * pltpu.roll(right, step, 1)
                + up[0:1] * pltpu.roll(right, back, 1)
            )
            step *= 2
        out_ref[k * levels : (k + 1) * levels] = right * (1.0 / mid)[0:1]


def column_inverses(kappa):
    levels = kappa.shape[0] - 1
    return pl.pallas_call(
        inverse_kernel,
        out_shape=kept(2 * levels, levels),
        name="column_inverses",
    )(kappa[None])


def on_chip(array):
    return pltpu.with_memory_space_constraint(array, pltpu.VMEM)


def kept(*shape):
    return pltpu.VMEM(shape, jnp.float32)


def next_row(array):
    return pltpu.roll(array, array.shape[0] - 1, 0)


def next_col(array):
    return pltpu.roll(array, array.shape[1] - 1, 1)


def last_row(array):
    return pltpu.roll(array, 1, 0)


def last_col(array):
    return pltpu.roll(array, 1, 1)


def corner_rates(u, v):
    u_next = next_col(u)
    v_next = next_col(v)
    u_sum, u_diff = (u + u_next, u_next - u)
    v_sum, v_diff = (v + v_next, v_next - v)
    along = next_row(u_sum) - u_sum
    across = v_diff + next_row(v_diff)
    shear = u_diff + next_row(u_diff) + (next_row(v_sum) - v_sum)
    return (along, across, shear)


def stress_back(rates, half_weight):
    along, across, shear = rates
    stress_x = half_weight * (2.0 * along + across)
    stress_y = half_weight * (2.0 * across + along)
    stress_s = 0.5 * half_weight * shear
    x_before = last_col(stress_x)
    y_before = last_col(stress_y)
    s_before = last_col(stress_s)
    x_sum, s_diff = (stress_x + x_before, s_before - stress_s)
    s_sum, y_diff = (stress_s + s_before, y_before - stress_y)
    first = last_row(x_sum + s_diff) + (s_diff - x_sum)
    second = last_row(s_sum + y_diff) + (y_diff - s_sum)
    return (first, second)


def half_weights(rates, corner_product):
    along, across, shear = rates
    square = 0.25 * (along * along + across * across + along * across) + 0.0625 * shear * shear
    return corner_product * jnp.exp(jnp.log(square + strain_floor) * (-1.0 / 3.0))


def krylov_basis(u, v, drag, driving, corner_product, own_row, keep):
    free = drag > 0.0
    rates = corner_rates(u, v)
    half_weight = half_weights(rates, corner_product)
    first, second = stress_back(rates, half_weight)
    r_u = jnp.where(free, driving[0] - first - drag * u, 0.0)
    r_v = jnp.where(free, driving[1] - second - drag * v, 0.0)

    def own(array):
        return array[own_row : own_row + 8, :128]

    basis_u, basis_v = ([r_u], [r_v])
    own_basis, own_image = ([(own(r_u), own(r_v))], [])
    keep(0, r_u, r_v)
    for k in range(KRYLOV):
        b_u, b_v = (basis_u[k], basis_v[k])
        first, second = stress_back(corner_rates(b_u, b_v), half_weight)
        a_u = jnp.where(free, first, 0.0) + drag * b_u
        a_v = jnp.where(free, second, 0.0) + drag * b_v
        own_image.append((own(a_u), own(a_v)))
        if k + 1 < KRYLOV:
            scale = (1.0 if k == 0 else 2.0) / RADIUS
            n_u = scale * a_u - (scale * MIDDLE) * b_u
            n_v = scale * a_v - (scale * MIDDLE) * b_v
            if k > 0:
                n_u = n_u - basis_u[k - 1]
                n_v = n_v - basis_v[k - 1]
            basis_u.append(n_u)
            basis_v.append(n_v)
            own_basis.append((own(n_u), own(n_v)))
            keep(k + 1, n_u, n_v)
    products = []
    for i in range(KRYLOV):
        for j in range(i, KRYLOV):
            products.append(
                own_basis[i][0] * own_image[j][0] + own_basis[i][1] * own_image[j][1]
            )
    for i in range(KRYLOV):
        products.append(own_basis[i][0] * own_basis[0][0] + own_basis[i][1] * own_basis[0][1])
    return products


def write_sums(products, out_ref):
    count = out_ref.shape[0]
    lines = [jnp.sum(p, axis=0, keepdims=True) for p in products]
    lines.append(jnp.zeros((128 - len(lines), 128), jnp.float32))
    table = jnp.concatenate(lines, axis=0)
    out_ref[...] = lax.dot_general(
        jnp.ones((count, 128), jnp.float32),
        table,
        (((1,), (1,)), ((), ())),
        precision=lax.Precision.HIGHEST,
        preferred_element_type=jnp.float32,
    )


def small_solve(parts):
    sums = jnp.broadcast_to(jnp.sum(parts, axis=0, keepdims=True), (8, 128))
    at = lambda k: jnp.broadcast_to(sums[:, k : k + 1], (8, 128))
    system = {}
    k = 0
    for i in range(KRYLOV):
        for j in range(i, KRYLOV):
            system[i, j] = at(k)
            k += 1
    start = [system[i, i] for i in range(KRYLOV)]
    right = [at(k + i) for i in range(KRYLOV)]
    least = None
    for p in range(KRYLOV):
        relative = system[p, p] / start[p]
        least = relative if least is None else jnp.minimum(least, relative)
        inverse = 1.0 / system[p, p]
        for i in range(p + 1, KRYLOV):
            factor = system[p, i] * inverse
            for j in range(i, KRYLOV):
                system[i, j] = system[i, j] - factor * system[p, j]
            right[i] = right[i] - factor * right[p]
        system[p, p] = inverse
    answer = [None] * KRYLOV
    for i in reversed(range(KRYLOV)):
        value = right[i]
        for m in range(i + 1, KRYLOV):
            value = value - system[i, m] * answer[m]
        answer[i] = value * system[i, i]
    return (answer, least)


def where_am_i():
    place = []
    for axes in (GX, GY):
        major, minor = axes
        length = lax.axis_size(minor)
        place.append((lax.axis_index(major) * length + lax.axis_index(minor)))
    return (place[0], place[1], lax.axis_size(GX), lax.axis_size(GY))


def first_picard_kernel(
    kappa_ref,
    mine_ref,
    left_ref,
    right_ref,
    inverses_ref,
    basis_ref,
    fixed_ref,
    sums_ref,
    own_ref,
):
    where_in = inside_grid(40, -OWN)
    take = lambda k: wide_field(k, mine_ref, left_ref, right_ref, *where_in)
    u, v, drag, thick, surface = (take(k) for k in range(5))
    transport = [take(k) for k in range(5, 11)]
    sums = [take(k) for k in range(11, 14)]
    stiff = stiffness_of(sums, *transport, kappa_ref[0], inverses_ref)
    stiff = jnp.where(jnp.concatenate(where_in, axis=1), stiff, 0.0)
    own_ref[...] = stiff[OWN : OWN + 8, :128]
    t_sum = thick + next_col(thick)
    s_sum = stiff + next_col(stiff)
    corner_product = (1.0 / 64.0) * (t_sum + next_row(t_sum)) * (s_sum + next_row(s_sum))
    driving = (
        -thick * 0.5 * (next_row(surface) - last_row(surface)),
        -thick * 0.5 * (next_col(surface) - last_col(surface)),
    )
    kept = slice(OWN - 8, OWN + 16)

    def keep(k, b_u, b_v):
        basis_ref[2 * k] = b_u[kept]
        basis_ref[2 * k + 1] = b_v[kept]

    for k, value in enumerate((u, v, drag, corner_product, driving[0], driving[1])):
        fixed_ref[k] = value[kept]
    products = krylov_basis(u, v, drag, driving, corner_product, OWN, keep)
    write_sums(products, sums_ref)


def second_picard_kernel(
    parts_ref, basis_ref, fixed_ref, next_ref, velocity_ref, sums_ref, least_ref
):
    answer, least = small_solve(parts_ref[...])
    u, v = (fixed_ref[0], fixed_ref[1])
    for k in range(KRYLOV):
        scale = jnp.tile(answer[k], (3, 2))
        u = u + scale * basis_ref[2 * k]
        v = v + scale * basis_ref[2 * k + 1]
    velocity_ref[0] = u[8:16, :128]
    velocity_ref[1] = v[8:16, :128]
    least_ref[...] = least

    def keep(k, b_u, b_v):
        next_ref[2 * k] = b_u[8:16, :128]
        next_ref[2 * k + 1] = b_v[8:16, :128]

    driving = (fixed_ref[4], fixed_ref[5])
    products = krylov_basis(u, v, fixed_ref[2], driving, fixed_ref[3], 8, keep)
    write_sums(products, sums_ref)


def last_kernel(parts_ref, basis_ref, velocity_ref, least_ref, out_ref, worst_ref):
    answer, least = small_solve(parts_ref[...])
    u, v = (velocity_ref[0], velocity_ref[1])
    for k in range(KRYLOV):
        u = u + answer[k] * basis_ref[2 * k]
        v = v + answer[k] * basis_ref[2 * k + 1]
    out_ref[0] = u
    out_ref[1] = v
    worst_ref[0, 0] = jnp.min(jnp.minimum(least_ref[...], least))


def over_all(sums):
    count = lax.axis_size(GX)
    part = lax.all_to_all(sums, GY, 0, 0, tiled=True)
    part = jnp.broadcast_to(jnp.sum(part, axis=0, keepdims=True), (count, 128))
    return lax.all_to_all(part, GX, 0, 0, tiled=True)


def shifted(array, axis, by):
    size = lax.axis_size(axis)
    return lax.ppermute(array, axis, [(i, (i + by) % size) for i in range(size)])


def momentum(kappa, mine, sides, inverses):
    smem = pl.BlockSpec(memory_space=pltpu.SMEM)
    vmem = pl.BlockSpec(memory_space=pltpu.VMEM)
    gy = lax.axis_size(GY)
    basis, fixed, sums, stiffness = pl.pallas_call(
        first_picard_kernel,
        out_shape=(
            kept(2 * KRYLOV, 24, 256),
            kept(6, 24, 256),
            kept(gy, 128),
            jax.ShapeDtypeStruct((8, 128), jnp.float32),
        ),
        in_specs=[smem] + [vmem] * 4,
        out_specs=(vmem,) * 4,
        name="first_picard",
    )(kappa, mine, *sides, inverses)
    basis, velocity, sums, least = pl.pallas_call(
        second_picard_kernel,
        out_shape=(
            kept(2 * KRYLOV, 8, 128),
            kept(2, 8, 128),
            kept(gy, 128),
            kept(8, 128),
        ),
        name="second_picard",
    )(*map(on_chip, (over_all(sums), basis, fixed)))
    velocity, worst = pl.pallas_call(
        last_kernel,
        out_shape=(
            jax.ShapeDtypeStruct((2, 8, 128), jnp.float32),
            jax.ShapeDtypeStruct((1, 1), jnp.float32),
        ),
        out_specs=(vmem, smem),
        name="last_picard",
    )(*map(on_chip, (over_all(sums), basis, velocity, least)))
    return (velocity, worst, stiffness)


def plain_picard(velocity, thickness, stiffness, surface, drag_term, projector):
    statics = with_halo(jnp.stack([thickness, stiffness, surface]), ((GX, 1), (GY, 2)), 1)
    thick_corner = corner_mean(statics[0])
    stiff_corner = corner_mean(statics[1])
    heights = statics[2]
    driving = jnp.stack(
        [
            -thickness * 0.5 * (heights[2:, 1:-1] - heights[:-2, 1:-1]),
            -thickness * 0.5 * (heights[1:-1, 2:] - heights[1:-1, :-2]),
        ]
    )

    def total(array):
        return one_axis_at_a_time(jnp.sum(array), GX_GY)

    def picard(_, velocity):
        rates = strains(with_halo(velocity, ((GX, 1), (GY, 2)), 1))
        weight = viscous_weight(rates, thick_corner, stiff_corner)
        residual = projector * (driving - stress_image(rates, weight, velocity, drag_term))

        def krylov(_, state):
            change, residual, direction, norm_now = state
            imaged = apply_field(direction, weight, drag_term, projector)
            step_size = norm_now / total(direction * imaged)
            change = change + step_size * direction
            residual = residual - step_size * imaged
            norm_next = total(residual * residual)
            direction = residual + norm_next / norm_now * direction
            return (change, residual, direction, norm_next)

        state = (jnp.zeros_like(velocity), residual, residual, total(residual * residual))
        return velocity + lax.fori_loop(0, KRYLOV, krylov, state)[0]

    return lax.fori_loop(0, PICARD, picard, velocity)


def column_tiles(planes):
    shape = (32, 1024)
    line = lax.broadcasted_iota(jnp.int32, shape, 0)
    spot = lax.broadcasted_iota(jnp.int32, shape, 1)
    within = line & 15
    column = jnp.where(line < 16, 0, 126) + (within & 1)
    pick = jnp.where(spot == (within >> 1) * 128 + column, 1.0, 0.0)
    tiles = lax.dot_general(
        pick,
        jnp.concatenate(planes, axis=1),
        (((1,), (1,)), ((), ())),
        precision=lax.Precision.HIGHEST,
        preferred_element_type=jnp.float32,
    )
    return (tiles[:16], tiles[16:])


def pack_kernel(
    enthalpy_ref,
    speed_ref,
    thick_ref,
    height_ref,
    friction_ref,
    ice_ref,
    grounded_ref,
    code_ref,
    surface_ref,
    flux_ref,
    low_ref,
    high_ref,
    left_ref,
    right_ref,
    planes_ref,
):
    planes = [enthalpy_ref[pl.ds(x, 128, stride=8), :] for x in range(8)]
    for x in range(8):
        planes_ref[x] = planes[x]
    free = (code_ref[...] == 0) & (ice_ref[...] == 1)
    held = free | (code_ref[...] == 2)
    drag = jnp.where(grounded_ref[...] == 1, friction_ref[...], 0.0) + shelf_drag
    statics = (
        jnp.where(held, speed_ref[0], 0.0),
        jnp.where(held, speed_ref[1], 0.0),
        jnp.where(free, drag, 0.0),
        thick_ref[...],
        height_ref[...],
        speed_ref[0],
        speed_ref[1],
        ice_ref[...].astype(jnp.float32),
        grounded_ref[...].astype(jnp.float32),
        surface_ref[...],
        flux_ref[...],
    )
    for out_ref, pair in ((low_ref, (0, 1)), (high_ref, (6, 7))):
        out_ref[0:128] = planes[pair[0]]
        out_ref[128:256] = planes[pair[1]]
        for k, value in enumerate(statics):
            out_ref[256 + 8 * k : 264 + 8 * k] = value
    first, last = column_tiles(planes)
    left_ref[0:16] = first
    left_ref[16:24] = speed_ref[1]
    right_ref[0:16] = last
    right_ref[16:24] = speed_ref[1]


def line_weights(low_face, high_face):
    p_high, m_high = (jnp.maximum(high_face, 0.0), jnp.minimum(high_face, 0.0))
    p_low, m_low = (jnp.maximum(low_face, 0.0), jnp.minimum(low_face, 0.0))
    q_high, n_high = (0.25 * p_high * (1.0 - p_high), 0.25 * m_high * (1.0 + m_high))
    q_low, n_low = (0.25 * p_low * (1.0 - p_low), 0.25 * m_low * (1.0 + m_low))
    return (
        -q_low,
        q_high + (p_low + n_low),
        (q_low + m_low) - (p_high + n_high),
        -(q_high + m_high) - n_low,
        n_high,
    )


def cell_weights(speed_ref, before_x, after_x, before_y, after_y):
    c_x, c_y = (speed_ref[0], speed_ref[1])
    row = lax.broadcasted_iota(jnp.int32, (8, 128), 0)
    lane = lax.broadcasted_iota(jnp.int32, (8, 128), 1)
    x_before = jnp.where(row == 0, pltpu.roll(before_x, 1, 0), pltpu.roll(c_x, 1, 0))
    x_after = jnp.where(row == 7, pltpu.roll(after_x, 7, 0), pltpu.roll(c_x, 7, 0))
    y_before = jnp.where(lane == 0, pltpu.roll(before_y, 1, 1), pltpu.roll(c_y, 1, 1))
    y_after = jnp.where(lane == 127, pltpu.roll(after_y, 127, 1), pltpu.roll(c_y, 127, 1))
    along_x = line_weights(0.5 * (x_before + c_x), 0.5 * (c_x + x_after))
    along_y = line_weights(0.5 * (y_before + c_y), 0.5 * (c_y + y_after))
    center = 1.0 + along_x[2] + along_y[2]
    return (center,) + along_x[:2] + along_x[3:] + along_y[:2] + along_y[3:]


def edge_products(weights, before_y, after_y):
    line = lax.broadcasted_iota(jnp.int32, (32, 128), 0)
    lane = lax.broadcasted_iota(jnp.int32, (32, 128), 1)
    back_2, back_1, ahead_1, ahead_2 = weights[5:]
    spread = []
    for x in range(8):
        b_2, b_1, a_1, a_2 = (w[x : x + 1] for w in (back_2, back_1, ahead_1, ahead_2))
        far = (line == 2 * x) & (lane == 0)
        far = far | ((line == 2 * x + 1) & (lane == 1))
        value = jnp.where(far, b_2, 0.0)
        value = jnp.where((line == 2 * x + 1) & (lane == 0), b_1, value)
        far = (line == 16 + 2 * x) & (lane == 126)
        far = far | ((line == 17 + 2 * x) & (lane == 127))
        value = jnp.where(far, a_2, value)
        value = jnp.where((line == 16 + 2 * x) & (lane == 127), a_1, value)
        spread.append(value)
    return lax.dot_general(
        jnp.concatenate([before_y, after_y], axis=0),
        jnp.concatenate(spread, axis=1),
        (((0,), (0,)), ((), ())),
        precision=lax.Precision.HIGHEST,
        preferred_element_type=jnp.float32,
    )


def substep(planes, weights, edges, inverses, first_kappa, ice, bed, surface_heat, heat_flux):
    lane = lax.broadcasted_iota(jnp.int32, (8, 128), 1)
    center, x_b2, x_b1, x_a1, x_a2, y_b2, y_b1, y_a1, y_a2 = weights
    y_b2 = jnp.where(lane < 2, 0.0, y_b2)
    y_b1 = jnp.where(lane < 1, 0.0, y_b1)
    y_a1 = jnp.where(lane > 126, 0.0, y_a1)
    y_a2 = jnp.where(lane > 125, 0.0, y_a2)
    level = lax.broadcasted_iota(jnp.int32, (128, 128), 0)
    done = []
    for x in range(0, 8, 2):
        moved, sides = ([], [])
        for r in (x, x + 1):
            at = lambda w: w[r : r + 1]
            e = planes[r + 2]
            value = at(center) * e + edges[:, r * 128 : r * 128 + 128]
            value = value + at(x_b2) * planes[r] + at(x_b1) * planes[r + 1]
            value = value + at(x_a1) * planes[r + 3] + at(x_a2) * planes[r + 4]
            value = value + at(y_b2) * pltpu.roll(e, 2, 1) + at(y_b1) * pltpu.roll(e, 1, 1)
            value = value + at(y_a1) * pltpu.roll(e, 127, 1) + at(y_a2) * pltpu.roll(e, 126, 1)
            moved.append(value)
            top = first_kappa * at(surface_heat)
            bottom = at(bed) * at(heat_flux)
            sides.append(
                value + jnp.where(level == 0, top, jnp.where(level == 127, bottom, 0.0))
            )
        solved = jnp.dot(
            inverses,
            jnp.concatenate(sides, axis=1),
            precision=lax.Precision.HIGHEST,
            preferred_element_type=jnp.float32,
        )
        for k, r in enumerate((x, x + 1)):
            mine = slice(k * 128, k * 128 + 128)
            choice = jnp.where(bed[r : r + 1] > 0.5, solved[:128, mine], solved[128:, mine])
            done.append(jnp.where(ice[r : r + 1] > 0.5, choice, moved[k]))
    return done


def inside(below_ref, above_ref, left_ref, right_ref):
    gx, gy, gx_size, gy_size = where_am_i()
    return (
        jnp.where(gx > 0, below_ref[...], 0.0),
        jnp.where(gx < gx_size - 1, above_ref[...], 0.0),
        jnp.where(gy > 0, left_ref[...], 0.0),
        jnp.where(gy < gy_size - 1, right_ref[...], 0.0),
    )


def sum_weights(inverses_ref):
    bed = jnp.sum(inverses_ref[0:128], axis=0, keepdims=True) * (1.0 / 128.0)
    shelf = jnp.sum(inverses_ref[128:256], axis=0, keepdims=True) * (1.0 / 128.0)
    return (bed, shelf, jnp.full((1, 128), 1.0 / 128.0, jnp.float32))


def level_sums(planes, inverses_ref):
    parts = sum_weights(inverses_ref)
    sums = jnp.dot(
        jnp.concatenate(parts + (jnp.zeros((5, 128), jnp.float32),), axis=0),
        jnp.concatenate(planes, axis=1),
        precision=lax.Precision.HIGHEST,
        preferred_element_type=jnp.float32,
    )
    rows = [sums[k : k + 1, x * 128 : x * 128 + 128] for k in range(3) for x in range(8)]
    return jnp.concatenate(rows, axis=0)


def gather_kernel(
    near_below_ref,
    near_above_ref,
    own_ref,
    below_ref,
    above_ref,
    far_below_ref,
    far_above_ref,
    sums_ref,
    first_ref,
    last_ref,
    mine_ref,
    left_ref,
    right_ref,
):
    left_ref[0:16] = first_ref[...]
    right_ref[0:16] = last_ref[...]
    blocks = (below_ref, near_below_ref, own_ref, near_above_ref, above_ref)
    fields = []
    for k in range(11):
        part = slice(256 + 8 * k, 264 + 8 * k)
        fields.append(jnp.concatenate([block_ref[part] for block_ref in blocks], axis=0))
    for k in range(3):
        end, middle = (slice(8 * k, 8 * k + 8), slice(344 + 8 * k, 352 + 8 * k))
        pieces = [far_below_ref[end], below_ref[middle], sums_ref[end]]
        pieces += [above_ref[middle], far_above_ref[end]]
        fields.append(jnp.concatenate(pieces, axis=0))
    quarter = lax.broadcasted_iota(jnp.int32, (40, 128), 1) // 32
    for group in range(4):
        low, high = (None, None)
        for k, field in enumerate(fields[4 * group : 4 * group + 4]):
            mine_ref[(4 * group + k) * 40 : (4 * group + k) * 40 + 40] = field
            if k == 0:
                low, high = (field, field)
            else:
                low = jnp.where(quarter == k, pltpu.roll(field, 32 * k, 1), low)
                high = jnp.where(quarter == 3 - k, pltpu.roll(field, 128 - 32 * k, 1), high)
        part = slice(16 + 40 * group, 56 + 40 * group)
        left_ref[part] = low
        right_ref[part] = high


def inside_grid(rows, first_row):
    gx, gy, gx_size, gy_size = where_am_i()
    lane = lax.broadcasted_iota(jnp.int32, (rows, 128), 1)
    row = lax.broadcasted_iota(jnp.int32, (rows, 128), 0) + (gx * 8 + first_row)
    row_in = (row >= 0) & (row < gx_size * 8)
    col = gy + jnp.where(lane < SIDE, 1, -1)
    return (row_in, row_in & (col >= 0) & (col < gy_size))


def wide_field(k, mine_ref, left_ref, right_ref, row_in, side_in):
    part = slice(16 + 40 * (k // 4), 56 + 40 * (k // 4))
    turn = 32 * (k % 4)
    right, left = (right_ref[part], left_ref[part])
    if turn:
        right, left = (pltpu.roll(right, 128 - turn, 1), pltpu.roll(left, turn, 1))
    lane = lax.broadcasted_iota(jnp.int32, (40, 128), 1)
    side = jnp.where(lane < SIDE, right, left)
    own = mine_ref[40 * k : 40 * k + 40]
    return jnp.concatenate(
        [jnp.where(row_in, own, 0.0), jnp.where(side_in, side, 0.0)], axis=1
    )


def stiffness_of(sums, c_x, c_y, ice, bed, heat, flux, first_kappa, inverses_ref):
    along_x = line_weights(0.5 * (last_row(c_x) + c_x), 0.5 * (c_x + next_row(c_x)))
    along_y = line_weights(0.5 * (last_col(c_y) + c_y), 0.5 * (c_y + next_col(c_y)))
    moved = []
    for e in sums:
        value = (1.0 + along_x[2] + along_y[2]) * e
        for axis, line in ((0, along_x), (1, along_y)):
            size = e.shape[axis]
            value = value + line[0] * pltpu.roll(e, 2, axis)
            value = value + line[1] * pltpu.roll(e, 1, axis)
            value = value + line[3] * pltpu.roll(e, size - 1, axis)
            value = value + line[4] * pltpu.roll(e, size - 2, axis)
        moved.append(value)
    on_bed, on_shelf, _ = sum_weights(inverses_ref)
    top = first_kappa * heat
    grounded = moved[0] + on_bed[:, 0:1] * top + on_bed[:, 127:128] * flux
    floating = moved[1] + on_shelf[:, 0:1] * top
    mean = jnp.where(ice > 0.5, jnp.where(bed > 0.5, grounded, floating), moved[2])
    return jnp.exp(mean * -soften)


def first_substep_kernel(
    kappa_ref,
    enthalpy_ref,
    speed_ref,
    below_ref,
    above_ref,
    left_ref,
    right_ref,
    inverses_ref,
    ice_ref,
    grounded_ref,
    surface_ref,
    flux_ref,
    out_ref,
    low_ref,
    high_ref,
    first_ref,
    last_ref,
    weights_ref,
    sums_ref,
):
    below, above, left, right = inside(below_ref, above_ref, left_ref, right_ref)
    weights = cell_weights(speed_ref, below[296:304], above[296:304], left[16:], right[16:])
    for k in range(9):
        weights_ref[k] = weights[k]
    edges = edge_products(weights, left[:16], right[:16])
    planes = [below[:128], below[128:256]]
    planes += [enthalpy_ref[x] for x in range(8)]
    planes += [above[:128], above[128:256]]
    done = substep(
        planes,
        weights,
        edges,
        inverses_ref[...],
        kappa_ref[0],
        ice_ref[...].astype(jnp.float32),
        grounded_ref[...].astype(jnp.float32),
        surface_ref[...],
        flux_ref[...],
    )
    for x in range(8):
        out_ref[x] = done[x]
    low_ref[0:128] = done[0]
    low_ref[128:256] = done[1]
    low_ref[256:344] = above[256:344]
    sums = level_sums(done, inverses_ref)
    low_ref[344:368] = sums
    high_ref[344:368] = sums
    sums_ref[...] = sums
    high_ref[0:128] = done[6]
    high_ref[128:256] = done[7]
    high_ref[256:344] = below[256:344]
    first_ref[...], last_ref[...] = column_tiles(done)


def second_substep_kernel(
    kappa_ref,
    enthalpy_ref,
    below_ref,
    above_ref,
    left_ref,
    right_ref,
    weights_ref,
    inverses_ref,
    ice_ref,
    grounded_ref,
    surface_ref,
    flux_ref,
    out_ref,
):
    sides = (below_ref.at[0:256], above_ref.at[0:256], left_ref.at[0:16], right_ref.at[0:16])
    below, above, left, right = inside(*sides)
    weights = tuple(weights_ref[k] for k in range(9))
    edges = edge_products(weights, left, right)
    planes = [below[:128], below[128:256]]
    planes += [enthalpy_ref[x] for x in range(8)]
    planes += [above[:128], above[128:256]]
    done = substep(
        planes,
        weights,
        edges,
        inverses_ref[...],
        kappa_ref[0],
        ice_ref[...].astype(jnp.float32),
        grounded_ref[...].astype(jnp.float32),
        surface_ref[...],
        flux_ref[...],
    )
    for x in range(8):
        out_ref[pl.ds(x, 128, stride=8), :] = done[x]


def beside(low, high, axis):
    return (on_chip(shifted(high, axis, 1)), on_chip(shifted(low, axis, -1)))


def shards(
    enthalpy,
    velocity_init,
    thickness,
    surface,
    friction,
    kappa,
    surface_enthalpy,
    geo_flux,
    ice_mask,
    grounded,
    boundary_code,
):
    f32 = jnp.float32
    smem = pl.BlockSpec(memory_space=pltpu.SMEM)
    vmem = pl.BlockSpec(memory_space=pltpu.VMEM)
    flat = enthalpy.reshape(1024, 128)
    columns = (ice_mask, grounded, surface_enthalpy, geo_flux)
    own, high, first, last, planes = pl.pallas_call(
        pack_kernel,
        out_shape=(
            kept(344, 128),
            kept(344, 128),
            kept(24, 128),
            kept(24, 128),
            kept(8, 128, 128),
        ),
        name="pack",
    )(
        flat,
        velocity_init,
        thickness,
        surface,
        friction,
        ice_mask,
        grounded,
        boundary_code,
        surface_enthalpy,
        geo_flux,
    )
    near = beside(own, high, GX)
    near_sides = beside(first, last, GY)
    inverses = on_chip(column_inverses(kappa))
    current, low, high, first, last, weights, sums = pl.pallas_call(
        first_substep_kernel,
        out_shape=(
            kept(8, 128, 128),
            kept(368, 128),
            kept(368, 128),
            kept(16, 128),
            kept(16, 128),
            kept(9, 8, 128),
            kept(24, 128),
        ),
        in_specs=[smem] + [vmem] * 11,
        out_specs=(vmem,) * 7,
        name="first_substep",
    )(kappa, on_chip(planes), velocity_init, *near, *near_sides, inverses, *columns)
    around = beside(low, high, GX)
    far = (on_chip(shifted(sums, GX, 2)), on_chip(shifted(sums, GX, -2)))
    mine, first, last = pl.pallas_call(
        gather_kernel,
        out_shape=(kept(560, 128), kept(176, 128), kept(176, 128)),
        name="gather",
    )(*near, on_chip(own), *around, *far, *map(on_chip, (sums, first, last)))
    sides = beside(first, last, GY)
    current = pl.pallas_call(
        second_substep_kernel,
        out_shape=jax.ShapeDtypeStruct((1024, 128), f32),
        in_specs=[smem] + [vmem] * 11,
        out_specs=vmem,
        name="second_substep",
    )(kappa, on_chip(current), *around, *sides, on_chip(weights), inverses, *columns)
    quick, worst, stiffness = momentum(kappa, on_chip(mine), sides, inverses)

    def plain():
        free_cells = (boundary_code == 0) & (ice_mask == 1)
        held_cells = free_cells | (boundary_code == 2)
        projector = free_cells.astype(f32)[None]
        drag_term = jnp.where(grounded == 1, friction, 0.0) + shelf_drag
        velocity = jnp.where(held_cells[None], velocity_init, 0.0)
        return plain_picard(
            velocity, thickness, stiffness, surface, drag_term, projector
        )

    velocity = lax.cond(worst[0, 0] > PIVOT_FLOOR, lambda: quick, plain)
    return (current.reshape(enthalpy.shape), velocity)


def solution(mesh):
    torus = Mesh(mesh.devices.reshape(TORUS), ("gx_0", "gx_1", "gy_0", "gy_1"))
    placed = (
        P(None, GX, GY),
        P(None, GX, GY),
        P(GX, GY),
        P(GX, GY),
        P(GX, GY),
        P(),
        P(GX, GY),
        P(GX, GY),
        P(GX, GY),
        P(GX, GY),
        P(GX, GY),
    )
    return jax.shard_map(
        shards,
        mesh=torus,
        in_specs=placed,
        out_specs=(P(None, GX, GY), P(None, GX, GY)),
        check_vma=False,
    )
```

```python
import functools

import jax
import jax.numpy as jnp
from jax import lax
from jax.experimental import pallas as pl
from jax.experimental.pallas import tpu as pltpu
from jax.sharding import Mesh
from jax.sharding import PartitionSpec as P

PICARD = 2
KRYLOV = 6
TORUS = (4, 8, 8, 2)
GX_GY = ("gx_0", "gx_1", "gy_0", "gy_1")
GX = ("gx_0", "gx_1")
GY = ("gy_0", "gy_1")


soften = 0.3
shelf_drag = 0.2
strain_floor = 0.01

MIDDLE = 17.0
RADIUS = 17.0
PIVOT_FLOOR = 2e-4
OWN = 16
SIDE = 64


def with_halo(shard, sides, width):
    for axis, dim in sides:
        size, length = (lax.axis_size(axis), shard.shape[dim])
        up = [(i, (i + 1) % size) for i in range(size - 1)]
        down = [(j, i) for i, j in up]
        last = lax.slice_in_dim(shard, length - width, length, axis=dim)
        first = lax.slice_in_dim(shard, 0, width, axis=dim)
        before = lax.ppermute(last, axis, up)
        after = lax.ppermute(first, axis, down)
        shard = jnp.concatenate([before, shard, after], axis=dim)
    return shard


def one_axis_at_a_time(shard, axes):
    return functools.reduce(lax.psum, axes, shard)


def corner_mean(array):
    return 0.25 * (array[:-1, :-1] + array[1:, :-1] + array[:-1, 1:] + array[1:, 1:])


def diff_rows(array):
    return 0.5 * (array[1:, :-1] - array[:-1, :-1] + (array[1:, 1:] - array[:-1, 1:]))


def diff_cols(array):
    return 0.5 * (array[:-1, 1:] - array[:-1, :-1] + (array[1:, 1:] - array[1:, :-1]))


def back_rows(array):
    return 0.5 * (array[:-1, :-1] + array[:-1, 1:] - array[1:, :-1] - array[1:, 1:])


def back_cols(array):
    return 0.5 * (array[:-1, :-1] + array[1:, :-1] - array[:-1, 1:] - array[1:, 1:])


def strains(padded):
    stretch_x = diff_rows(padded[0])
    stretch_y = diff_cols(padded[1])
    shear_rate = 0.5 * (diff_cols(padded[0]) + diff_rows(padded[1]))
    return (stretch_x, stretch_y, shear_rate)


def viscous_weight(rates, thick_corner, stiff_corner):
    stretch_x, stretch_y, shear_rate = rates
    square = (
        stretch_x * stretch_x
        + stretch_y * stretch_y
        + stretch_x * stretch_y
        + shear_rate * shear_rate
    )
    return 0.5 * stiff_corner * thick_corner * jnp.power(square + strain_floor, -1.0 / 3.0)


def stress_image(rates, weight, center, drag_term):
    stretch_x, stretch_y, shear_rate = rates
    stress_x = weight * (4.0 * stretch_x + 2.0 * stretch_y)
    stress_y = weight * (4.0 * stretch_y + 2.0 * stretch_x)
    shear_stress = 2.0 * weight * shear_rate
    first = back_rows(stress_x) + back_cols(shear_stress) + drag_term * center[0]
    second = back_rows(shear_stress) + back_cols(stress_y) + drag_term * center[1]
    return jnp.stack([first, second])


def apply_field(direction, weight, drag_term, projector):
    padded = with_halo(direction, ((GX, 1), (GY, 2)), 1)
    return projector * stress_image(strains(padded), weight, direction, drag_term)


def inverse_kernel(kappa_ref, out_ref):
    levels = out_ref.shape[1]
    above = jnp.broadcast_to(kappa_ref[:, :levels], (8, levels))
    below = jnp.broadcast_to(kappa_ref[:, 1:], (8, levels))
    lane = lax.broadcasted_iota(jnp.int32, (8, levels), 1)
    rows = lax.broadcasted_iota(jnp.int32, (levels, levels), 0)
    cols = lax.broadcasted_iota(jnp.int32, (levels, levels), 1)
    floating = 1.0 + above + below
    on_bed = jnp.where(lane == levels - 1, 1.0 + above, floating)
    for k, diagonal in enumerate((on_bed, floating)):
        low = jnp.where(lane == 0, 0.0, -above)
        high = jnp.where(lane == levels - 1, 0.0, -below)
        mid = diagonal
        right = jnp.where(rows == cols, 1.0, 0.0)
        step = 1
        while step < levels:
            back = levels - step
            down = -low / pltpu.roll(mid, step, 1)
            up = -high / pltpu.roll(mid, back, 1)
            mid = mid + down * pltpu.roll(high, step, 1) + up * pltpu.roll(low, back, 1)
            low = down * pltpu.roll(low, step, 1)
            high = up * pltpu.roll(high, back, 1)
            right = (
                right
                + down[0:1] * pltpu.roll(right, step, 1)
                + up[0:1] * pltpu.roll(right, back, 1)
            )
            step *= 2
        out_ref[k * levels : (k + 1) * levels] = right * (1.0 / mid)[0:1]


def column_inverses(kappa):
    levels = kappa.shape[0] - 1
    return pl.pallas_call(
        inverse_kernel,
        out_shape=kept(2 * levels, levels),
        name="column_inverses",
    )(kappa[None])


def on_chip(array):
    return pltpu.with_memory_space_constraint(array, pltpu.VMEM)


def kept(*shape):
    return pltpu.VMEM(shape, jnp.float32)


def next_row(array):
    return pltpu.roll(array, array.shape[0] - 1, 0)


def next_col(array):
    return pltpu.roll(array, array.shape[1] - 1, 1)


def last_row(array):
    return pltpu.roll(array, 1, 0)


def last_col(array):
    return pltpu.roll(array, 1, 1)


def corner_rates(u, v):
    u_next = next_col(u)
    v_next = next_col(v)
    u_sum, u_diff = (u + u_next, u_next - u)
    v_sum, v_diff = (v + v_next, v_next - v)
    along = next_row(u_sum) - u_sum
    across = v_diff + next_row(v_diff)
    shear = u_diff + next_row(u_diff) + (next_row(v_sum) - v_sum)
    return (along, across, shear)


def stress_back(rates, half_weight):
    along, across, shear = rates
    stress_x = half_weight * (2.0 * along + across)
    stress_y = half_weight * (2.0 * across + along)
    stress_s = 0.5 * half_weight * shear
    x_before = last_col(stress_x)
    y_before = last_col(stress_y)
    s_before = last_col(stress_s)
    x_sum, s_diff = (stress_x + x_before, s_before - stress_s)
    s_sum, y_diff = (stress_s + s_before, y_before - stress_y)
    first = last_row(x_sum + s_diff) + (s_diff - x_sum)
    second = last_row(s_sum + y_diff) + (y_diff - s_sum)
    return (first, second)


def half_weights(rates, corner_product):
    along, across, shear = rates
    square = 0.25 * (along * along + across * across + along * across) + 0.0625 * shear * shear
    return corner_product * jnp.exp(jnp.log(square + strain_floor) * (-1.0 / 3.0))


def krylov_basis(u, v, drag, driving, corner_product, own_row, keep):
    free = drag > 0.0
    rates = corner_rates(u, v)
    half_weight = half_weights(rates, corner_product)
    first, second = stress_back(rates, half_weight)
    r_u = jnp.where(free, driving[0] - first - drag * u, 0.0)
    r_v = jnp.where(free, driving[1] - second - drag * v, 0.0)

    def own(array):
        return array[own_row : own_row + 8, :128]

    basis_u, basis_v = ([r_u], [r_v])
    own_basis, own_image = ([(own(r_u), own(r_v))], [])
    keep(0, r_u, r_v)
    for k in range(KRYLOV):
        b_u, b_v = (basis_u[k], basis_v[k])
        first, second = stress_back(corner_rates(b_u, b_v), half_weight)
        a_u = jnp.where(free, first, 0.0) + drag * b_u
        a_v = jnp.where(free, second, 0.0) + drag * b_v
        own_image.append((own(a_u), own(a_v)))
        if k + 1 < KRYLOV:
            scale = (1.0 if k == 0 else 2.0) / RADIUS
            n_u = scale * a_u - (scale * MIDDLE) * b_u
            n_v = scale * a_v - (scale * MIDDLE) * b_v
            if k > 0:
                n_u = n_u - basis_u[k - 1]
                n_v = n_v - basis_v[k - 1]
            basis_u.append(n_u)
            basis_v.append(n_v)
            own_basis.append((own(n_u), own(n_v)))
            keep(k + 1, n_u, n_v)
    products = []
    for i in range(KRYLOV):
        for j in range(i, KRYLOV):
            products.append(
                own_basis[i][0] * own_image[j][0] + own_basis[i][1] * own_image[j][1]
            )
    for i in range(KRYLOV):
        products.append(own_basis[i][0] * own_basis[0][0] + own_basis[i][1] * own_basis[0][1])
    return products


def write_sums(products, out_ref):
    count = out_ref.shape[0]
    lines = [jnp.sum(p, axis=0, keepdims=True) for p in products]
    lines.append(jnp.zeros((128 - len(lines), 128), jnp.float32))
    table = jnp.concatenate(lines, axis=0)
    out_ref[...] = lax.dot_general(
        jnp.ones((count, 128), jnp.float32),
        table,
        (((1,), (1,)), ((), ())),
        precision=lax.Precision.HIGHEST,
        preferred_element_type=jnp.float32,
    )


def small_solve(parts):
    sums = jnp.broadcast_to(jnp.sum(parts, axis=0, keepdims=True), (8, 128))
    at = lambda k: jnp.broadcast_to(sums[:, k : k + 1], (8, 128))
    system = {}
    k = 0
    for i in range(KRYLOV):
        for j in range(i, KRYLOV):
            system[i, j] = at(k)
            k += 1
    start = [system[i, i] for i in range(KRYLOV)]
    right = [at(k + i) for i in range(KRYLOV)]
    least = None
    for p in range(KRYLOV):
        relative = system[p, p] / start[p]
        least = relative if least is None else jnp.minimum(least, relative)
        inverse = 1.0 / system[p, p]
        for i in range(p + 1, KRYLOV):
            factor = system[p, i] * inverse
            for j in range(i, KRYLOV):
                system[i, j] = system[i, j] - factor * system[p, j]
            right[i] = right[i] - factor * right[p]
        system[p, p] = inverse
    answer = [None] * KRYLOV
    for i in reversed(range(KRYLOV)):
        value = right[i]
        for m in range(i + 1, KRYLOV):
            value = value - system[i, m] * answer[m]
        answer[i] = value * system[i, i]
    return (answer, least)


def where_am_i():
    place = []
    for axes in (GX, GY):
        major, minor = axes
        length = lax.axis_size(minor)
        place.append((lax.axis_index(major) * length + lax.axis_index(minor)))
    return (place[0], place[1], lax.axis_size(GX), lax.axis_size(GY))


def first_picard_kernel(
    kappa_ref,
    mine_ref,
    left_ref,
    right_ref,
    inverses_ref,
    basis_ref,
    fixed_ref,
    sums_ref,
    own_ref,
):
    where_in = inside_grid(40, -OWN)
    take = lambda k: wide_field(k, mine_ref, left_ref, right_ref, *where_in)
    u, v, drag, thick, surface = (take(k) for k in range(5))
    transport = [take(k) for k in range(5, 11)]
    sums = [take(k) for k in range(11, 14)]
    stiff = stiffness_of(sums, *transport, kappa_ref[0], inverses_ref)
    stiff = jnp.where(jnp.concatenate(where_in, axis=1), stiff, 0.0)
    own_ref[...] = stiff[OWN : OWN + 8, :128]
    t_sum = thick + next_col(thick)
    s_sum = stiff + next_col(stiff)
    corner_product = (1.0 / 64.0) * (t_sum + next_row(t_sum)) * (s_sum + next_row(s_sum))
    driving = (
        -thick * 0.5 * (next_row(surface) - last_row(surface)),
        -thick * 0.5 * (next_col(surface) - last_col(surface)),
    )
    kept = slice(OWN - 8, OWN + 16)

    def keep(k, b_u, b_v):
        basis_ref[2 * k] = b_u[kept]
        basis_ref[2 * k + 1] = b_v[kept]

    for k, value in enumerate((u, v, drag, corner_product, driving[0], driving[1])):
        fixed_ref[k] = value[kept]
    products = krylov_basis(u, v, drag, driving, corner_product, OWN, keep)
    write_sums(products, sums_ref)


def second_picard_kernel(
    parts_ref, basis_ref, fixed_ref, next_ref, velocity_ref, sums_ref, least_ref
):
    answer, least = small_solve(parts_ref[...])
    u, v = (fixed_ref[0], fixed_ref[1])
    for k in range(KRYLOV):
        scale = jnp.tile(answer[k], (3, 2))
        u = u + scale * basis_ref[2 * k]
        v = v + scale * basis_ref[2 * k + 1]
    velocity_ref[0] = u[8:16, :128]
    velocity_ref[1] = v[8:16, :128]
    least_ref[...] = least

    def keep(k, b_u, b_v):
        next_ref[2 * k] = b_u[8:16, :128]
        next_ref[2 * k + 1] = b_v[8:16, :128]

    driving = (fixed_ref[4], fixed_ref[5])
    products = krylov_basis(u, v, fixed_ref[2], driving, fixed_ref[3], 8, keep)
    write_sums(products, sums_ref)


def last_kernel(parts_ref, basis_ref, velocity_ref, least_ref, out_ref, worst_ref):
    answer, least = small_solve(parts_ref[...])
    u, v = (velocity_ref[0], velocity_ref[1])
    for k in range(KRYLOV):
        u = u + answer[k] * basis_ref[2 * k]
        v = v + answer[k] * basis_ref[2 * k + 1]
    out_ref[0] = u
    out_ref[1] = v
    worst_ref[0, 0] = jnp.min(jnp.minimum(least_ref[...], least))


def over_all(sums):
    count = lax.axis_size(GX)
    part = lax.all_to_all(sums, GY, 0, 0, tiled=True)
    part = jnp.broadcast_to(jnp.sum(part, axis=0, keepdims=True), (count, 128))
    return lax.all_to_all(part, GX, 0, 0, tiled=True)


def shifted(array, axis, by):
    size = lax.axis_size(axis)
    return lax.ppermute(array, axis, [(i, (i + by) % size) for i in range(size)])


def momentum(kappa, mine, sides, inverses):
    smem = pl.BlockSpec(memory_space=pltpu.SMEM)
    vmem = pl.BlockSpec(memory_space=pltpu.VMEM)
    gy = lax.axis_size(GY)
    basis, fixed, sums, stiffness = pl.pallas_call(
        first_picard_kernel,
        out_shape=(
            kept(2 * KRYLOV, 24, 256),
            kept(6, 24, 256),
            kept(gy, 128),
            jax.ShapeDtypeStruct((8, 128), jnp.float32),
        ),
        in_specs=[smem] + [vmem] * 4,
        out_specs=(vmem,) * 4,
        name="first_picard",
    )(kappa, mine, *sides, inverses)
    basis, velocity, sums, least = pl.pallas_call(
        second_picard_kernel,
        out_shape=(
            kept(2 * KRYLOV, 8, 128),
            kept(2, 8, 128),
            kept(gy, 128),
            kept(8, 128),
        ),
        name="second_picard",
    )(*map(on_chip, (over_all(sums), basis, fixed)))
    velocity, worst = pl.pallas_call(
        last_kernel,
        out_shape=(
            jax.ShapeDtypeStruct((2, 8, 128), jnp.float32),
            jax.ShapeDtypeStruct((1, 1), jnp.float32),
        ),
        out_specs=(vmem, smem),
        name="last_picard",
    )(*map(on_chip, (over_all(sums), basis, velocity, least)))
    return (velocity, worst, stiffness)


def plain_picard(velocity, thickness, stiffness, surface, drag_term, projector):
    statics = with_halo(jnp.stack([thickness, stiffness, surface]), ((GX, 1), (GY, 2)), 1)
    thick_corner = corner_mean(statics[0])
    stiff_corner = corner_mean(statics[1])
    heights = statics[2]
    driving = jnp.stack(
        [
            -thickness * 0.5 * (heights[2:, 1:-1] - heights[:-2, 1:-1]),
            -thickness * 0.5 * (heights[1:-1, 2:] - heights[1:-1, :-2]),
        ]
    )

    def total(array):
        return one_axis_at_a_time(jnp.sum(array), GX_GY)

    def picard(_, velocity):
        rates = strains(with_halo(velocity, ((GX, 1), (GY, 2)), 1))
        weight = viscous_weight(rates, thick_corner, stiff_corner)
        residual = projector * (driving - stress_image(rates, weight, velocity, drag_term))

        def krylov(_, state):
            change, residual, direction, norm_now = state
            imaged = apply_field(direction, weight, drag_term, projector)
            step_size = norm_now / total(direction * imaged)
            change = change + step_size * direction
            residual = residual - step_size * imaged
            norm_next = total(residual * residual)
            direction = residual + norm_next / norm_now * direction
            return (change, residual, direction, norm_next)

        state = (jnp.zeros_like(velocity), residual, residual, total(residual * residual))
        return velocity + lax.fori_loop(0, KRYLOV, krylov, state)[0]

    return lax.fori_loop(0, PICARD, picard, velocity)


def column_tiles(planes):
    shape = (32, 1024)
    line = lax.broadcasted_iota(jnp.int32, shape, 0)
    spot = lax.broadcasted_iota(jnp.int32, shape, 1)
    within = line & 15
    column = jnp.where(line < 16, 0, 126) + (within & 1)
    pick = jnp.where(spot == (within >> 1) * 128 + column, 1.0, 0.0)
    tiles = lax.dot_general(
        pick,
        jnp.concatenate(planes, axis=1),
        (((1,), (1,)), ((), ())),
        precision=lax.Precision.HIGHEST,
        preferred_element_type=jnp.float32,
    )
    return (tiles[:16], tiles[16:])


def pack_kernel(
    enthalpy_ref,
    speed_ref,
    thick_ref,
    height_ref,
    friction_ref,
    ice_ref,
    grounded_ref,
    code_ref,
    surface_ref,
    flux_ref,
    low_ref,
    high_ref,
    left_ref,
    right_ref,
    planes_ref,
):
    planes = [enthalpy_ref[pl.ds(x, 128, stride=8), :] for x in range(8)]
    for x in range(8):
        planes_ref[x] = planes[x]
    free = (code_ref[...] == 0) & (ice_ref[...] == 1)
    held = free | (code_ref[...] == 2)
    drag = jnp.where(grounded_ref[...] == 1, friction_ref[...], 0.0) + shelf_drag
    statics = (
        jnp.where(held, speed_ref[0], 0.0),
        jnp.where(held, speed_ref[1], 0.0),
        jnp.where(free, drag, 0.0),
        thick_ref[...],
        height_ref[...],
        speed_ref[0],
        speed_ref[1],
        ice_ref[...].astype(jnp.float32),
        grounded_ref[...].astype(jnp.float32),
        surface_ref[...],
        flux_ref[...],
    )
    for out_ref, pair in ((low_ref, (0, 1)), (high_ref, (6, 7))):
        out_ref[0:128] = planes[pair[0]]
        out_ref[128:256] = planes[pair[1]]
        for k, value in enumerate(statics):
            out_ref[256 + 8 * k : 264 + 8 * k] = value
    first, last = column_tiles(planes)
    left_ref[0:16] = first
    left_ref[16:24] = speed_ref[1]
    right_ref[0:16] = last
    right_ref[16:24] = speed_ref[1]


def line_weights(low_face, high_face):
    p_high, m_high = (jnp.maximum(high_face, 0.0), jnp.minimum(high_face, 0.0))
    p_low, m_low = (jnp.maximum(low_face, 0.0), jnp.minimum(low_face, 0.0))
    q_high, n_high = (0.25 * p_high * (1.0 - p_high), 0.25 * m_high * (1.0 + m_high))
    q_low, n_low = (0.25 * p_low * (1.0 - p_low), 0.25 * m_low * (1.0 + m_low))
    return (
        -q_low,
        q_high + (p_low + n_low),
        (q_low + m_low) - (p_high + n_high),
        -(q_high + m_high) - n_low,
        n_high,
    )


def cell_weights(speed_ref, before_x, after_x, before_y, after_y):
    c_x, c_y = (speed_ref[0], speed_ref[1])
    row = lax.broadcasted_iota(jnp.int32, (8, 128), 0)
    lane = lax.broadcasted_iota(jnp.int32, (8, 128), 1)
    x_before = jnp.where(row == 0, pltpu.roll(before_x, 1, 0), pltpu.roll(c_x, 1, 0))
    x_after = jnp.where(row == 7, pltpu.roll(after_x, 7, 0), pltpu.roll(c_x, 7, 0))
    y_before = jnp.where(lane == 0, pltpu.roll(before_y, 1, 1), pltpu.roll(c_y, 1, 1))
    y_after = jnp.where(lane == 127, pltpu.roll(after_y, 127, 1), pltpu.roll(c_y, 127, 1))
    along_x = line_weights(0.5 * (x_before + c_x), 0.5 * (c_x + x_after))
    along_y = line_weights(0.5 * (y_before + c_y), 0.5 * (c_y + y_after))
    center = 1.0 + along_x[2] + along_y[2]
    return (center,) + along_x[:2] + along_x[3:] + along_y[:2] + along_y[3:]


def edge_products(weights, before_y, after_y):
    line = lax.broadcasted_iota(jnp.int32, (8, 128), 0)
    lane = lax.broadcasted_iota(jnp.int32, (8, 128), 1)
    back_2, back_1, ahead_1, ahead_2 = weights[5:]
    before = (
        jnp.where(lane == 0, back_2, 0.0),
        jnp.where(lane == 0, back_1, jnp.where(lane == 1, back_2, 0.0)),
    )
    after = (
        jnp.where(lane == 127, ahead_1, jnp.where(lane == 126, ahead_2, 0.0)),
        jnp.where(lane == 127, ahead_2, 0.0),
    )
    nothing = jnp.zeros((8, 128), jnp.float32)
    spread = []
    for x in range(8):
        at = 2 * (x % 4)
        tiles = []
        for near, far in (before, after):
            tile = jnp.where(line == at, near[x : x + 1], 0.0)
            tile = jnp.where(line == at + 1, far[x : x + 1], tile)
            tiles += [tile, nothing] if x < 4 else [nothing, tile]
        spread.append(jnp.concatenate(tiles, axis=0))
    return lax.dot_general(
        jnp.concatenate([before_y, after_y], axis=0),
        jnp.concatenate(spread, axis=1),
        (((0,), (0,)), ((), ())),
        precision=lax.Precision.HIGHEST,
        preferred_element_type=jnp.float32,
    )


def substep(planes, weights, edges, inverses, first_kappa, ice, bed, surface_heat, heat_flux):
    lane = lax.broadcasted_iota(jnp.int32, (8, 128), 1)
    center, x_b2, x_b1, x_a1, x_a2, y_b2, y_b1, y_a1, y_a2 = weights
    y_b2 = jnp.where(lane < 2, 0.0, y_b2)
    y_b1 = jnp.where(lane < 1, 0.0, y_b1)
    y_a1 = jnp.where(lane > 126, 0.0, y_a1)
    y_a2 = jnp.where(lane > 125, 0.0, y_a2)
    level = lax.broadcasted_iota(jnp.int32, (128, 128), 0)
    done = []
    for x in range(0, 8, 2):
        moved, sides = ([], [])
        for r in (x, x + 1):
            at = lambda w: w[r : r + 1]
            e = planes[r + 2]
            value = at(center) * e + edges[:, r * 128 : r * 128 + 128]
            value = value + at(x_b2) * planes[r] + at(x_b1) * planes[r + 1]
            value = value + at(x_a1) * planes[r + 3] + at(x_a2) * planes[r + 4]
            value = value + at(y_b2) * pltpu.roll(e, 2, 1) + at(y_b1) * pltpu.roll(e, 1, 1)
            value = value + at(y_a1) * pltpu.roll(e, 127, 1) + at(y_a2) * pltpu.roll(e, 126, 1)
            moved.append(value)
            top = first_kappa * at(surface_heat)
            bottom = at(bed) * at(heat_flux)
            sides.append(
                value + jnp.where(level == 0, top, jnp.where(level == 127, bottom, 0.0))
            )
        solved = jnp.dot(
            inverses,
            jnp.concatenate(sides, axis=1),
            precision=lax.Precision.HIGHEST,
            preferred_element_type=jnp.float32,
        )
        for k, r in enumerate((x, x + 1)):
            mine = slice(k * 128, k * 128 + 128)
            choice = jnp.where(bed[r : r + 1] > 0.5, solved[:128, mine], solved[128:, mine])
            done.append(jnp.where(ice[r : r + 1] > 0.5, choice, moved[k]))
    return done


def inside(below_ref, above_ref, left_ref, right_ref):
    gx, gy, gx_size, gy_size = where_am_i()
    return (
        jnp.where(gx > 0, below_ref[...], 0.0),
        jnp.where(gx < gx_size - 1, above_ref[...], 0.0),
        jnp.where(gy > 0, left_ref[...], 0.0),
        jnp.where(gy < gy_size - 1, right_ref[...], 0.0),
    )


def sum_weights(inverses_ref):
    bed = jnp.sum(inverses_ref[0:128], axis=0, keepdims=True) * (1.0 / 128.0)
    shelf = jnp.sum(inverses_ref[128:256], axis=0, keepdims=True) * (1.0 / 128.0)
    return (bed, shelf, jnp.full((1, 128), 1.0 / 128.0, jnp.float32))


def level_sums(planes, inverses_ref):
    parts = sum_weights(inverses_ref)
    sums = jnp.dot(
        jnp.concatenate(parts + (jnp.zeros((5, 128), jnp.float32),), axis=0),
        jnp.concatenate(planes, axis=1),
        precision=lax.Precision.HIGHEST,
        preferred_element_type=jnp.float32,
    )
    rows = [sums[k : k + 1, x * 128 : x * 128 + 128] for k in range(3) for x in range(8)]
    return jnp.concatenate(rows, axis=0)


def tiles_kernel(planes_ref, first_ref, last_ref):
    first_ref[...], last_ref[...] = column_tiles([planes_ref[x] for x in range(8)])


def gather_kernel(
    near_below_ref,
    near_above_ref,
    own_ref,
    below_ref,
    above_ref,
    far_below_ref,
    far_above_ref,
    sums_ref,
    first_ref,
    last_ref,
    mine_ref,
    left_ref,
    right_ref,
):
    left_ref[0:16] = first_ref[...]
    right_ref[0:16] = last_ref[...]
    blocks = (below_ref, near_below_ref, own_ref, near_above_ref, above_ref)
    fields = []
    for k in range(11):
        part = slice(256 + 8 * k, 264 + 8 * k)
        fields.append(jnp.concatenate([block_ref[part] for block_ref in blocks], axis=0))
    for k in range(3):
        end, middle = (slice(8 * k, 8 * k + 8), slice(344 + 8 * k, 352 + 8 * k))
        pieces = [far_below_ref[end], below_ref[middle], sums_ref[end]]
        pieces += [above_ref[middle], far_above_ref[end]]
        fields.append(jnp.concatenate(pieces, axis=0))
    eighth = lax.broadcasted_iota(jnp.int32, (40, 128), 1) // 16
    for group in range(2):
        low, high = (None, None)
        for k, field in enumerate(fields[8 * group : 8 * group + 8]):
            mine_ref[(8 * group + k) * 40 : (8 * group + k) * 40 + 40] = field
            if k == 0:
                low, high = (field, field)
            else:
                low = jnp.where(eighth == k, pltpu.roll(field, 16 * k, 1), low)
                high = jnp.where(eighth == 7 - k, pltpu.roll(field, 128 - 16 * k, 1), high)
        part = slice(16 + 40 * group, 56 + 40 * group)
        left_ref[part] = low
        right_ref[part] = high


def inside_grid(rows, first_row):
    gx, gy, gx_size, gy_size = where_am_i()
    lane = lax.broadcasted_iota(jnp.int32, (rows, 128), 1)
    row = lax.broadcasted_iota(jnp.int32, (rows, 128), 0) + (gx * 8 + first_row)
    row_in = (row >= 0) & (row < gx_size * 8)
    col = gy + jnp.where(lane < SIDE, 1, -1)
    return (row_in, row_in & (col >= 0) & (col < gy_size))


def wide_field(k, mine_ref, left_ref, right_ref, row_in, side_in):
    part = slice(16 + 40 * (k // 8), 56 + 40 * (k // 8))
    turn = 16 * (k % 8)
    right, left = (right_ref[part], left_ref[part])
    if turn:
        right, left = (pltpu.roll(right, 128 - turn, 1), pltpu.roll(left, turn, 1))
    lane = lax.broadcasted_iota(jnp.int32, (40, 128), 1)
    side = jnp.where(lane < SIDE, right, left)
    own = mine_ref[40 * k : 40 * k + 40]
    return jnp.concatenate(
        [jnp.where(row_in, own, 0.0), jnp.where(side_in, side, 0.0)], axis=1
    )


def stiffness_of(sums, c_x, c_y, ice, bed, heat, flux, first_kappa, inverses_ref):
    along_x = line_weights(0.5 * (last_row(c_x) + c_x), 0.5 * (c_x + next_row(c_x)))
    along_y = line_weights(0.5 * (last_col(c_y) + c_y), 0.5 * (c_y + next_col(c_y)))
    moved = []
    for e in sums:
        value = (1.0 + along_x[2] + along_y[2]) * e
        for axis, line in ((0, along_x), (1, along_y)):
            size = e.shape[axis]
            value = value + line[0] * pltpu.roll(e, 2, axis)
            value = value + line[1] * pltpu.roll(e, 1, axis)
            value = value + line[3] * pltpu.roll(e, size - 1, axis)
            value = value + line[4] * pltpu.roll(e, size - 2, axis)
        moved.append(value)
    on_bed, on_shelf, _ = sum_weights(inverses_ref)
    top = first_kappa * heat
    grounded = moved[0] + on_bed[:, 0:1] * top + on_bed[:, 127:128] * flux
    floating = moved[1] + on_shelf[:, 0:1] * top
    mean = jnp.where(ice > 0.5, jnp.where(bed > 0.5, grounded, floating), moved[2])
    return jnp.exp(mean * -soften)


def first_substep_kernel(
    kappa_ref,
    enthalpy_ref,
    speed_ref,
    below_ref,
    above_ref,
    left_ref,
    right_ref,
    inverses_ref,
    ice_ref,
    grounded_ref,
    surface_ref,
    flux_ref,
    out_ref,
    low_ref,
    high_ref,
    weights_ref,
    sums_ref,
):
    below, above, left, right = inside(below_ref, above_ref, left_ref, right_ref)
    weights = cell_weights(speed_ref, below[296:304], above[296:304], left[16:], right[16:])
    for k in range(9):
        weights_ref[k] = weights[k]
    edges = edge_products(weights, left[:16], right[:16])
    planes = [below[:128], below[128:256]]
    planes += [enthalpy_ref[x] for x in range(8)]
    planes += [above[:128], above[128:256]]
    done = substep(
        planes,
        weights,
        edges,
        inverses_ref[...],
        kappa_ref[0],
        ice_ref[...].astype(jnp.float32),
        grounded_ref[...].astype(jnp.float32),
        surface_ref[...],
        flux_ref[...],
    )
    for x in range(8):
        out_ref[x] = done[x]
    low_ref[0:128] = done[0]
    low_ref[128:256] = done[1]
    low_ref[256:344] = above[256:344]
    sums = level_sums(done, inverses_ref)
    low_ref[344:368] = sums
    high_ref[344:368] = sums
    sums_ref[...] = sums
    high_ref[0:128] = done[6]
    high_ref[128:256] = done[7]
    high_ref[256:344] = below[256:344]


def second_substep_kernel(
    kappa_ref,
    enthalpy_ref,
    below_ref,
    above_ref,
    left_ref,
    right_ref,
    weights_ref,
    inverses_ref,
    ice_ref,
    grounded_ref,
    surface_ref,
    flux_ref,
    out_ref,
):
    sides = (below_ref.at[0:256], above_ref.at[0:256], left_ref.at[0:16], right_ref.at[0:16])
    below, above, left, right = inside(*sides)
    weights = tuple(weights_ref[k] for k in range(9))
    edges = edge_products(weights, left, right)
    planes = [below[:128], below[128:256]]
    planes += [enthalpy_ref[x] for x in range(8)]
    planes += [above[:128], above[128:256]]
    done = substep(
        planes,
        weights,
        edges,
        inverses_ref[...],
        kappa_ref[0],
        ice_ref[...].astype(jnp.float32),
        grounded_ref[...].astype(jnp.float32),
        surface_ref[...],
        flux_ref[...],
    )
    for x in range(8):
        out_ref[pl.ds(x, 128, stride=8), :] = done[x]


def beside(low, high, axis):
    return (on_chip(shifted(high, axis, 1)), on_chip(shifted(low, axis, -1)))


def shards(
    enthalpy,
    velocity_init,
    thickness,
    surface,
    friction,
    kappa,
    surface_enthalpy,
    geo_flux,
    ice_mask,
    grounded,
    boundary_code,
):
    f32 = jnp.float32
    smem = pl.BlockSpec(memory_space=pltpu.SMEM)
    vmem = pl.BlockSpec(memory_space=pltpu.VMEM)
    flat = enthalpy.reshape(1024, 128)
    columns = (ice_mask, grounded, surface_enthalpy, geo_flux)
    own, high, first, last, planes = pl.pallas_call(
        pack_kernel,
        out_shape=(
            kept(344, 128),
            kept(344, 128),
            kept(24, 128),
            kept(24, 128),
            kept(8, 128, 128),
        ),
        name="pack",
    )(
        flat,
        velocity_init,
        thickness,
        surface,
        friction,
        ice_mask,
        grounded,
        boundary_code,
        surface_enthalpy,
        geo_flux,
    )
    near = beside(own, high, GX)
    near_sides = beside(first, last, GY)
    inverses = on_chip(column_inverses(kappa))
    current, low, high, weights, sums = pl.pallas_call(
        first_substep_kernel,
        out_shape=(
            kept(8, 128, 128),
            kept(368, 128),
            kept(368, 128),
            kept(9, 8, 128),
            kept(24, 128),
        ),
        in_specs=[smem] + [vmem] * 11,
        out_specs=(vmem,) * 5,
        name="first_substep",
    )(kappa, on_chip(planes), velocity_init, *near, *near_sides, inverses, *columns)
    around = beside(low, high, GX)
    far = (on_chip(shifted(sums, GX, 2)), on_chip(shifted(sums, GX, -2)))
    current = on_chip(current)
    first, last = pl.pallas_call(
        tiles_kernel,
        out_shape=(kept(16, 128), kept(16, 128)),
        name="tiles",
    )(current)
    mine, first, last = pl.pallas_call(
        gather_kernel,
        out_shape=(kept(560, 128), kept(96, 128), kept(96, 128)),
        name="gather",
    )(*near, on_chip(own), *around, *far, *map(on_chip, (sums, first, last)))
    sides = beside(first, last, GY)
    current = pl.pallas_call(
        second_substep_kernel,
        out_shape=jax.ShapeDtypeStruct((1024, 128), f32),
        in_specs=[smem] + [vmem] * 11,
        out_specs=vmem,
        name="second_substep",
    )(kappa, current, *around, *sides, on_chip(weights), inverses, *columns)
    quick, worst, stiffness = momentum(kappa, on_chip(mine), sides, inverses)

    def plain():
        free_cells = (boundary_code == 0) & (ice_mask == 1)
        held_cells = free_cells | (boundary_code == 2)
        projector = free_cells.astype(f32)[None]
        drag_term = jnp.where(grounded == 1, friction, 0.0) + shelf_drag
        velocity = jnp.where(held_cells[None], velocity_init, 0.0)
        return plain_picard(
            velocity, thickness, stiffness, surface, drag_term, projector
        )

    velocity = lax.cond(worst[0, 0] > PIVOT_FLOOR, lambda: quick, plain)
    return (current.reshape(enthalpy.shape), velocity)


def solution(mesh):
    torus = Mesh(mesh.devices.reshape(TORUS), ("gx_0", "gx_1", "gy_0", "gy_1"))
    placed = (
        P(None, GX, GY),
        P(None, GX, GY),
        P(GX, GY),
        P(GX, GY),
        P(GX, GY),
        P(),
        P(GX, GY),
        P(GX, GY),
        P(GX, GY),
        P(GX, GY),
        P(GX, GY),
    )
    return jax.shard_map(
        shards,
        mesh=torus,
        in_specs=placed,
        out_specs=(P(None, GX, GY), P(None, GX, GY)),
        check_vma=False,
    )
```

```python
import functools

import jax
import jax.numpy as jnp
from jax import lax
from jax.experimental import pallas as pl
from jax.experimental.pallas import tpu as pltpu
from jax.sharding import Mesh
from jax.sharding import PartitionSpec as P

PICARD = 2
KRYLOV = 6
TORUS = (4, 8, 8, 2)
GX_GY = ("gx_0", "gx_1", "gy_0", "gy_1")
GX = ("gx_0", "gx_1")
GY = ("gy_0", "gy_1")


soften = 0.3
shelf_drag = 0.2
strain_floor = 0.01

MIDDLE = 17.0
RADIUS = 17.0
PIVOT_FLOOR = 2e-4
OWN = 16
SIDE = 64


def with_halo(shard, sides, width):
    for axis, dim in sides:
        size, length = (lax.axis_size(axis), shard.shape[dim])
        up = [(i, (i + 1) % size) for i in range(size - 1)]
        down = [(j, i) for i, j in up]
        last = lax.slice_in_dim(shard, length - width, length, axis=dim)
        first = lax.slice_in_dim(shard, 0, width, axis=dim)
        before = lax.ppermute(last, axis, up)
        after = lax.ppermute(first, axis, down)
        shard = jnp.concatenate([before, shard, after], axis=dim)
    return shard


def one_axis_at_a_time(shard, axes):
    return functools.reduce(lax.psum, axes, shard)


def corner_mean(array):
    return 0.25 * (array[:-1, :-1] + array[1:, :-1] + array[:-1, 1:] + array[1:, 1:])


def diff_rows(array):
    return 0.5 * (array[1:, :-1] - array[:-1, :-1] + (array[1:, 1:] - array[:-1, 1:]))


def diff_cols(array):
    return 0.5 * (array[:-1, 1:] - array[:-1, :-1] + (array[1:, 1:] - array[1:, :-1]))


def back_rows(array):
    return 0.5 * (array[:-1, :-1] + array[:-1, 1:] - array[1:, :-1] - array[1:, 1:])


def back_cols(array):
    return 0.5 * (array[:-1, :-1] + array[1:, :-1] - array[:-1, 1:] - array[1:, 1:])


def strains(padded):
    stretch_x = diff_rows(padded[0])
    stretch_y = diff_cols(padded[1])
    shear_rate = 0.5 * (diff_cols(padded[0]) + diff_rows(padded[1]))
    return (stretch_x, stretch_y, shear_rate)


def viscous_weight(rates, thick_corner, stiff_corner):
    stretch_x, stretch_y, shear_rate = rates
    square = (
        stretch_x * stretch_x
        + stretch_y * stretch_y
        + stretch_x * stretch_y
        + shear_rate * shear_rate
    )
    return 0.5 * stiff_corner * thick_corner * jnp.power(square + strain_floor, -1.0 / 3.0)


def stress_image(rates, weight, center, drag_term):
    stretch_x, stretch_y, shear_rate = rates
    stress_x = weight * (4.0 * stretch_x + 2.0 * stretch_y)
    stress_y = weight * (4.0 * stretch_y + 2.0 * stretch_x)
    shear_stress = 2.0 * weight * shear_rate
    first = back_rows(stress_x) + back_cols(shear_stress) + drag_term * center[0]
    second = back_rows(shear_stress) + back_cols(stress_y) + drag_term * center[1]
    return jnp.stack([first, second])


def apply_field(direction, weight, drag_term, projector):
    padded = with_halo(direction, ((GX, 1), (GY, 2)), 1)
    return projector * stress_image(strains(padded), weight, direction, drag_term)


def inverse_kernel(kappa_ref, out_ref):
    levels = out_ref.shape[1]
    out_ref[2 * levels :] = jnp.broadcast_to(kappa_ref[:, 0:1], (8, levels))
    above = jnp.broadcast_to(kappa_ref[:, :levels], (8, levels))
    below = jnp.broadcast_to(kappa_ref[:, 1:], (8, levels))
    lane = lax.broadcasted_iota(jnp.int32, (8, levels), 1)
    rows = lax.broadcasted_iota(jnp.int32, (levels, levels), 0)
    cols = lax.broadcasted_iota(jnp.int32, (levels, levels), 1)
    floating = 1.0 + above + below
    on_bed = jnp.where(lane == levels - 1, 1.0 + above, floating)
    for k, diagonal in enumerate((on_bed, floating)):
        low = jnp.where(lane == 0, 0.0, -above)
        high = jnp.where(lane == levels - 1, 0.0, -below)
        mid = diagonal
        right = jnp.where(rows == cols, 1.0, 0.0)
        step = 1
        while step < levels:
            back = levels - step
            down = -low / pltpu.roll(mid, step, 1)
            up = -high / pltpu.roll(mid, back, 1)
            mid = mid + down * pltpu.roll(high, step, 1) + up * pltpu.roll(low, back, 1)
            low = down * pltpu.roll(low, step, 1)
            high = up * pltpu.roll(high, back, 1)
            right = (
                right
                + down[0:1] * pltpu.roll(right, step, 1)
                + up[0:1] * pltpu.roll(right, back, 1)
            )
            step *= 2
        out_ref[k * levels : (k + 1) * levels] = right * (1.0 / mid)[0:1]


def column_inverses(kappa):
    levels = kappa.shape[0] - 1
    return pl.pallas_call(
        inverse_kernel,
        out_shape=kept(2 * levels + 8, levels),
        name="column_inverses",
    )(kappa[None])


def on_chip(array):
    return pltpu.with_memory_space_constraint(array, pltpu.VMEM)


def kept(*shape):
    return pltpu.VMEM(shape, jnp.float32)


def next_row(array):
    return pltpu.roll(array, array.shape[0] - 1, 0)


def next_col(array):
    return pltpu.roll(array, array.shape[1] - 1, 1)


def last_row(array):
    return pltpu.roll(array, 1, 0)


def last_col(array):
    return pltpu.roll(array, 1, 1)


def corner_rates(u, v):
    u_next = next_col(u)
    v_next = next_col(v)
    u_sum, u_diff = (u + u_next, u_next - u)
    v_sum, v_diff = (v + v_next, v_next - v)
    along = next_row(u_sum) - u_sum
    across = v_diff + next_row(v_diff)
    shear = u_diff + next_row(u_diff) + (next_row(v_sum) - v_sum)
    return (along, across, shear)


def stress_back(rates, half_weight):
    along, across, shear = rates
    stress_x = half_weight * (2.0 * along + across)
    stress_y = half_weight * (2.0 * across + along)
    stress_s = 0.5 * half_weight * shear
    x_before = last_col(stress_x)
    y_before = last_col(stress_y)
    s_before = last_col(stress_s)
    x_sum, s_diff = (stress_x + x_before, s_before - stress_s)
    s_sum, y_diff = (stress_s + s_before, y_before - stress_y)
    first = last_row(x_sum + s_diff) + (s_diff - x_sum)
    second = last_row(s_sum + y_diff) + (y_diff - s_sum)
    return (first, second)


def half_weights(rates, corner_product):
    along, across, shear = rates
    square = 0.25 * (along * along + across * across + along * across) + 0.0625 * shear * shear
    return corner_product * jnp.exp(jnp.log(square + strain_floor) * (-1.0 / 3.0))


def krylov_basis(u, v, drag, driving, corner_product, own_row, keep):
    free = drag > 0.0
    rates = corner_rates(u, v)
    half_weight = half_weights(rates, corner_product)
    first, second = stress_back(rates, half_weight)
    r_u = jnp.where(free, driving[0] - first - drag * u, 0.0)
    r_v = jnp.where(free, driving[1] - second - drag * v, 0.0)

    def own(array):
        return array[own_row : own_row + 8, :128]

    basis_u, basis_v = ([r_u], [r_v])
    own_basis, own_image = ([(own(r_u), own(r_v))], [])
    keep(0, r_u, r_v)
    for k in range(KRYLOV):
        b_u, b_v = (basis_u[k], basis_v[k])
        first, second = stress_back(corner_rates(b_u, b_v), half_weight)
        a_u = jnp.where(free, first, 0.0) + drag * b_u
        a_v = jnp.where(free, second, 0.0) + drag * b_v
        own_image.append((own(a_u), own(a_v)))
        if k + 1 < KRYLOV:
            scale = (1.0 if k == 0 else 2.0) / RADIUS
            n_u = scale * a_u - (scale * MIDDLE) * b_u
            n_v = scale * a_v - (scale * MIDDLE) * b_v
            if k > 0:
                n_u = n_u - basis_u[k - 1]
                n_v = n_v - basis_v[k - 1]
            basis_u.append(n_u)
            basis_v.append(n_v)
            own_basis.append((own(n_u), own(n_v)))
            keep(k + 1, n_u, n_v)
    products = []
    for i in range(KRYLOV):
        for j in range(i, KRYLOV):
            products.append(
                own_basis[i][0] * own_image[j][0] + own_basis[i][1] * own_image[j][1]
            )
    for i in range(KRYLOV):
        products.append(own_basis[i][0] * own_basis[0][0] + own_basis[i][1] * own_basis[0][1])
    return products


def write_sums(products, out_ref):
    count = out_ref.shape[0]
    lines = [jnp.sum(p, axis=0, keepdims=True) for p in products]
    lines.append(jnp.zeros((128 - len(lines), 128), jnp.float32))
    table = jnp.concatenate(lines, axis=0)
    out_ref[...] = lax.dot_general(
        jnp.ones((count, 128), jnp.float32),
        table,
        (((1,), (1,)), ((), ())),
        precision=lax.Precision.HIGHEST,
        preferred_element_type=jnp.float32,
    )


def small_solve(parts):
    sums = jnp.broadcast_to(jnp.sum(parts, axis=0, keepdims=True), (8, 128))
    at = lambda k: jnp.broadcast_to(sums[:, k : k + 1], (8, 128))
    system = {}
    k = 0
    for i in range(KRYLOV):
        for j in range(i, KRYLOV):
            system[i, j] = at(k)
            k += 1
    start = [system[i, i] for i in range(KRYLOV)]
    right = [at(k + i) for i in range(KRYLOV)]
    least = None
    for p in range(KRYLOV):
        relative = system[p, p] / start[p]
        least = relative if least is None else jnp.minimum(least, relative)
        inverse = 1.0 / system[p, p]
        for i in range(p + 1, KRYLOV):
            factor = system[p, i] * inverse
            for j in range(i, KRYLOV):
                system[i, j] = system[i, j] - factor * system[p, j]
            right[i] = right[i] - factor * right[p]
        system[p, p] = inverse
    answer = [None] * KRYLOV
    for i in reversed(range(KRYLOV)):
        value = right[i]
        for m in range(i + 1, KRYLOV):
            value = value - system[i, m] * answer[m]
        answer[i] = value * system[i, i]
    return (answer, least)


def where_am_i():
    place = []
    for axes in (GX, GY):
        major, minor = axes
        length = lax.axis_size(minor)
        place.append((lax.axis_index(major) * length + lax.axis_index(minor)))
    return (place[0], place[1], lax.axis_size(GX), lax.axis_size(GY))


def first_picard_kernel(
    mine_ref,
    left_ref,
    right_ref,
    inverses_ref,
    basis_ref,
    fixed_ref,
    sums_ref,
    own_ref,
):
    where_in = inside_grid(40, -OWN)
    take = lambda k: wide_field(k, mine_ref, left_ref, right_ref, *where_in)
    u, v, drag, thick, surface = (take(k) for k in range(5))
    transport = [take(k) for k in range(5, 11)]
    sums = [take(k) for k in range(11, 14)]
    stiff = stiffness_of(sums, *transport, inverses_ref)
    stiff = jnp.where(jnp.concatenate(where_in, axis=1), stiff, 0.0)
    own_ref[...] = stiff[OWN : OWN + 8, :128]
    t_sum = thick + next_col(thick)
    s_sum = stiff + next_col(stiff)
    corner_product = (1.0 / 64.0) * (t_sum + next_row(t_sum)) * (s_sum + next_row(s_sum))
    driving = (
        -thick * 0.5 * (next_row(surface) - last_row(surface)),
        -thick * 0.5 * (next_col(surface) - last_col(surface)),
    )
    kept = slice(OWN - 8, OWN + 16)

    def keep(k, b_u, b_v):
        basis_ref[2 * k] = b_u[kept]
        basis_ref[2 * k + 1] = b_v[kept]

    for k, value in enumerate((u, v, drag, corner_product, driving[0], driving[1])):
        fixed_ref[k] = value[kept]
    products = krylov_basis(u, v, drag, driving, corner_product, OWN, keep)
    write_sums(products, sums_ref)


def second_picard_kernel(
    parts_ref, basis_ref, fixed_ref, next_ref, velocity_ref, sums_ref, least_ref
):
    answer, least = small_solve(parts_ref[...])
    u, v = (fixed_ref[0], fixed_ref[1])
    for k in range(KRYLOV):
        scale = jnp.tile(answer[k], (3, 2))
        u = u + scale * basis_ref[2 * k]
        v = v + scale * basis_ref[2 * k + 1]
    velocity_ref[0] = u[8:16, :128]
    velocity_ref[1] = v[8:16, :128]
    least_ref[...] = least

    def keep(k, b_u, b_v):
        next_ref[2 * k] = b_u[8:16, :128]
        next_ref[2 * k + 1] = b_v[8:16, :128]

    driving = (fixed_ref[4], fixed_ref[5])
    products = krylov_basis(u, v, fixed_ref[2], driving, fixed_ref[3], 8, keep)
    write_sums(products, sums_ref)


def last_kernel(parts_ref, basis_ref, velocity_ref, least_ref, out_ref, worst_ref):
    answer, least = small_solve(parts_ref[...])
    u, v = (velocity_ref[0], velocity_ref[1])
    for k in range(KRYLOV):
        u = u + answer[k] * basis_ref[2 * k]
        v = v + answer[k] * basis_ref[2 * k + 1]
    out_ref[0] = u
    out_ref[1] = v
    worst_ref[0, 0] = jnp.min(jnp.minimum(least_ref[...], least))


def over_all(sums):
    count = lax.axis_size(GX)
    part = lax.all_to_all(sums, GY, 0, 0, tiled=True)
    part = jnp.broadcast_to(jnp.sum(part, axis=0, keepdims=True), (count, 128))
    return lax.all_to_all(part, GX, 0, 0, tiled=True)


def shifted(array, axis, by):
    size = lax.axis_size(axis)
    return lax.ppermute(array, axis, [(i, (i + by) % size) for i in range(size)])


def momentum(mine, sides, inverses):
    smem = pl.BlockSpec(memory_space=pltpu.SMEM)
    vmem = pl.BlockSpec(memory_space=pltpu.VMEM)
    gy = lax.axis_size(GY)
    basis, fixed, sums, stiffness = pl.pallas_call(
        first_picard_kernel,
        out_shape=(
            kept(2 * KRYLOV, 24, 256),
            kept(6, 24, 256),
            kept(gy, 128),
            jax.ShapeDtypeStruct((8, 128), jnp.float32),
        ),
        name="first_picard",
    )(mine, *sides, inverses)
    basis, velocity, sums, least = pl.pallas_call(
        second_picard_kernel,
        out_shape=(
            kept(2 * KRYLOV, 8, 128),
            kept(2, 8, 128),
            kept(gy, 128),
            kept(8, 128),
        ),
        name="second_picard",
    )(*map(on_chip, (over_all(sums), basis, fixed)))
    velocity, worst = pl.pallas_call(
        last_kernel,
        out_shape=(
            jax.ShapeDtypeStruct((2, 8, 128), jnp.float32),
            jax.ShapeDtypeStruct((1, 1), jnp.float32),
        ),
        out_specs=(vmem, smem),
        name="last_picard",
    )(*map(on_chip, (over_all(sums), basis, velocity, least)))
    return (velocity, worst, stiffness)


def plain_picard(velocity, thickness, stiffness, surface, drag_term, projector):
    statics = with_halo(jnp.stack([thickness, stiffness, surface]), ((GX, 1), (GY, 2)), 1)
    thick_corner = corner_mean(statics[0])
    stiff_corner = corner_mean(statics[1])
    heights = statics[2]
    driving = jnp.stack(
        [
            -thickness * 0.5 * (heights[2:, 1:-1] - heights[:-2, 1:-1]),
            -thickness * 0.5 * (heights[1:-1, 2:] - heights[1:-1, :-2]),
        ]
    )

    def total(array):
        return one_axis_at_a_time(jnp.sum(array), GX_GY)

    def picard(_, velocity):
        rates = strains(with_halo(velocity, ((GX, 1), (GY, 2)), 1))
        weight = viscous_weight(rates, thick_corner, stiff_corner)
        residual = projector * (driving - stress_image(rates, weight, velocity, drag_term))

        def krylov(_, state):
            change, residual, direction, norm_now = state
            imaged = apply_field(direction, weight, drag_term, projector)
            step_size = norm_now / total(direction * imaged)
            change = change + step_size * direction
            residual = residual - step_size * imaged
            norm_next = total(residual * residual)
            direction = residual + norm_next / norm_now * direction
            return (change, residual, direction, norm_next)

        state = (jnp.zeros_like(velocity), residual, residual, total(residual * residual))
        return velocity + lax.fori_loop(0, KRYLOV, krylov, state)[0]

    return lax.fori_loop(0, PICARD, picard, velocity)


def column_tiles(planes):
    shape = (32, 1024)
    line = lax.broadcasted_iota(jnp.int32, shape, 0)
    spot = lax.broadcasted_iota(jnp.int32, shape, 1)
    within = line & 15
    column = jnp.where(line < 16, 0, 126) + (within & 1)
    pick = jnp.where(spot == (within >> 1) * 128 + column, 1.0, 0.0)
    tiles = lax.dot_general(
        pick,
        jnp.concatenate(planes, axis=1),
        (((1,), (1,)), ((), ())),
        precision=lax.Precision.HIGHEST,
        preferred_element_type=jnp.float32,
    )
    return (tiles[:16], tiles[16:])


def pack_kernel(
    enthalpy_ref,
    speed_ref,
    thick_ref,
    height_ref,
    friction_ref,
    ice_ref,
    grounded_ref,
    code_ref,
    surface_ref,
    flux_ref,
    low_ref,
    high_ref,
    left_ref,
    right_ref,
    planes_ref,
):
    planes = [enthalpy_ref[pl.ds(x, 128, stride=8), :] for x in range(8)]
    for x in range(8):
        planes_ref[x] = planes[x]
    free = (code_ref[...] == 0) & (ice_ref[...] == 1)
    held = free | (code_ref[...] == 2)
    drag = jnp.where(grounded_ref[...] == 1, friction_ref[...], 0.0) + shelf_drag
    statics = (
        jnp.where(held, speed_ref[0], 0.0),
        jnp.where(held, speed_ref[1], 0.0),
        jnp.where(free, drag, 0.0),
        thick_ref[...],
        height_ref[...],
        speed_ref[0],
        speed_ref[1],
        ice_ref[...].astype(jnp.float32),
        grounded_ref[...].astype(jnp.float32),
        surface_ref[...],
        flux_ref[...],
    )
    for out_ref, pair in ((low_ref, (0, 1)), (high_ref, (6, 7))):
        out_ref[0:128] = planes[pair[0]]
        out_ref[128:256] = planes[pair[1]]
        for k, value in enumerate(statics):
            out_ref[256 + 8 * k : 264 + 8 * k] = value
    first, last = column_tiles(planes)
    left_ref[0:16] = first
    left_ref[16:24] = speed_ref[1]
    right_ref[0:16] = last
    right_ref[16:24] = speed_ref[1]


def line_weights(low_face, high_face):
    p_high, m_high = (jnp.maximum(high_face, 0.0), jnp.minimum(high_face, 0.0))
    p_low, m_low = (jnp.maximum(low_face, 0.0), jnp.minimum(low_face, 0.0))
    q_high, n_high = (0.25 * p_high * (1.0 - p_high), 0.25 * m_high * (1.0 + m_high))
    q_low, n_low = (0.25 * p_low * (1.0 - p_low), 0.25 * m_low * (1.0 + m_low))
    return (
        -q_low,
        q_high + (p_low + n_low),
        (q_low + m_low) - (p_high + n_high),
        -(q_high + m_high) - n_low,
        n_high,
    )


def cell_weights(c_x, c_y, before_x, after_x, before_y, after_y):
    row = lax.broadcasted_iota(jnp.int32, (8, 128), 0)
    lane = lax.broadcasted_iota(jnp.int32, (8, 128), 1)
    x_before = jnp.where(row == 0, pltpu.roll(before_x, 1, 0), pltpu.roll(c_x, 1, 0))
    x_after = jnp.where(row == 7, pltpu.roll(after_x, 7, 0), pltpu.roll(c_x, 7, 0))
    y_before = jnp.where(lane == 0, pltpu.roll(before_y, 1, 1), pltpu.roll(c_y, 1, 1))
    y_after = jnp.where(lane == 127, pltpu.roll(after_y, 127, 1), pltpu.roll(c_y, 127, 1))
    along_x = line_weights(0.5 * (x_before + c_x), 0.5 * (c_x + x_after))
    along_y = line_weights(0.5 * (y_before + c_y), 0.5 * (c_y + y_after))
    center = 1.0 + along_x[2] + along_y[2]
    return (center,) + along_x[:2] + along_x[3:] + along_y[:2] + along_y[3:]


def edge_products(weights, before_y, after_y):
    line = lax.broadcasted_iota(jnp.int32, (8, 128), 0)
    lane = lax.broadcasted_iota(jnp.int32, (8, 128), 1)
    back_2, back_1, ahead_1, ahead_2 = weights[5:]
    before = (
        jnp.where(lane == 0, back_2, 0.0),
        jnp.where(lane == 0, back_1, jnp.where(lane == 1, back_2, 0.0)),
    )
    after = (
        jnp.where(lane == 127, ahead_1, jnp.where(lane == 126, ahead_2, 0.0)),
        jnp.where(lane == 127, ahead_2, 0.0),
    )
    nothing = jnp.zeros((8, 128), jnp.float32)
    spread = []
    for x in range(8):
        at = 2 * (x % 4)
        tiles = []
        for near, far in (before, after):
            tile = jnp.where(line == at, near[x : x + 1], 0.0)
            tile = jnp.where(line == at + 1, far[x : x + 1], tile)
            tiles += [tile, nothing] if x < 4 else [nothing, tile]
        spread.append(jnp.concatenate(tiles, axis=0))
    return lax.dot_general(
        jnp.concatenate([before_y, after_y], axis=0),
        jnp.concatenate(spread, axis=1),
        (((0,), (0,)), ((), ())),
        precision=lax.Precision.HIGHEST,
        preferred_element_type=jnp.float32,
    )


def columns_of(own_ref):
    return tuple(own_ref[312 + 8 * k : 320 + 8 * k] for k in range(4))


def substep(planes, weights, edges, inverses_ref, ice, bed, surface_heat, heat_flux):
    lane = lax.broadcasted_iota(jnp.int32, (8, 128), 1)
    center, x_b2, x_b1, x_a1, x_a2, y_b2, y_b1, y_a1, y_a2 = weights
    y_b2 = jnp.where(lane < 2, 0.0, y_b2)
    y_b1 = jnp.where(lane < 1, 0.0, y_b1)
    y_a1 = jnp.where(lane > 126, 0.0, y_a1)
    y_a2 = jnp.where(lane > 125, 0.0, y_a2)
    level = lax.broadcasted_iota(jnp.int32, (128, 128), 0)
    inverses = inverses_ref[0:256]
    first_kappa = inverses_ref[256:257]
    done = []
    for x in range(0, 8, 2):
        moved, sides = ([], [])
        for r in (x, x + 1):
            at = lambda w: w[r : r + 1]
            e = planes[r + 2]
            value = at(center) * e + edges[:, r * 128 : r * 128 + 128]
            value = value + at(x_b2) * planes[r] + at(x_b1) * planes[r + 1]
            value = value + at(x_a1) * planes[r + 3] + at(x_a2) * planes[r + 4]
            value = value + at(y_b2) * pltpu.roll(e, 2, 1) + at(y_b1) * pltpu.roll(e, 1, 1)
            value = value + at(y_a1) * pltpu.roll(e, 127, 1) + at(y_a2) * pltpu.roll(e, 126, 1)
            moved.append(value)
            top = first_kappa * at(surface_heat)
            bottom = at(bed) * at(heat_flux)
            sides.append(
                value + jnp.where(level == 0, top, jnp.where(level == 127, bottom, 0.0))
            )
        solved = jnp.dot(
            inverses,
            jnp.concatenate(sides, axis=1),
            precision=lax.Precision.HIGHEST,
            preferred_element_type=jnp.float32,
        )
        for k, r in enumerate((x, x + 1)):
            mine = slice(k * 128, k * 128 + 128)
            choice = jnp.where(bed[r : r + 1] > 0.5, solved[:128, mine], solved[128:, mine])
            done.append(jnp.where(ice[r : r + 1] > 0.5, choice, moved[k]))
    return done


def inside(below_ref, above_ref, left_ref, right_ref):
    gx, gy, gx_size, gy_size = where_am_i()
    return (
        jnp.where(gx > 0, below_ref[...], 0.0),
        jnp.where(gx < gx_size - 1, above_ref[...], 0.0),
        jnp.where(gy > 0, left_ref[...], 0.0),
        jnp.where(gy < gy_size - 1, right_ref[...], 0.0),
    )


def sum_weights(inverses_ref):
    bed = jnp.sum(inverses_ref[0:128], axis=0, keepdims=True) * (1.0 / 128.0)
    shelf = jnp.sum(inverses_ref[128:256], axis=0, keepdims=True) * (1.0 / 128.0)
    return (bed, shelf, jnp.full((1, 128), 1.0 / 128.0, jnp.float32))


def level_sums(planes, inverses_ref):
    parts = sum_weights(inverses_ref)
    sums = jnp.dot(
        jnp.concatenate(parts + (jnp.zeros((5, 128), jnp.float32),), axis=0),
        jnp.concatenate(planes, axis=1),
        precision=lax.Precision.HIGHEST,
        preferred_element_type=jnp.float32,
    )
    rows = [sums[k : k + 1, x * 128 : x * 128 + 128] for k in range(3) for x in range(8)]
    return jnp.concatenate(rows, axis=0)


def tiles_kernel(planes_ref, first_ref, last_ref):
    first_ref[...], last_ref[...] = column_tiles([planes_ref[x] for x in range(8)])


def gather_kernel(
    near_below_ref,
    near_above_ref,
    own_ref,
    below_ref,
    above_ref,
    far_below_ref,
    far_above_ref,
    sums_ref,
    first_ref,
    last_ref,
    mine_ref,
    left_ref,
    right_ref,
):
    left_ref[0:16] = first_ref[...]
    right_ref[0:16] = last_ref[...]
    blocks = (below_ref, near_below_ref, own_ref, near_above_ref, above_ref)
    fields = []
    for k in range(11):
        part = slice(256 + 8 * k, 264 + 8 * k)
        fields.append(jnp.concatenate([block_ref[part] for block_ref in blocks], axis=0))
    for k in range(3):
        end, middle = (slice(8 * k, 8 * k + 8), slice(344 + 8 * k, 352 + 8 * k))
        pieces = [far_below_ref[end], below_ref[middle], sums_ref[end]]
        pieces += [above_ref[middle], far_above_ref[end]]
        fields.append(jnp.concatenate(pieces, axis=0))
    eighth = lax.broadcasted_iota(jnp.int32, (40, 128), 1) // 16
    for group in range(2):
        low, high = (None, None)
        for k, field in enumerate(fields[8 * group : 8 * group + 8]):
            mine_ref[(8 * group + k) * 40 : (8 * group + k) * 40 + 40] = field
            if k == 0:
                low, high = (field, field)
            else:
                low = jnp.where(eighth == k, pltpu.roll(field, 16 * k, 1), low)
                high = jnp.where(eighth == 7 - k, pltpu.roll(field, 128 - 16 * k, 1), high)
        part = slice(16 + 40 * group, 56 + 40 * group)
        left_ref[part] = low
        right_ref[part] = high


def inside_grid(rows, first_row):
    gx, gy, gx_size, gy_size = where_am_i()
    lane = lax.broadcasted_iota(jnp.int32, (rows, 128), 1)
    row = lax.broadcasted_iota(jnp.int32, (rows, 128), 0) + (gx * 8 + first_row)
    row_in = (row >= 0) & (row < gx_size * 8)
    col = gy + jnp.where(lane < SIDE, 1, -1)
    return (row_in, row_in & (col >= 0) & (col < gy_size))


def wide_field(k, mine_ref, left_ref, right_ref, row_in, side_in):
    part = slice(16 + 40 * (k // 8), 56 + 40 * (k // 8))
    turn = 16 * (k % 8)
    right, left = (right_ref[part], left_ref[part])
    if turn:
        right, left = (pltpu.roll(right, 128 - turn, 1), pltpu.roll(left, turn, 1))
    lane = lax.broadcasted_iota(jnp.int32, (40, 128), 1)
    side = jnp.where(lane < SIDE, right, left)
    own = mine_ref[40 * k : 40 * k + 40]
    return jnp.concatenate(
        [jnp.where(row_in, own, 0.0), jnp.where(side_in, side, 0.0)], axis=1
    )


def stiffness_of(sums, c_x, c_y, ice, bed, heat, flux, inverses_ref):
    along_x = line_weights(0.5 * (last_row(c_x) + c_x), 0.5 * (c_x + next_row(c_x)))
    along_y = line_weights(0.5 * (last_col(c_y) + c_y), 0.5 * (c_y + next_col(c_y)))
    moved = []
    for e in sums:
        value = (1.0 + along_x[2] + along_y[2]) * e
        for axis, line in ((0, along_x), (1, along_y)):
            size = e.shape[axis]
            value = value + line[0] * pltpu.roll(e, 2, axis)
            value = value + line[1] * pltpu.roll(e, 1, axis)
            value = value + line[3] * pltpu.roll(e, size - 1, axis)
            value = value + line[4] * pltpu.roll(e, size - 2, axis)
        moved.append(value)
    on_bed, on_shelf, _ = sum_weights(inverses_ref)
    top = inverses_ref[256:257, 0:1] * heat
    grounded = moved[0] + on_bed[:, 0:1] * top + on_bed[:, 127:128] * flux
    floating = moved[1] + on_shelf[:, 0:1] * top
    mean = jnp.where(ice > 0.5, jnp.where(bed > 0.5, grounded, floating), moved[2])
    return jnp.exp(mean * -soften)


def first_substep_kernel(
    enthalpy_ref,
    own_ref,
    below_ref,
    above_ref,
    left_ref,
    right_ref,
    inverses_ref,
    out_ref,
    low_ref,
    high_ref,
    weights_ref,
    sums_ref,
):
    below, above, left, right = inside(below_ref, above_ref, left_ref, right_ref)
    weights = cell_weights(
        own_ref[296:304],
        own_ref[304:312],
        below[296:304],
        above[296:304],
        left[16:],
        right[16:],
    )
    for k in range(9):
        weights_ref[k] = weights[k]
    edges = edge_products(weights, left[:16], right[:16])
    planes = [below[:128], below[128:256]]
    planes += [enthalpy_ref[x] for x in range(8)]
    planes += [above[:128], above[128:256]]
    done = substep(planes, weights, edges, inverses_ref, *columns_of(own_ref))
    for x in range(8):
        out_ref[x] = done[x]
    low_ref[0:128] = done[0]
    low_ref[128:256] = done[1]
    low_ref[256:344] = above[256:344]
    sums = level_sums(done, inverses_ref)
    low_ref[344:368] = sums
    high_ref[344:368] = sums
    sums_ref[...] = sums
    high_ref[0:128] = done[6]
    high_ref[128:256] = done[7]
    high_ref[256:344] = below[256:344]


def second_substep_kernel(
    enthalpy_ref,
    own_ref,
    below_ref,
    above_ref,
    left_ref,
    right_ref,
    weights_ref,
    inverses_ref,
    out_ref,
):
    sides = (below_ref.at[0:256], above_ref.at[0:256], left_ref.at[0:16], right_ref.at[0:16])
    below, above, left, right = inside(*sides)
    weights = tuple(weights_ref[k] for k in range(9))
    edges = edge_products(weights, left, right)
    planes = [below[:128], below[128:256]]
    planes += [enthalpy_ref[x] for x in range(8)]
    planes += [above[:128], above[128:256]]
    done = substep(planes, weights, edges, inverses_ref, *columns_of(own_ref))
    for x in range(8):
        out_ref[pl.ds(x, 128, stride=8), :] = done[x]


def beside(low, high, axis):
    return (on_chip(shifted(high, axis, 1)), on_chip(shifted(low, axis, -1)))


def shards(
    enthalpy,
    velocity_init,
    thickness,
    surface,
    friction,
    kappa,
    surface_enthalpy,
    geo_flux,
    ice_mask,
    grounded,
    boundary_code,
):
    f32 = jnp.float32
    flat = enthalpy.reshape(1024, 128)
    own, high, first, last, planes = pl.pallas_call(
        pack_kernel,
        out_shape=(
            kept(344, 128),
            kept(344, 128),
            kept(24, 128),
            kept(24, 128),
            kept(8, 128, 128),
        ),
        name="pack",
    )(
        flat,
        velocity_init,
        thickness,
        surface,
        friction,
        ice_mask,
        grounded,
        boundary_code,
        surface_enthalpy,
        geo_flux,
    )
    own = on_chip(own)
    near = beside(own, high, GX)
    near_sides = beside(first, last, GY)
    inverses = on_chip(column_inverses(kappa))
    current, low, high, weights, sums = pl.pallas_call(
        first_substep_kernel,
        out_shape=(
            kept(8, 128, 128),
            kept(368, 128),
            kept(368, 128),
            kept(9, 8, 128),
            kept(24, 128),
        ),
        name="first_substep",
    )(on_chip(planes), own, *near, *near_sides, inverses)
    around = beside(low, high, GX)
    far = (on_chip(shifted(sums, GX, 2)), on_chip(shifted(sums, GX, -2)))
    current = on_chip(current)
    first, last = pl.pallas_call(
        tiles_kernel,
        out_shape=(kept(16, 128), kept(16, 128)),
        name="tiles",
    )(current)
    mine, first, last = pl.pallas_call(
        gather_kernel,
        out_shape=(kept(560, 128), kept(96, 128), kept(96, 128)),
        name="gather",
    )(*near, own, *around, *far, *map(on_chip, (sums, first, last)))
    sides = beside(first, last, GY)
    current = pl.pallas_call(
        second_substep_kernel,
        out_shape=jax.ShapeDtypeStruct((1024, 128), f32),
        name="second_substep",
    )(current, own, *around, *sides, on_chip(weights), inverses)
    quick, worst, stiffness = momentum(on_chip(mine), sides, inverses)

    def plain():
        free_cells = (boundary_code == 0) & (ice_mask == 1)
        held_cells = free_cells | (boundary_code == 2)
        projector = free_cells.astype(f32)[None]
        drag_term = jnp.where(grounded == 1, friction, 0.0) + shelf_drag
        velocity = jnp.where(held_cells[None], velocity_init, 0.0)
        return plain_picard(
            velocity, thickness, stiffness, surface, drag_term, projector
        )

    velocity = lax.cond(worst[0, 0] > PIVOT_FLOOR, lambda: quick, plain)
    return (current.reshape(enthalpy.shape), velocity)


def solution(mesh):
    torus = Mesh(mesh.devices.reshape(TORUS), ("gx_0", "gx_1", "gy_0", "gy_1"))
    placed = (
        P(None, GX, GY),
        P(None, GX, GY),
        P(GX, GY),
        P(GX, GY),
        P(GX, GY),
        P(),
        P(GX, GY),
        P(GX, GY),
        P(GX, GY),
        P(GX, GY),
        P(GX, GY),
    )
    return jax.shard_map(
        shards,
        mesh=torus,
        in_specs=placed,
        out_specs=(P(None, GX, GY), P(None, GX, GY)),
        check_vma=False,
    )
```

```python
import functools

import jax
import jax.numpy as jnp
from jax import lax
from jax.experimental import pallas as pl
from jax.experimental.pallas import tpu as pltpu
from jax.sharding import Mesh
from jax.sharding import PartitionSpec as P

PICARD = 2
KRYLOV = 6
TORUS = (4, 8, 8, 2)
GX_GY = ("gx_0", "gx_1", "gy_0", "gy_1")
GX = ("gx_0", "gx_1")
GY = ("gy_0", "gy_1")


soften = 0.3
shelf_drag = 0.2
strain_floor = 0.01

MIDDLE = 17.0
RADIUS = 17.0
PIVOT_FLOOR = 1e-2
OWN = 16
SIDE = 64


def with_halo(shard, sides, width):
    for axis, dim in sides:
        size, length = (lax.axis_size(axis), shard.shape[dim])
        up = [(i, (i + 1) % size) for i in range(size - 1)]
        down = [(j, i) for i, j in up]
        last = lax.slice_in_dim(shard, length - width, length, axis=dim)
        first = lax.slice_in_dim(shard, 0, width, axis=dim)
        before = lax.ppermute(last, axis, up)
        after = lax.ppermute(first, axis, down)
        shard = jnp.concatenate([before, shard, after], axis=dim)
    return shard


def one_axis_at_a_time(shard, axes):
    return functools.reduce(lax.psum, axes, shard)


def corner_mean(array):
    return 0.25 * (array[:-1, :-1] + array[1:, :-1] + array[:-1, 1:] + array[1:, 1:])


def diff_rows(array):
    return 0.5 * (array[1:, :-1] - array[:-1, :-1] + (array[1:, 1:] - array[:-1, 1:]))


def diff_cols(array):
    return 0.5 * (array[:-1, 1:] - array[:-1, :-1] + (array[1:, 1:] - array[1:, :-1]))


def back_rows(array):
    return 0.5 * (array[:-1, :-1] + array[:-1, 1:] - array[1:, :-1] - array[1:, 1:])


def back_cols(array):
    return 0.5 * (array[:-1, :-1] + array[1:, :-1] - array[:-1, 1:] - array[1:, 1:])


def strains(padded):
    stretch_x = diff_rows(padded[0])
    stretch_y = diff_cols(padded[1])
    shear_rate = 0.5 * (diff_cols(padded[0]) + diff_rows(padded[1]))
    return (stretch_x, stretch_y, shear_rate)


def viscous_weight(rates, thick_corner, stiff_corner):
    stretch_x, stretch_y, shear_rate = rates
    square = (
        stretch_x * stretch_x
        + stretch_y * stretch_y
        + stretch_x * stretch_y
        + shear_rate * shear_rate
    )
    return 0.5 * stiff_corner * thick_corner * jnp.power(square + strain_floor, -1.0 / 3.0)


def stress_image(rates, weight, center, drag_term):
    stretch_x, stretch_y, shear_rate = rates
    stress_x = weight * (4.0 * stretch_x + 2.0 * stretch_y)
    stress_y = weight * (4.0 * stretch_y + 2.0 * stretch_x)
    shear_stress = 2.0 * weight * shear_rate
    first = back_rows(stress_x) + back_cols(shear_stress) + drag_term * center[0]
    second = back_rows(shear_stress) + back_cols(stress_y) + drag_term * center[1]
    return jnp.stack([first, second])


def apply_field(direction, weight, drag_term, projector):
    padded = with_halo(direction, ((GX, 1), (GY, 2)), 1)
    return projector * stress_image(strains(padded), weight, direction, drag_term)


def inverse_kernel(kappa_ref, out_ref):
    levels = out_ref.shape[1]
    out_ref[2 * levels :] = jnp.broadcast_to(kappa_ref[:, 0:1], (8, levels))
    above = jnp.broadcast_to(kappa_ref[:, :levels], (8, levels))
    below = jnp.broadcast_to(kappa_ref[:, 1:], (8, levels))
    lane = lax.broadcasted_iota(jnp.int32, (8, levels), 1)
    rows = lax.broadcasted_iota(jnp.int32, (levels, levels), 0)
    cols = lax.broadcasted_iota(jnp.int32, (levels, levels), 1)
    floating = 1.0 + above + below
    on_bed = jnp.where(lane == levels - 1, 1.0 + above, floating)
    for k, diagonal in enumerate((on_bed, floating)):
        low = jnp.where(lane == 0, 0.0, -above)
        high = jnp.where(lane == levels - 1, 0.0, -below)
        mid = diagonal
        right = jnp.where(rows == cols, 1.0, 0.0)
        step = 1
        while step < levels:
            back = levels - step
            down = -low / pltpu.roll(mid, step, 1)
            up = -high / pltpu.roll(mid, back, 1)
            mid = mid + down * pltpu.roll(high, step, 1) + up * pltpu.roll(low, back, 1)
            low = down * pltpu.roll(low, step, 1)
            high = up * pltpu.roll(high, back, 1)
            right = (
                right
                + down[0:1] * pltpu.roll(right, step, 1)
                + up[0:1] * pltpu.roll(right, back, 1)
            )
            step *= 2
        out_ref[k * levels : (k + 1) * levels] = right * (1.0 / mid)[0:1]


def column_inverses(kappa):
    levels = kappa.shape[0] - 1
    return pl.pallas_call(
        inverse_kernel,
        out_shape=kept(2 * levels + 8, levels),
        name="column_inverses",
    )(kappa[None])


def on_chip(array):
    return pltpu.with_memory_space_constraint(array, pltpu.VMEM)


def kept(*shape):
    return pltpu.VMEM(shape, jnp.float32)


def next_row(array):
    return pltpu.roll(array, array.shape[0] - 1, 0)


def next_col(array):
    return pltpu.roll(array, array.shape[1] - 1, 1)


def last_row(array):
    return pltpu.roll(array, 1, 0)


def last_col(array):
    return pltpu.roll(array, 1, 1)


def corner_rates(u, v):
    u_next = next_col(u)
    v_next = next_col(v)
    u_sum, u_diff = (u + u_next, u_next - u)
    v_sum, v_diff = (v + v_next, v_next - v)
    along = next_row(u_sum) - u_sum
    across = v_diff + next_row(v_diff)
    shear = u_diff + next_row(u_diff) + (next_row(v_sum) - v_sum)
    return (along, across, shear)


def stress_back(rates, half_weight):
    along, across, shear = rates
    stress_x = half_weight * (2.0 * along + across)
    stress_y = half_weight * (2.0 * across + along)
    stress_s = 0.5 * half_weight * shear
    x_before = last_col(stress_x)
    y_before = last_col(stress_y)
    s_before = last_col(stress_s)
    x_sum, s_diff = (stress_x + x_before, s_before - stress_s)
    s_sum, y_diff = (stress_s + s_before, y_before - stress_y)
    first = last_row(x_sum + s_diff) + (s_diff - x_sum)
    second = last_row(s_sum + y_diff) + (y_diff - s_sum)
    return (first, second)


def half_weights(rates, corner_product):
    along, across, shear = rates
    square = 0.25 * (along * along + across * across + along * across) + 0.0625 * shear * shear
    return corner_product * jnp.exp(jnp.log(square + strain_floor) * (-1.0 / 3.0))


def krylov_basis(u, v, drag, driving, corner_product, own_row, keep):
    free = drag > 0.0
    rates = corner_rates(u, v)
    half_weight = half_weights(rates, corner_product)
    first, second = stress_back(rates, half_weight)
    r_u = jnp.where(free, driving[0] - first - drag * u, 0.0)
    r_v = jnp.where(free, driving[1] - second - drag * v, 0.0)

    def own(array):
        return array[own_row : own_row + 8, :128]

    basis_u, basis_v = ([r_u], [r_v])
    own_basis, own_image = ([(own(r_u), own(r_v))], [])
    keep(0, r_u, r_v)
    for k in range(KRYLOV):
        b_u, b_v = (basis_u[k], basis_v[k])
        first, second = stress_back(corner_rates(b_u, b_v), half_weight)
        a_u = jnp.where(free, first, 0.0) + drag * b_u
        a_v = jnp.where(free, second, 0.0) + drag * b_v
        own_image.append((own(a_u), own(a_v)))
        if k + 1 < KRYLOV:
            scale = (1.0 if k == 0 else 2.0) / RADIUS
            n_u = scale * a_u - (scale * MIDDLE) * b_u
            n_v = scale * a_v - (scale * MIDDLE) * b_v
            if k > 0:
                n_u = n_u - basis_u[k - 1]
                n_v = n_v - basis_v[k - 1]
            basis_u.append(n_u)
            basis_v.append(n_v)
            own_basis.append((own(n_u), own(n_v)))
            keep(k + 1, n_u, n_v)
    products = []
    for i in range(KRYLOV):
        for j in range(i, KRYLOV):
            products.append(
                own_basis[i][0] * own_image[j][0] + own_basis[i][1] * own_image[j][1]
            )
    for i in range(KRYLOV):
        products.append(own_basis[i][0] * own_basis[0][0] + own_basis[i][1] * own_basis[0][1])
    return products


def write_sums(products, out_ref):
    count = out_ref.shape[0]
    lines = [jnp.sum(p, axis=0, keepdims=True) for p in products]
    lines.append(jnp.zeros((128 - len(lines), 128), jnp.float32))
    table = jnp.concatenate(lines, axis=0)
    out_ref[...] = lax.dot_general(
        jnp.ones((count, 128), jnp.float32),
        table,
        (((1,), (1,)), ((), ())),
        precision=lax.Precision.HIGHEST,
        preferred_element_type=jnp.float32,
    )


def small_solve(parts):
    sums = jnp.broadcast_to(jnp.sum(parts, axis=0, keepdims=True), (8, 128))
    at = lambda k: jnp.broadcast_to(sums[:, k : k + 1], (8, 128))
    system = {}
    k = 0
    for i in range(KRYLOV):
        for j in range(i, KRYLOV):
            system[i, j] = at(k)
            k += 1
    start = [system[i, i] for i in range(KRYLOV)]
    right = [at(k + i) for i in range(KRYLOV)]
    least = None
    for p in range(KRYLOV):
        relative = system[p, p] / start[p]
        least = relative if least is None else jnp.minimum(least, relative)
        inverse = 1.0 / system[p, p]
        for i in range(p + 1, KRYLOV):
            factor = system[p, i] * inverse
            for j in range(i, KRYLOV):
                system[i, j] = system[i, j] - factor * system[p, j]
            right[i] = right[i] - factor * right[p]
        system[p, p] = inverse
    answer = [None] * KRYLOV
    for i in reversed(range(KRYLOV)):
        value = right[i]
        for m in range(i + 1, KRYLOV):
            value = value - system[i, m] * answer[m]
        answer[i] = value * system[i, i]
    return (answer, least)


def where_am_i():
    place = []
    for axes in (GX, GY):
        major, minor = axes
        length = lax.axis_size(minor)
        place.append((lax.axis_index(major) * length + lax.axis_index(minor)))
    return (place[0], place[1], lax.axis_size(GX), lax.axis_size(GY))


def first_picard_kernel(
    mine_ref,
    left_ref,
    right_ref,
    inverses_ref,
    basis_ref,
    fixed_ref,
    sums_ref,
    own_ref,
):
    where_in = inside_grid(40, -OWN)
    take = lambda k: wide_field(k, mine_ref, left_ref, right_ref, *where_in)
    u, v, drag, thick, surface = (take(k) for k in range(5))
    transport = [take(k) for k in range(5, 11)]
    sums = [take(k) for k in range(11, 14)]
    stiff = stiffness_of(sums, *transport, inverses_ref)
    stiff = jnp.where(jnp.concatenate(where_in, axis=1), stiff, 0.0)
    own_ref[...] = stiff[OWN : OWN + 8, :128]
    t_sum = thick + next_col(thick)
    s_sum = stiff + next_col(stiff)
    corner_product = (1.0 / 64.0) * (t_sum + next_row(t_sum)) * (s_sum + next_row(s_sum))
    driving = (
        -thick * 0.5 * (next_row(surface) - last_row(surface)),
        -thick * 0.5 * (next_col(surface) - last_col(surface)),
    )
    kept = slice(OWN - 8, OWN + 16)

    def keep(k, b_u, b_v):
        basis_ref[2 * k] = b_u[kept]
        basis_ref[2 * k + 1] = b_v[kept]

    for k, value in enumerate((u, v, drag, corner_product, driving[0], driving[1])):
        fixed_ref[k] = value[kept]
    products = krylov_basis(u, v, drag, driving, corner_product, OWN, keep)
    write_sums(products, sums_ref)


def second_picard_kernel(
    parts_ref, basis_ref, fixed_ref, next_ref, velocity_ref, sums_ref, least_ref
):
    answer, least = small_solve(parts_ref[...])
    u, v = (fixed_ref[0], fixed_ref[1])
    for k in range(KRYLOV):
        scale = jnp.tile(answer[k], (3, 2))
        u = u + scale * basis_ref[2 * k]
        v = v + scale * basis_ref[2 * k + 1]
    velocity_ref[0] = u[8:16, :128]
    velocity_ref[1] = v[8:16, :128]
    least_ref[...] = least

    def keep(k, b_u, b_v):
        next_ref[2 * k] = b_u[8:16, :128]
        next_ref[2 * k + 1] = b_v[8:16, :128]

    driving = (fixed_ref[4], fixed_ref[5])
    products = krylov_basis(u, v, fixed_ref[2], driving, fixed_ref[3], 8, keep)
    write_sums(products, sums_ref)


def last_kernel(parts_ref, basis_ref, velocity_ref, least_ref, out_ref, worst_ref):
    answer, least = small_solve(parts_ref[...])
    u, v = (velocity_ref[0], velocity_ref[1])
    for k in range(KRYLOV):
        u = u + answer[k] * basis_ref[2 * k]
        v = v + answer[k] * basis_ref[2 * k + 1]
    out_ref[0] = u
    out_ref[1] = v
    worst_ref[0, 0] = jnp.min(jnp.minimum(least_ref[...], least))


def over_all(sums):
    count = lax.axis_size(GX)
    part = lax.all_to_all(sums, GY, 0, 0, tiled=True)
    part = jnp.broadcast_to(jnp.sum(part, axis=0, keepdims=True), (count, 128))
    return lax.all_to_all(part, GX, 0, 0, tiled=True)


def shifted(array, axis, by):
    size = lax.axis_size(axis)
    return lax.ppermute(array, axis, [(i, (i + by) % size) for i in range(size)])


def momentum(mine, sides, inverses):
    smem = pl.BlockSpec(memory_space=pltpu.SMEM)
    vmem = pl.BlockSpec(memory_space=pltpu.VMEM)
    gy = lax.axis_size(GY)
    basis, fixed, sums, stiffness = pl.pallas_call(
        first_picard_kernel,
        out_shape=(
            kept(2 * KRYLOV, 24, 256),
            kept(6, 24, 256),
            kept(gy, 128),
            jax.ShapeDtypeStruct((8, 128), jnp.float32),
        ),
        name="first_picard",
    )(mine, *sides, inverses)
    basis, velocity, sums, least = pl.pallas_call(
        second_picard_kernel,
        out_shape=(
            kept(2 * KRYLOV, 8, 128),
            kept(2, 8, 128),
            kept(gy, 128),
            kept(8, 128),
        ),
        name="second_picard",
    )(*map(on_chip, (over_all(sums), basis, fixed)))
    velocity, worst = pl.pallas_call(
        last_kernel,
        out_shape=(
            jax.ShapeDtypeStruct((2, 8, 128), jnp.float32),
            jax.ShapeDtypeStruct((1, 1), jnp.float32),
        ),
        out_specs=(vmem, smem),
        name="last_picard",
    )(*map(on_chip, (over_all(sums), basis, velocity, least)))
    return (velocity, worst, stiffness)


def plain_picard(velocity, thickness, stiffness, surface, drag_term, projector):
    statics = with_halo(jnp.stack([thickness, stiffness, surface]), ((GX, 1), (GY, 2)), 1)
    thick_corner = corner_mean(statics[0])
    stiff_corner = corner_mean(statics[1])
    heights = statics[2]
    driving = jnp.stack(
        [
            -thickness * 0.5 * (heights[2:, 1:-1] - heights[:-2, 1:-1]),
            -thickness * 0.5 * (heights[1:-1, 2:] - heights[1:-1, :-2]),
        ]
    )

    def total(array):
        return one_axis_at_a_time(jnp.sum(array), GX_GY)

    def picard(_, velocity):
        rates = strains(with_halo(velocity, ((GX, 1), (GY, 2)), 1))
        weight = viscous_weight(rates, thick_corner, stiff_corner)
        residual = projector * (driving - stress_image(rates, weight, velocity, drag_term))

        def krylov(_, state):
            change, residual, direction, norm_now = state
            imaged = apply_field(direction, weight, drag_term, projector)
            step_size = norm_now / total(direction * imaged)
            change = change + step_size * direction
            residual = residual - step_size * imaged
            norm_next = total(residual * residual)
            direction = residual + norm_next / norm_now * direction
            return (change, residual, direction, norm_next)

        state = (jnp.zeros_like(velocity), residual, residual, total(residual * residual))
        return velocity + lax.fori_loop(0, KRYLOV, krylov, state)[0]

    return lax.fori_loop(0, PICARD, picard, velocity)


def column_tiles(planes):
    shape = (32, 1024)
    line = lax.broadcasted_iota(jnp.int32, shape, 0)
    spot = lax.broadcasted_iota(jnp.int32, shape, 1)
    within = line & 15
    column = jnp.where(line < 16, 0, 126) + (within & 1)
    pick = jnp.where(spot == (within >> 1) * 128 + column, 1.0, 0.0)
    tiles = lax.dot_general(
        pick,
        jnp.concatenate(planes, axis=1),
        (((1,), (1,)), ((), ())),
        precision=lax.Precision.HIGHEST,
        preferred_element_type=jnp.float32,
    )
    return (tiles[:16], tiles[16:])


def pack_kernel(
    enthalpy_ref,
    speed_ref,
    thick_ref,
    height_ref,
    friction_ref,
    ice_ref,
    grounded_ref,
    code_ref,
    surface_ref,
    flux_ref,
    low_ref,
    high_ref,
    planes_ref,
):
    planes = [enthalpy_ref[pl.ds(x, 128, stride=8), :] for x in range(8)]
    for x in range(8):
        planes_ref[x] = planes[x]
    free = (code_ref[...] == 0) & (ice_ref[...] == 1)
    held = free | (code_ref[...] == 2)
    drag = jnp.where(grounded_ref[...] == 1, friction_ref[...], 0.0) + shelf_drag
    statics = (
        jnp.where(held, speed_ref[0], 0.0),
        jnp.where(held, speed_ref[1], 0.0),
        jnp.where(free, drag, 0.0),
        thick_ref[...],
        height_ref[...],
        speed_ref[0],
        speed_ref[1],
        ice_ref[...].astype(jnp.float32),
        grounded_ref[...].astype(jnp.float32),
        surface_ref[...],
        flux_ref[...],
    )
    for out_ref, pair in ((low_ref, (0, 1)), (high_ref, (6, 7))):
        out_ref[0:128] = planes[pair[0]]
        out_ref[128:256] = planes[pair[1]]
        for k, value in enumerate(statics):
            out_ref[256 + 8 * k : 264 + 8 * k] = value


def line_weights(low_face, high_face):
    p_high, m_high = (jnp.maximum(high_face, 0.0), jnp.minimum(high_face, 0.0))
    p_low, m_low = (jnp.maximum(low_face, 0.0), jnp.minimum(low_face, 0.0))
    q_high, n_high = (0.25 * p_high * (1.0 - p_high), 0.25 * m_high * (1.0 + m_high))
    q_low, n_low = (0.25 * p_low * (1.0 - p_low), 0.25 * m_low * (1.0 + m_low))
    return (
        -q_low,
        q_high + (p_low + n_low),
        (q_low + m_low) - (p_high + n_high),
        -(q_high + m_high) - n_low,
        n_high,
    )


def cell_weights(c_x, c_y, before_x, after_x, before_y, after_y):
    row = lax.broadcasted_iota(jnp.int32, (8, 128), 0)
    lane = lax.broadcasted_iota(jnp.int32, (8, 128), 1)
    x_before = jnp.where(row == 0, pltpu.roll(before_x, 1, 0), pltpu.roll(c_x, 1, 0))
    x_after = jnp.where(row == 7, pltpu.roll(after_x, 7, 0), pltpu.roll(c_x, 7, 0))
    y_before = jnp.where(lane == 0, pltpu.roll(before_y, 1, 1), pltpu.roll(c_y, 1, 1))
    y_after = jnp.where(lane == 127, pltpu.roll(after_y, 127, 1), pltpu.roll(c_y, 127, 1))
    along_x = line_weights(0.5 * (x_before + c_x), 0.5 * (c_x + x_after))
    along_y = line_weights(0.5 * (y_before + c_y), 0.5 * (c_y + y_after))
    center = 1.0 + along_x[2] + along_y[2]
    return (center,) + along_x[:2] + along_x[3:] + along_y[:2] + along_y[3:]


def edge_products(weights, before_y, after_y):
    line = lax.broadcasted_iota(jnp.int32, (8, 128), 0)
    lane = lax.broadcasted_iota(jnp.int32, (8, 128), 1)
    back_2, back_1, ahead_1, ahead_2 = weights[5:]
    before = (
        jnp.where(lane == 0, back_2, 0.0),
        jnp.where(lane == 0, back_1, jnp.where(lane == 1, back_2, 0.0)),
    )
    after = (
        jnp.where(lane == 127, ahead_1, jnp.where(lane == 126, ahead_2, 0.0)),
        jnp.where(lane == 127, ahead_2, 0.0),
    )
    nothing = jnp.zeros((8, 128), jnp.float32)
    spread = []
    for x in range(8):
        at = 2 * (x % 4)
        tiles = []
        for near, far in (before, after):
            tile = jnp.where(line == at, near[x : x + 1], 0.0)
            tile = jnp.where(line == at + 1, far[x : x + 1], tile)
            tiles += [tile, nothing] if x < 4 else [nothing, tile]
        spread.append(jnp.concatenate(tiles, axis=0))
    return lax.dot_general(
        jnp.concatenate([before_y, after_y], axis=0),
        jnp.concatenate(spread, axis=1),
        (((0,), (0,)), ((), ())),
        precision=lax.Precision.HIGHEST,
        preferred_element_type=jnp.float32,
    )


def columns_of(own_ref):
    return tuple(own_ref[312 + 8 * k : 320 + 8 * k] for k in range(4))


def substep(planes, weights, edges, inverses_ref, ice, bed, surface_heat, heat_flux):
    lane = lax.broadcasted_iota(jnp.int32, (8, 128), 1)
    center, x_b2, x_b1, x_a1, x_a2, y_b2, y_b1, y_a1, y_a2 = weights
    y_b2 = jnp.where(lane < 2, 0.0, y_b2)
    y_b1 = jnp.where(lane < 1, 0.0, y_b1)
    y_a1 = jnp.where(lane > 126, 0.0, y_a1)
    y_a2 = jnp.where(lane > 125, 0.0, y_a2)
    level = lax.broadcasted_iota(jnp.int32, (128, 128), 0)
    inverses = inverses_ref[0:256]
    first_kappa = inverses_ref[256:257]
    done = []
    for x in range(0, 8, 2):
        moved, sides = ([], [])
        for r in (x, x + 1):
            at = lambda w: w[r : r + 1]
            e = planes[r + 2]
            value = at(center) * e + edges[:, r * 128 : r * 128 + 128]
            value = value + at(x_b2) * planes[r] + at(x_b1) * planes[r + 1]
            value = value + at(x_a1) * planes[r + 3] + at(x_a2) * planes[r + 4]
            value = value + at(y_b2) * pltpu.roll(e, 2, 1) + at(y_b1) * pltpu.roll(e, 1, 1)
            value = value + at(y_a1) * pltpu.roll(e, 127, 1) + at(y_a2) * pltpu.roll(e, 126, 1)
            moved.append(value)
            top = first_kappa * at(surface_heat)
            bottom = at(bed) * at(heat_flux)
            sides.append(
                value + jnp.where(level == 0, top, jnp.where(level == 127, bottom, 0.0))
            )
        solved = jnp.dot(
            inverses,
            jnp.concatenate(sides, axis=1),
            precision=lax.Precision.HIGHEST,
            preferred_element_type=jnp.float32,
        )
        for k, r in enumerate((x, x + 1)):
            mine = slice(k * 128, k * 128 + 128)
            choice = jnp.where(bed[r : r + 1] > 0.5, solved[:128, mine], solved[128:, mine])
            done.append(jnp.where(ice[r : r + 1] > 0.5, choice, moved[k]))
    return done


def inside(below_ref, above_ref, left_ref, right_ref):
    gx, gy, gx_size, gy_size = where_am_i()
    return (
        jnp.where(gx > 0, below_ref[...], 0.0),
        jnp.where(gx < gx_size - 1, above_ref[...], 0.0),
        jnp.where(gy > 0, left_ref[...], 0.0),
        jnp.where(gy < gy_size - 1, right_ref[...], 0.0),
    )


def sum_weights(inverses_ref):
    bed = jnp.sum(inverses_ref[0:128], axis=0, keepdims=True) * (1.0 / 128.0)
    shelf = jnp.sum(inverses_ref[128:256], axis=0, keepdims=True) * (1.0 / 128.0)
    return (bed, shelf, jnp.full((1, 128), 1.0 / 128.0, jnp.float32))


def level_sums(planes, inverses_ref):
    parts = sum_weights(inverses_ref)
    sums = jnp.dot(
        jnp.concatenate(parts + (jnp.zeros((5, 128), jnp.float32),), axis=0),
        jnp.concatenate(planes, axis=1),
        precision=lax.Precision.HIGHEST,
        preferred_element_type=jnp.float32,
    )
    rows = [sums[k : k + 1, x * 128 : x * 128 + 128] for k in range(3) for x in range(8)]
    return jnp.concatenate(rows, axis=0)


def tiles_kernel(planes_ref, own_ref, first_ref, last_ref):
    tiles = column_tiles([planes_ref[x] for x in range(8)])
    for out_ref, tile in zip((first_ref, last_ref), tiles):
        out_ref[0:16] = tile
        out_ref[16:24] = own_ref[304:312]


def edge_columns(planes, own):
    return pl.pallas_call(
        tiles_kernel,
        out_shape=(kept(24, 128), kept(24, 128)),
        name="tiles",
    )(planes, own)


def gather_kernel(
    near_below_ref,
    near_above_ref,
    own_ref,
    below_ref,
    above_ref,
    far_below_ref,
    far_above_ref,
    sums_ref,
    first_ref,
    last_ref,
    mine_ref,
    left_ref,
    right_ref,
):
    left_ref[0:16] = first_ref[0:16]
    right_ref[0:16] = last_ref[0:16]
    blocks = (below_ref, near_below_ref, own_ref, near_above_ref, above_ref)
    fields = []
    for k in range(11):
        part = slice(256 + 8 * k, 264 + 8 * k)
        fields.append(jnp.concatenate([block_ref[part] for block_ref in blocks], axis=0))
    for k in range(3):
        end, middle = (slice(8 * k, 8 * k + 8), slice(344 + 8 * k, 352 + 8 * k))
        pieces = [far_below_ref[end], below_ref[middle], sums_ref[end]]
        pieces += [above_ref[middle], far_above_ref[end]]
        fields.append(jnp.concatenate(pieces, axis=0))
    eighth = lax.broadcasted_iota(jnp.int32, (40, 128), 1) // 16
    for group in range(2):
        low, high = (None, None)
        for k, field in enumerate(fields[8 * group : 8 * group + 8]):
            mine_ref[(8 * group + k) * 40 : (8 * group + k) * 40 + 40] = field
            if k == 0:
                low, high = (field, field)
            else:
                low = jnp.where(eighth == k, pltpu.roll(field, 16 * k, 1), low)
                high = jnp.where(eighth == 7 - k, pltpu.roll(field, 128 - 16 * k, 1), high)
        part = slice(16 + 40 * group, 56 + 40 * group)
        left_ref[part] = low
        right_ref[part] = high


def inside_grid(rows, first_row):
    gx, gy, gx_size, gy_size = where_am_i()
    lane = lax.broadcasted_iota(jnp.int32, (rows, 128), 1)
    row = lax.broadcasted_iota(jnp.int32, (rows, 128), 0) + (gx * 8 + first_row)
    row_in = (row >= 0) & (row < gx_size * 8)
    col = gy + jnp.where(lane < SIDE, 1, -1)
    return (row_in, row_in & (col >= 0) & (col < gy_size))


def wide_field(k, mine_ref, left_ref, right_ref, row_in, side_in):
    part = slice(16 + 40 * (k // 8), 56 + 40 * (k // 8))
    turn = 16 * (k % 8)
    right, left = (right_ref[part], left_ref[part])
    if turn:
        right, left = (pltpu.roll(right, 128 - turn, 1), pltpu.roll(left, turn, 1))
    lane = lax.broadcasted_iota(jnp.int32, (40, 128), 1)
    side = jnp.where(lane < SIDE, right, left)
    own = mine_ref[40 * k : 40 * k + 40]
    return jnp.concatenate(
        [jnp.where(row_in, own, 0.0), jnp.where(side_in, side, 0.0)], axis=1
    )


def stiffness_of(sums, c_x, c_y, ice, bed, heat, flux, inverses_ref):
    along_x = line_weights(0.5 * (last_row(c_x) + c_x), 0.5 * (c_x + next_row(c_x)))
    along_y = line_weights(0.5 * (last_col(c_y) + c_y), 0.5 * (c_y + next_col(c_y)))
    moved = []
    for e in sums:
        value = (1.0 + along_x[2] + along_y[2]) * e
        for axis, line in ((0, along_x), (1, along_y)):
            size = e.shape[axis]
            value = value + line[0] * pltpu.roll(e, 2, axis)
            value = value + line[1] * pltpu.roll(e, 1, axis)
            value = value + line[3] * pltpu.roll(e, size - 1, axis)
            value = value + line[4] * pltpu.roll(e, size - 2, axis)
        moved.append(value)
    on_bed, on_shelf, _ = sum_weights(inverses_ref)
    top = inverses_ref[256:257, 0:1] * heat
    grounded = moved[0] + on_bed[:, 0:1] * top + on_bed[:, 127:128] * flux
    floating = moved[1] + on_shelf[:, 0:1] * top
    mean = jnp.where(ice > 0.5, jnp.where(bed > 0.5, grounded, floating), moved[2])
    return jnp.exp(mean * -soften)


def first_substep_kernel(
    enthalpy_ref,
    own_ref,
    below_ref,
    above_ref,
    left_ref,
    right_ref,
    inverses_ref,
    out_ref,
    low_ref,
    high_ref,
    weights_ref,
    sums_ref,
):
    below, above, left, right = inside(below_ref, above_ref, left_ref, right_ref)
    weights = cell_weights(
        own_ref[296:304],
        own_ref[304:312],
        below[296:304],
        above[296:304],
        left[16:],
        right[16:],
    )
    for k in range(9):
        weights_ref[k] = weights[k]
    edges = edge_products(weights, left[:16], right[:16])
    planes = [below[:128], below[128:256]]
    planes += [enthalpy_ref[x] for x in range(8)]
    planes += [above[:128], above[128:256]]
    done = substep(planes, weights, edges, inverses_ref, *columns_of(own_ref))
    for x in range(8):
        out_ref[x] = done[x]
    low_ref[0:128] = done[0]
    low_ref[128:256] = done[1]
    low_ref[256:344] = above[256:344]
    sums = level_sums(done, inverses_ref)
    low_ref[344:368] = sums
    high_ref[344:368] = sums
    sums_ref[...] = sums
    high_ref[0:128] = done[6]
    high_ref[128:256] = done[7]
    high_ref[256:344] = below[256:344]


def second_substep_kernel(
    enthalpy_ref,
    own_ref,
    below_ref,
    above_ref,
    left_ref,
    right_ref,
    weights_ref,
    inverses_ref,
    out_ref,
):
    sides = (below_ref.at[0:256], above_ref.at[0:256], left_ref.at[0:16], right_ref.at[0:16])
    below, above, left, right = inside(*sides)
    weights = tuple(weights_ref[k] for k in range(9))
    edges = edge_products(weights, left, right)
    planes = [below[:128], below[128:256]]
    planes += [enthalpy_ref[x] for x in range(8)]
    planes += [above[:128], above[128:256]]
    done = substep(planes, weights, edges, inverses_ref, *columns_of(own_ref))
    for x in range(8):
        out_ref[pl.ds(x, 128, stride=8), :] = done[x]


def beside(low, high, axis):
    return (on_chip(shifted(high, axis, 1)), on_chip(shifted(low, axis, -1)))


def shards(
    enthalpy,
    velocity_init,
    thickness,
    surface,
    friction,
    kappa,
    surface_enthalpy,
    geo_flux,
    ice_mask,
    grounded,
    boundary_code,
):
    f32 = jnp.float32
    flat = enthalpy.reshape(1024, 128)
    own, high, planes = pl.pallas_call(
        pack_kernel,
        out_shape=(
            kept(344, 128),
            kept(344, 128),
            kept(8, 128, 128),
        ),
        name="pack",
    )(
        flat,
        velocity_init,
        thickness,
        surface,
        friction,
        ice_mask,
        grounded,
        boundary_code,
        surface_enthalpy,
        geo_flux,
    )
    own, planes = (on_chip(own), on_chip(planes))
    near = beside(own, high, GX)
    near_sides = beside(*edge_columns(planes, own), GY)
    inverses = on_chip(column_inverses(kappa))
    current, low, high, weights, sums = pl.pallas_call(
        first_substep_kernel,
        out_shape=(
            kept(8, 128, 128),
            kept(368, 128),
            kept(368, 128),
            kept(9, 8, 128),
            kept(24, 128),
        ),
        name="first_substep",
    )(planes, own, *near, *near_sides, inverses)
    around = beside(low, high, GX)
    far = (on_chip(shifted(sums, GX, 2)), on_chip(shifted(sums, GX, -2)))
    current = on_chip(current)
    first, last = edge_columns(current, own)
    mine, first, last = pl.pallas_call(
        gather_kernel,
        out_shape=(kept(560, 128), kept(96, 128), kept(96, 128)),
        name="gather",
    )(*near, own, *around, *far, *map(on_chip, (sums, first, last)))
    sides = beside(first, last, GY)
    current = pl.pallas_call(
        second_substep_kernel,
        out_shape=jax.ShapeDtypeStruct((1024, 128), f32),
        name="second_substep",
    )(current, own, *around, *sides, on_chip(weights), inverses)
    quick, worst, stiffness = momentum(on_chip(mine), sides, inverses)

    def plain():
        free_cells = (boundary_code == 0) & (ice_mask == 1)
        held_cells = free_cells | (boundary_code == 2)
        projector = free_cells.astype(f32)[None]
        drag_term = jnp.where(grounded == 1, friction, 0.0) + shelf_drag
        velocity = jnp.where(held_cells[None], velocity_init, 0.0)
        return plain_picard(
            velocity, thickness, stiffness, surface, drag_term, projector
        )

    velocity = lax.cond(worst[0, 0] > PIVOT_FLOOR, lambda: quick, plain)
    return (current.reshape(enthalpy.shape), velocity)


def solution(mesh):
    torus = Mesh(mesh.devices.reshape(TORUS), ("gx_0", "gx_1", "gy_0", "gy_1"))
    placed = (
        P(None, GX, GY),
        P(None, GX, GY),
        P(GX, GY),
        P(GX, GY),
        P(GX, GY),
        P(),
        P(GX, GY),
        P(GX, GY),
        P(GX, GY),
        P(GX, GY),
        P(GX, GY),
    )
    return jax.shard_map(
        shards,
        mesh=torus,
        in_specs=placed,
        out_specs=(P(None, GX, GY), P(None, GX, GY)),
        check_vma=False,
    )
```

```python
import functools

import jax
import jax.numpy as jnp
from jax import lax
from jax.experimental import pallas as pl
from jax.experimental.pallas import tpu as pltpu
from jax.sharding import Mesh
from jax.sharding import PartitionSpec as P

PICARD = 2
KRYLOV = 6
TORUS = (4, 8, 8, 2)
GX_GY = ("gx_0", "gx_1", "gy_0", "gy_1")
GX = ("gx_0", "gx_1")
GY = ("gy_0", "gy_1")


soften = 0.3
shelf_drag = 0.2
strain_floor = 0.01

MIDDLE = 17.0
RADIUS = 17.0
PIVOT_FLOOR = 1e-2
OWN = 16
SIDE = 64


def with_halo(shard, sides, width):
    for axis, dim in sides:
        size, length = (lax.axis_size(axis), shard.shape[dim])
        up = [(i, (i + 1) % size) for i in range(size - 1)]
        down = [(j, i) for i, j in up]
        last = lax.slice_in_dim(shard, length - width, length, axis=dim)
        first = lax.slice_in_dim(shard, 0, width, axis=dim)
        before = lax.ppermute(last, axis, up)
        after = lax.ppermute(first, axis, down)
        shard = jnp.concatenate([before, shard, after], axis=dim)
    return shard


def one_axis_at_a_time(shard, axes):
    return functools.reduce(lax.psum, axes, shard)


def corner_mean(array):
    return 0.25 * (array[:-1, :-1] + array[1:, :-1] + array[:-1, 1:] + array[1:, 1:])


def diff_rows(array):
    return 0.5 * (array[1:, :-1] - array[:-1, :-1] + (array[1:, 1:] - array[:-1, 1:]))


def diff_cols(array):
    return 0.5 * (array[:-1, 1:] - array[:-1, :-1] + (array[1:, 1:] - array[1:, :-1]))


def back_rows(array):
    return 0.5 * (array[:-1, :-1] + array[:-1, 1:] - array[1:, :-1] - array[1:, 1:])


def back_cols(array):
    return 0.5 * (array[:-1, :-1] + array[1:, :-1] - array[:-1, 1:] - array[1:, 1:])


def strains(padded):
    stretch_x = diff_rows(padded[0])
    stretch_y = diff_cols(padded[1])
    shear_rate = 0.5 * (diff_cols(padded[0]) + diff_rows(padded[1]))
    return (stretch_x, stretch_y, shear_rate)


def viscous_weight(rates, thick_corner, stiff_corner):
    stretch_x, stretch_y, shear_rate = rates
    square = (
        stretch_x * stretch_x
        + stretch_y * stretch_y
        + stretch_x * stretch_y
        + shear_rate * shear_rate
    )
    return 0.5 * stiff_corner * thick_corner * jnp.power(square + strain_floor, -1.0 / 3.0)


def stress_image(rates, weight, center, drag_term):
    stretch_x, stretch_y, shear_rate = rates
    stress_x = weight * (4.0 * stretch_x + 2.0 * stretch_y)
    stress_y = weight * (4.0 * stretch_y + 2.0 * stretch_x)
    shear_stress = 2.0 * weight * shear_rate
    first = back_rows(stress_x) + back_cols(shear_stress) + drag_term * center[0]
    second = back_rows(shear_stress) + back_cols(stress_y) + drag_term * center[1]
    return jnp.stack([first, second])


def apply_field(direction, weight, drag_term, projector):
    padded = with_halo(direction, ((GX, 1), (GY, 2)), 1)
    return projector * stress_image(strains(padded), weight, direction, drag_term)


def inverse_kernel(kappa_ref, out_ref):
    levels = out_ref.shape[1]
    out_ref[2 * levels :] = jnp.broadcast_to(kappa_ref[:, 0:1], (8, levels))
    above = jnp.broadcast_to(kappa_ref[:, :levels], (8, levels))
    below = jnp.broadcast_to(kappa_ref[:, 1:], (8, levels))
    lane = lax.broadcasted_iota(jnp.int32, (8, levels), 1)
    rows = lax.broadcasted_iota(jnp.int32, (levels, levels), 0)
    cols = lax.broadcasted_iota(jnp.int32, (levels, levels), 1)
    floating = 1.0 + above + below
    on_bed = jnp.where(lane == levels - 1, 1.0 + above, floating)
    for k, diagonal in enumerate((on_bed, floating)):
        low = jnp.where(lane == 0, 0.0, -above)
        high = jnp.where(lane == levels - 1, 0.0, -below)
        mid = diagonal
        right = jnp.where(rows == cols, 1.0, 0.0)
        step = 1
        while step < levels:
            back = levels - step
            down = -low / pltpu.roll(mid, step, 1)
            up = -high / pltpu.roll(mid, back, 1)
            mid = mid + down * pltpu.roll(high, step, 1) + up * pltpu.roll(low, back, 1)
            low = down * pltpu.roll(low, step, 1)
            high = up * pltpu.roll(high, back, 1)
            right = (
                right
                + down[0:1] * pltpu.roll(right, step, 1)
                + up[0:1] * pltpu.roll(right, back, 1)
            )
            step *= 2
        out_ref[k * levels : (k + 1) * levels] = right * (1.0 / mid)[0:1]


def column_inverses(kappa):
    levels = kappa.shape[0] - 1
    return pl.pallas_call(
        inverse_kernel,
        out_shape=kept(2 * levels + 8, levels),
        name="column_inverses",
    )(kappa[None])


def on_chip(array):
    return pltpu.with_memory_space_constraint(array, pltpu.VMEM)


def kept(*shape):
    return pltpu.VMEM(shape, jnp.float32)


def next_row(array):
    return pltpu.roll(array, array.shape[0] - 1, 0)


def next_col(array):
    return pltpu.roll(array, array.shape[1] - 1, 1)


def last_row(array):
    return pltpu.roll(array, 1, 0)


def last_col(array):
    return pltpu.roll(array, 1, 1)


def corner_rates(u, v):
    u_next = next_col(u)
    v_next = next_col(v)
    u_sum, u_diff = (u + u_next, u_next - u)
    v_sum, v_diff = (v + v_next, v_next - v)
    along = next_row(u_sum) - u_sum
    across = v_diff + next_row(v_diff)
    shear = u_diff + next_row(u_diff) + (next_row(v_sum) - v_sum)
    return (along, across, shear)


def stress_back(rates, half_weight):
    along, across, shear = rates
    stress_x = half_weight * (2.0 * along + across)
    stress_y = half_weight * (2.0 * across + along)
    stress_s = 0.5 * half_weight * shear
    x_before = last_col(stress_x)
    y_before = last_col(stress_y)
    s_before = last_col(stress_s)
    x_sum, s_diff = (stress_x + x_before, s_before - stress_s)
    s_sum, y_diff = (stress_s + s_before, y_before - stress_y)
    first = last_row(x_sum + s_diff) + (s_diff - x_sum)
    second = last_row(s_sum + y_diff) + (y_diff - s_sum)
    return (first, second)


def half_weights(rates, corner_product):
    along, across, shear = rates
    square = 0.25 * (along * along + across * across + along * across) + 0.0625 * shear * shear
    return corner_product * jnp.exp(jnp.log(square + strain_floor) * (-1.0 / 3.0))


def krylov_basis(u, v, drag, driving, corner_product, own_row, keep):
    free = drag > 0.0
    rates = corner_rates(u, v)
    half_weight = half_weights(rates, corner_product)
    first, second = stress_back(rates, half_weight)
    r_u = jnp.where(free, driving[0] - first - drag * u, 0.0)
    r_v = jnp.where(free, driving[1] - second - drag * v, 0.0)

    def own(array):
        return array[own_row : own_row + 8, :128]

    basis_u, basis_v = ([r_u], [r_v])
    own_basis, own_image = ([(own(r_u), own(r_v))], [])
    keep(0, r_u, r_v)
    for k in range(KRYLOV):
        b_u, b_v = (basis_u[k], basis_v[k])
        first, second = stress_back(corner_rates(b_u, b_v), half_weight)
        a_u = jnp.where(free, first, 0.0) + drag * b_u
        a_v = jnp.where(free, second, 0.0) + drag * b_v
        own_image.append((own(a_u), own(a_v)))
        if k + 1 < KRYLOV:
            scale = (1.0 if k == 0 else 2.0) / RADIUS
            n_u = scale * a_u - (scale * MIDDLE) * b_u
            n_v = scale * a_v - (scale * MIDDLE) * b_v
            if k > 0:
                n_u = n_u - basis_u[k - 1]
                n_v = n_v - basis_v[k - 1]
            basis_u.append(n_u)
            basis_v.append(n_v)
            own_basis.append((own(n_u), own(n_v)))
            keep(k + 1, n_u, n_v)
    products = []
    for i in range(KRYLOV):
        for j in range(i, KRYLOV):
            products.append(
                own_basis[i][0] * own_image[j][0] + own_basis[i][1] * own_image[j][1]
            )
    for i in range(KRYLOV):
        products.append(own_basis[i][0] * own_basis[0][0] + own_basis[i][1] * own_basis[0][1])
    return products


def write_sums(products, out_ref):
    count = out_ref.shape[0]
    lines = [jnp.sum(p, axis=0, keepdims=True) for p in products]
    lines.append(jnp.zeros((128 - len(lines), 128), jnp.float32))
    table = jnp.concatenate(lines, axis=0)
    out_ref[...] = lax.dot_general(
        jnp.ones((count, 128), jnp.float32),
        table,
        (((1,), (1,)), ((), ())),
        precision=lax.Precision.HIGHEST,
        preferred_element_type=jnp.float32,
    )


def small_solve(parts):
    sums = jnp.broadcast_to(jnp.sum(parts, axis=0, keepdims=True), (8, 128))
    at = lambda k: jnp.broadcast_to(sums[:, k : k + 1], (8, 128))
    system = {}
    k = 0
    for i in range(KRYLOV):
        for j in range(i, KRYLOV):
            system[i, j] = at(k)
            k += 1
    start = [system[i, i] for i in range(KRYLOV)]
    right = [at(k + i) for i in range(KRYLOV)]
    least = None
    for p in range(KRYLOV):
        relative = system[p, p] / start[p]
        least = relative if least is None else jnp.minimum(least, relative)
        inverse = 1.0 / system[p, p]
        for i in range(p + 1, KRYLOV):
            factor = system[p, i] * inverse
            for j in range(i, KRYLOV):
                system[i, j] = system[i, j] - factor * system[p, j]
            right[i] = right[i] - factor * right[p]
        system[p, p] = inverse
    answer = [None] * KRYLOV
    for i in reversed(range(KRYLOV)):
        value = right[i]
        for m in range(i + 1, KRYLOV):
            value = value - system[i, m] * answer[m]
        answer[i] = value * system[i, i]
    return (answer, least)


def where_am_i():
    place = []
    for axes in (GX, GY):
        major, minor = axes
        length = lax.axis_size(minor)
        place.append((lax.axis_index(major) * length + lax.axis_index(minor)))
    return (place[0], place[1], lax.axis_size(GX), lax.axis_size(GY))


def first_picard_kernel(
    mine_ref,
    left_ref,
    right_ref,
    inverses_ref,
    basis_ref,
    fixed_ref,
    sums_ref,
    own_ref,
):
    where_in = inside_grid(40, -OWN)
    take = lambda k: wide_field(k, mine_ref, left_ref, right_ref, *where_in)
    u, v, drag, thick, surface = (take(k) for k in range(5))
    transport = [take(k) for k in range(5, 11)]
    sums = [take(k) for k in range(11, 14)]
    stiff = stiffness_of(sums, *transport, inverses_ref)
    stiff = jnp.where(jnp.concatenate(where_in, axis=1), stiff, 0.0)
    own_ref[...] = stiff[OWN : OWN + 8, :128]
    t_sum = thick + next_col(thick)
    s_sum = stiff + next_col(stiff)
    corner_product = (1.0 / 64.0) * (t_sum + next_row(t_sum)) * (s_sum + next_row(s_sum))
    driving = (
        -thick * 0.5 * (next_row(surface) - last_row(surface)),
        -thick * 0.5 * (next_col(surface) - last_col(surface)),
    )
    kept = slice(OWN - 8, OWN + 16)

    def keep(k, b_u, b_v):
        basis_ref[2 * k] = b_u[kept]
        basis_ref[2 * k + 1] = b_v[kept]

    for k, value in enumerate((u, v, drag, corner_product, driving[0], driving[1])):
        fixed_ref[k] = value[kept]
    products = krylov_basis(u, v, drag, driving, corner_product, OWN, keep)
    write_sums(products, sums_ref)


def second_picard_kernel(
    parts_ref, basis_ref, fixed_ref, next_ref, velocity_ref, sums_ref, least_ref
):
    answer, least = small_solve(parts_ref[...])
    u, v = (fixed_ref[0], fixed_ref[1])
    for k in range(KRYLOV):
        scale = jnp.tile(answer[k], (3, 2))
        u = u + scale * basis_ref[2 * k]
        v = v + scale * basis_ref[2 * k + 1]
    velocity_ref[0] = u[8:16, :128]
    velocity_ref[1] = v[8:16, :128]
    least_ref[...] = least

    def keep(k, b_u, b_v):
        next_ref[2 * k] = b_u[8:16, :128]
        next_ref[2 * k + 1] = b_v[8:16, :128]

    driving = (fixed_ref[4], fixed_ref[5])
    products = krylov_basis(u, v, fixed_ref[2], driving, fixed_ref[3], 8, keep)
    write_sums(products, sums_ref)


def last_kernel(parts_ref, basis_ref, velocity_ref, least_ref, out_ref, worst_ref):
    answer, least = small_solve(parts_ref[...])
    u, v = (velocity_ref[0], velocity_ref[1])
    for k in range(KRYLOV):
        u = u + answer[k] * basis_ref[2 * k]
        v = v + answer[k] * basis_ref[2 * k + 1]
    out_ref[0] = u
    out_ref[1] = v
    worst_ref[0, 0] = jnp.min(jnp.minimum(least_ref[...], least))


def over_all(sums):
    count = lax.axis_size(GX)
    part = lax.all_to_all(sums, GY, 0, 0, tiled=True)
    part = jnp.broadcast_to(jnp.sum(part, axis=0, keepdims=True), (count, 128))
    return lax.all_to_all(part, GX, 0, 0, tiled=True)


def shifted(array, axis, by):
    size = lax.axis_size(axis)
    return lax.ppermute(array, axis, [(i, (i + by) % size) for i in range(size)])


def momentum(mine, sides, inverses):
    smem = pl.BlockSpec(memory_space=pltpu.SMEM)
    vmem = pl.BlockSpec(memory_space=pltpu.VMEM)
    gy = lax.axis_size(GY)
    basis, fixed, sums, stiffness = pl.pallas_call(
        first_picard_kernel,
        out_shape=(
            kept(2 * KRYLOV, 24, 256),
            kept(6, 24, 256),
            kept(gy, 128),
            jax.ShapeDtypeStruct((8, 128), jnp.float32),
        ),
        name="first_picard",
    )(mine, *sides, inverses)
    basis, velocity, sums, least = pl.pallas_call(
        second_picard_kernel,
        out_shape=(
            kept(2 * KRYLOV, 8, 128),
            kept(2, 8, 128),
            kept(gy, 128),
            kept(8, 128),
        ),
        name="second_picard",
    )(*map(on_chip, (over_all(sums), basis, fixed)))
    velocity, worst = pl.pallas_call(
        last_kernel,
        out_shape=(
            jax.ShapeDtypeStruct((2, 8, 128), jnp.float32),
            jax.ShapeDtypeStruct((1, 1), jnp.float32),
        ),
        out_specs=(vmem, smem),
        name="last_picard",
    )(*map(on_chip, (over_all(sums), basis, velocity, least)))
    return (velocity, worst, stiffness)


def plain_picard(velocity, thickness, stiffness, surface, drag_term, projector):
    statics = with_halo(jnp.stack([thickness, stiffness, surface]), ((GX, 1), (GY, 2)), 1)
    thick_corner = corner_mean(statics[0])
    stiff_corner = corner_mean(statics[1])
    heights = statics[2]
    driving = jnp.stack(
        [
            -thickness * 0.5 * (heights[2:, 1:-1] - heights[:-2, 1:-1]),
            -thickness * 0.5 * (heights[1:-1, 2:] - heights[1:-1, :-2]),
        ]
    )

    def total(array):
        return one_axis_at_a_time(jnp.sum(array), GX_GY)

    def picard(_, velocity):
        rates = strains(with_halo(velocity, ((GX, 1), (GY, 2)), 1))
        weight = viscous_weight(rates, thick_corner, stiff_corner)
        residual = projector * (driving - stress_image(rates, weight, velocity, drag_term))

        def krylov(_, state):
            change, residual, direction, norm_now = state
            imaged = apply_field(direction, weight, drag_term, projector)
            step_size = norm_now / total(direction * imaged)
            change = change + step_size * direction
            residual = residual - step_size * imaged
            norm_next = total(residual * residual)
            direction = residual + norm_next / norm_now * direction
            return (change, residual, direction, norm_next)

        state = (jnp.zeros_like(velocity), residual, residual, total(residual * residual))
        return velocity + lax.fori_loop(0, KRYLOV, krylov, state)[0]

    return lax.fori_loop(0, PICARD, picard, velocity)


def column_tiles(planes):
    shape = (32, 1024)
    line = lax.broadcasted_iota(jnp.int32, shape, 0)
    spot = lax.broadcasted_iota(jnp.int32, shape, 1)
    within = line & 15
    column = jnp.where(line < 16, 0, 126) + (within & 1)
    pick = jnp.where(spot == (within >> 1) * 128 + column, 1.0, 0.0)
    tiles = lax.dot_general(
        pick,
        jnp.concatenate(planes, axis=1),
        (((1,), (1,)), ((), ())),
        precision=lax.Precision.HIGHEST,
        preferred_element_type=jnp.float32,
    )
    return (tiles[:16], tiles[16:])


def pack_kernel(
    enthalpy_ref,
    speed_ref,
    thick_ref,
    height_ref,
    friction_ref,
    ice_ref,
    grounded_ref,
    code_ref,
    surface_ref,
    flux_ref,
    low_ref,
    high_ref,
    planes_ref,
):
    planes = [enthalpy_ref[pl.ds(x, 128, stride=8), :] for x in range(8)]
    for x in range(8):
        planes_ref[x] = planes[x]
    free = (code_ref[...] == 0) & (ice_ref[...] == 1)
    held = free | (code_ref[...] == 2)
    drag = jnp.where(grounded_ref[...] == 1, friction_ref[...], 0.0) + shelf_drag
    statics = (
        jnp.where(held, speed_ref[0], 0.0),
        jnp.where(held, speed_ref[1], 0.0),
        jnp.where(free, drag, 0.0),
        thick_ref[...],
        height_ref[...],
        speed_ref[0],
        speed_ref[1],
        ice_ref[...].astype(jnp.float32),
        grounded_ref[...].astype(jnp.float32),
        surface_ref[...],
        flux_ref[...],
    )
    for out_ref, pair in ((low_ref, (0, 1)), (high_ref, (6, 7))):
        out_ref[0:128] = planes[pair[0]]
        out_ref[128:256] = planes[pair[1]]
        for k, value in enumerate(statics):
            out_ref[256 + 8 * k : 264 + 8 * k] = value


def line_weights(low_face, high_face):
    p_high, m_high = (jnp.maximum(high_face, 0.0), jnp.minimum(high_face, 0.0))
    p_low, m_low = (jnp.maximum(low_face, 0.0), jnp.minimum(low_face, 0.0))
    q_high, n_high = (0.25 * p_high * (1.0 - p_high), 0.25 * m_high * (1.0 + m_high))
    q_low, n_low = (0.25 * p_low * (1.0 - p_low), 0.25 * m_low * (1.0 + m_low))
    return (
        -q_low,
        q_high + (p_low + n_low),
        (q_low + m_low) - (p_high + n_high),
        -(q_high + m_high) - n_low,
        n_high,
    )


def cell_weights(c_x, c_y, before_x, after_x, before_y, after_y):
    row = lax.broadcasted_iota(jnp.int32, (8, 128), 0)
    lane = lax.broadcasted_iota(jnp.int32, (8, 128), 1)
    x_before = jnp.where(row == 0, pltpu.roll(before_x, 1, 0), pltpu.roll(c_x, 1, 0))
    x_after = jnp.where(row == 7, pltpu.roll(after_x, 7, 0), pltpu.roll(c_x, 7, 0))
    y_before = jnp.where(lane == 0, pltpu.roll(before_y, 1, 1), pltpu.roll(c_y, 1, 1))
    y_after = jnp.where(lane == 127, pltpu.roll(after_y, 127, 1), pltpu.roll(c_y, 127, 1))
    along_x = line_weights(0.5 * (x_before + c_x), 0.5 * (c_x + x_after))
    along_y = line_weights(0.5 * (y_before + c_y), 0.5 * (c_y + y_after))
    center = 1.0 + along_x[2] + along_y[2]
    return (center,) + along_x[:2] + along_x[3:] + along_y[:2] + along_y[3:]


def edge_products(weights, before_y, after_y):
    line = lax.broadcasted_iota(jnp.int32, (8, 128), 0)
    lane = lax.broadcasted_iota(jnp.int32, (8, 128), 1)
    back_2, back_1, ahead_1, ahead_2 = weights[5:]
    before = (
        jnp.where(lane == 0, back_2, 0.0),
        jnp.where(lane == 0, back_1, jnp.where(lane == 1, back_2, 0.0)),
    )
    after = (
        jnp.where(lane == 127, ahead_1, jnp.where(lane == 126, ahead_2, 0.0)),
        jnp.where(lane == 127, ahead_2, 0.0),
    )
    nothing = jnp.zeros((8, 128), jnp.float32)
    spread = []
    for x in range(8):
        at = 2 * (x % 4)
        tiles = []
        for near, far in (before, after):
            tile = jnp.where(line == at, near[x : x + 1], 0.0)
            tile = jnp.where(line == at + 1, far[x : x + 1], tile)
            tiles += [tile, nothing] if x < 4 else [nothing, tile]
        spread.append(jnp.concatenate(tiles, axis=0))
    return lax.dot_general(
        jnp.concatenate([before_y, after_y], axis=0),
        jnp.concatenate(spread, axis=1),
        (((0,), (0,)), ((), ())),
        precision=lax.Precision.HIGHEST,
        preferred_element_type=jnp.float32,
    )


def columns_of(own_ref):
    return tuple(own_ref[312 + 8 * k : 320 + 8 * k] for k in range(4))


def substep(planes, weights, edges, inverses_ref, ice, bed, surface_heat, heat_flux):
    lane = lax.broadcasted_iota(jnp.int32, (8, 128), 1)
    center, x_b2, x_b1, x_a1, x_a2, y_b2, y_b1, y_a1, y_a2 = weights
    y_b2 = jnp.where(lane < 2, 0.0, y_b2)
    y_b1 = jnp.where(lane < 1, 0.0, y_b1)
    y_a1 = jnp.where(lane > 126, 0.0, y_a1)
    y_a2 = jnp.where(lane > 125, 0.0, y_a2)
    level = lax.broadcasted_iota(jnp.int32, (128, 128), 0)
    inverses = inverses_ref[0:256]
    first_kappa = inverses_ref[256:257]
    done = []
    for x in range(0, 8, 2):
        moved, sides = ([], [])
        for r in (x, x + 1):
            at = lambda w: w[r : r + 1]
            e = planes[r + 2]
            value = at(center) * e + edges[:, r * 128 : r * 128 + 128]
            value = value + at(x_b2) * planes[r] + at(x_b1) * planes[r + 1]
            value = value + at(x_a1) * planes[r + 3] + at(x_a2) * planes[r + 4]
            value = value + at(y_b2) * pltpu.roll(e, 2, 1) + at(y_b1) * pltpu.roll(e, 1, 1)
            value = value + at(y_a1) * pltpu.roll(e, 127, 1) + at(y_a2) * pltpu.roll(e, 126, 1)
            moved.append(value)
            top = first_kappa * at(surface_heat)
            bottom = at(bed) * at(heat_flux)
            sides.append(
                value + jnp.where(level == 0, top, jnp.where(level == 127, bottom, 0.0))
            )
        solved = jnp.dot(
            inverses,
            jnp.concatenate(sides, axis=1),
            precision=lax.Precision.HIGHEST,
            preferred_element_type=jnp.float32,
        )
        for k, r in enumerate((x, x + 1)):
            mine = slice(k * 128, k * 128 + 128)
            choice = jnp.where(bed[r : r + 1] > 0.5, solved[:128, mine], solved[128:, mine])
            done.append(jnp.where(ice[r : r + 1] > 0.5, choice, moved[k]))
    return done


def inside(below_ref, above_ref, left_ref, right_ref):
    gx, gy, gx_size, gy_size = where_am_i()
    return (
        jnp.where(gx > 0, below_ref[...], 0.0),
        jnp.where(gx < gx_size - 1, above_ref[...], 0.0),
        jnp.where(gy > 0, left_ref[...], 0.0),
        jnp.where(gy < gy_size - 1, right_ref[...], 0.0),
    )


def sum_weights(inverses_ref):
    bed = jnp.sum(inverses_ref[0:128], axis=0, keepdims=True) * (1.0 / 128.0)
    shelf = jnp.sum(inverses_ref[128:256], axis=0, keepdims=True) * (1.0 / 128.0)
    return (bed, shelf, jnp.full((1, 128), 1.0 / 128.0, jnp.float32))


def level_sums(planes, inverses_ref):
    parts = sum_weights(inverses_ref)
    sums = jnp.dot(
        jnp.concatenate(parts + (jnp.zeros((5, 128), jnp.float32),), axis=0),
        jnp.concatenate(planes, axis=1),
        precision=lax.Precision.HIGHEST,
        preferred_element_type=jnp.float32,
    )
    rows = [sums[k : k + 1, x * 128 : x * 128 + 128] for k in range(3) for x in range(8)]
    return jnp.concatenate(rows, axis=0)


def rows_kernel(planes_ref, below_ref, above_ref, sums_ref, low_ref, high_ref):
    for out_ref, first, behind_ref in ((low_ref, 0, above_ref), (high_ref, 6, below_ref)):
        out_ref[0:128] = planes_ref[first]
        out_ref[128:256] = planes_ref[first + 1]
        out_ref[256:344] = behind_ref[256:344]
        out_ref[344:368] = sums_ref[...]


def tiles_kernel(planes_ref, own_ref, first_ref, last_ref):
    tiles = column_tiles([planes_ref[x] for x in range(8)])
    for out_ref, tile in zip((first_ref, last_ref), tiles):
        out_ref[0:16] = tile
        out_ref[16:24] = own_ref[304:312]


def edge_columns(planes, own):
    return pl.pallas_call(
        tiles_kernel,
        out_shape=(kept(24, 128), kept(24, 128)),
        name="tiles",
    )(planes, own)


def gather_kernel(
    near_below_ref,
    near_above_ref,
    own_ref,
    below_ref,
    above_ref,
    far_below_ref,
    far_above_ref,
    sums_ref,
    first_ref,
    last_ref,
    mine_ref,
    left_ref,
    right_ref,
):
    left_ref[0:16] = first_ref[0:16]
    right_ref[0:16] = last_ref[0:16]
    blocks = (below_ref, near_below_ref, own_ref, near_above_ref, above_ref)
    fields = []
    for k in range(11):
        part = slice(256 + 8 * k, 264 + 8 * k)
        fields.append(jnp.concatenate([block_ref[part] for block_ref in blocks], axis=0))
    for k in range(3):
        end, middle = (slice(8 * k, 8 * k + 8), slice(344 + 8 * k, 352 + 8 * k))
        pieces = [far_below_ref[end], below_ref[middle], sums_ref[end]]
        pieces += [above_ref[middle], far_above_ref[end]]
        fields.append(jnp.concatenate(pieces, axis=0))
    eighth = lax.broadcasted_iota(jnp.int32, (40, 128), 1) // 16
    for group in range(2):
        low, high = (None, None)
        for k, field in enumerate(fields[8 * group : 8 * group + 8]):
            mine_ref[(8 * group + k) * 40 : (8 * group + k) * 40 + 40] = field
            if k == 0:
                low, high = (field, field)
            else:
                low = jnp.where(eighth == k, pltpu.roll(field, 16 * k, 1), low)
                high = jnp.where(eighth == 7 - k, pltpu.roll(field, 128 - 16 * k, 1), high)
        part = slice(16 + 40 * group, 56 + 40 * group)
        left_ref[part] = low
        right_ref[part] = high


def inside_grid(rows, first_row):
    gx, gy, gx_size, gy_size = where_am_i()
    lane = lax.broadcasted_iota(jnp.int32, (rows, 128), 1)
    row = lax.broadcasted_iota(jnp.int32, (rows, 128), 0) + (gx * 8 + first_row)
    row_in = (row >= 0) & (row < gx_size * 8)
    col = gy + jnp.where(lane < SIDE, 1, -1)
    return (row_in, row_in & (col >= 0) & (col < gy_size))


def wide_field(k, mine_ref, left_ref, right_ref, row_in, side_in):
    part = slice(16 + 40 * (k // 8), 56 + 40 * (k // 8))
    turn = 16 * (k % 8)
    right, left = (right_ref[part], left_ref[part])
    if turn:
        right, left = (pltpu.roll(right, 128 - turn, 1), pltpu.roll(left, turn, 1))
    lane = lax.broadcasted_iota(jnp.int32, (40, 128), 1)
    side = jnp.where(lane < SIDE, right, left)
    own = mine_ref[40 * k : 40 * k + 40]
    return jnp.concatenate(
        [jnp.where(row_in, own, 0.0), jnp.where(side_in, side, 0.0)], axis=1
    )


def stiffness_of(sums, c_x, c_y, ice, bed, heat, flux, inverses_ref):
    along_x = line_weights(0.5 * (last_row(c_x) + c_x), 0.5 * (c_x + next_row(c_x)))
    along_y = line_weights(0.5 * (last_col(c_y) + c_y), 0.5 * (c_y + next_col(c_y)))
    moved = []
    for e in sums:
        value = (1.0 + along_x[2] + along_y[2]) * e
        for axis, line in ((0, along_x), (1, along_y)):
            size = e.shape[axis]
            value = value + line[0] * pltpu.roll(e, 2, axis)
            value = value + line[1] * pltpu.roll(e, 1, axis)
            value = value + line[3] * pltpu.roll(e, size - 1, axis)
            value = value + line[4] * pltpu.roll(e, size - 2, axis)
        moved.append(value)
    on_bed, on_shelf, _ = sum_weights(inverses_ref)
    top = inverses_ref[256:257, 0:1] * heat
    grounded = moved[0] + on_bed[:, 0:1] * top + on_bed[:, 127:128] * flux
    floating = moved[1] + on_shelf[:, 0:1] * top
    mean = jnp.where(ice > 0.5, jnp.where(bed > 0.5, grounded, floating), moved[2])
    return jnp.exp(mean * -soften)


def first_substep_kernel(
    enthalpy_ref,
    own_ref,
    below_ref,
    above_ref,
    left_ref,
    right_ref,
    inverses_ref,
    out_ref,
    weights_ref,
    sums_ref,
):
    below, above, left, right = inside(below_ref, above_ref, left_ref, right_ref)
    weights = cell_weights(
        own_ref[296:304],
        own_ref[304:312],
        below[296:304],
        above[296:304],
        left[16:],
        right[16:],
    )
    for k in range(9):
        weights_ref[k] = weights[k]
    edges = edge_products(weights, left[:16], right[:16])
    planes = [below[:128], below[128:256]]
    planes += [enthalpy_ref[x] for x in range(8)]
    planes += [above[:128], above[128:256]]
    done = substep(planes, weights, edges, inverses_ref, *columns_of(own_ref))
    for x in range(8):
        out_ref[x] = done[x]
    sums_ref[...] = level_sums(done, inverses_ref)


def second_substep_kernel(
    enthalpy_ref,
    own_ref,
    below_ref,
    above_ref,
    left_ref,
    right_ref,
    weights_ref,
    inverses_ref,
    out_ref,
):
    sides = (below_ref.at[0:256], above_ref.at[0:256], left_ref.at[0:16], right_ref.at[0:16])
    below, above, left, right = inside(*sides)
    weights = tuple(weights_ref[k] for k in range(9))
    edges = edge_products(weights, left, right)
    planes = [below[:128], below[128:256]]
    planes += [enthalpy_ref[x] for x in range(8)]
    planes += [above[:128], above[128:256]]
    done = substep(planes, weights, edges, inverses_ref, *columns_of(own_ref))
    for x in range(8):
        out_ref[pl.ds(x, 128, stride=8), :] = done[x]


def beside(low, high, axis):
    return (on_chip(shifted(high, axis, 1)), on_chip(shifted(low, axis, -1)))


def shards(
    enthalpy,
    velocity_init,
    thickness,
    surface,
    friction,
    kappa,
    surface_enthalpy,
    geo_flux,
    ice_mask,
    grounded,
    boundary_code,
):
    f32 = jnp.float32
    flat = enthalpy.reshape(1024, 128)
    own, high, planes = pl.pallas_call(
        pack_kernel,
        out_shape=(
            kept(344, 128),
            kept(344, 128),
            kept(8, 128, 128),
        ),
        name="pack",
    )(
        flat,
        velocity_init,
        thickness,
        surface,
        friction,
        ice_mask,
        grounded,
        boundary_code,
        surface_enthalpy,
        geo_flux,
    )
    own, planes = (on_chip(own), on_chip(planes))
    near = beside(own, high, GX)
    near_sides = beside(*edge_columns(planes, own), GY)
    inverses = on_chip(column_inverses(kappa))
    current, weights, sums = pl.pallas_call(
        first_substep_kernel,
        out_shape=(
            kept(8, 128, 128),
            kept(9, 8, 128),
            kept(24, 128),
        ),
        name="first_substep",
    )(planes, own, *near, *near_sides, inverses)
    current, sums = (on_chip(current), on_chip(sums))
    far = (on_chip(shifted(sums, GX, 2)), on_chip(shifted(sums, GX, -2)))
    low, high = pl.pallas_call(
        rows_kernel,
        out_shape=(kept(368, 128), kept(368, 128)),
        name="rows",
    )(current, *near, sums)
    around = beside(low, high, GX)
    first, last = edge_columns(current, own)
    mine, first, last = pl.pallas_call(
        gather_kernel,
        out_shape=(kept(560, 128), kept(96, 128), kept(96, 128)),
        name="gather",
    )(*near, own, *around, *far, sums, *map(on_chip, (first, last)))
    sides = beside(first, last, GY)
    current = pl.pallas_call(
        second_substep_kernel,
        out_shape=jax.ShapeDtypeStruct((1024, 128), f32),
        name="second_substep",
    )(current, own, *around, *sides, on_chip(weights), inverses)
    quick, worst, stiffness = momentum(on_chip(mine), sides, inverses)

    def plain():
        free_cells = (boundary_code == 0) & (ice_mask == 1)
        held_cells = free_cells | (boundary_code == 2)
        projector = free_cells.astype(f32)[None]
        drag_term = jnp.where(grounded == 1, friction, 0.0) + shelf_drag
        velocity = jnp.where(held_cells[None], velocity_init, 0.0)
        return plain_picard(
            velocity, thickness, stiffness, surface, drag_term, projector
        )

    velocity = lax.cond(worst[0, 0] > PIVOT_FLOOR, lambda: quick, plain)
    return (current.reshape(enthalpy.shape), velocity)


def solution(mesh):
    torus = Mesh(mesh.devices.reshape(TORUS), ("gx_0", "gx_1", "gy_0", "gy_1"))
    placed = (
        P(None, GX, GY),
        P(None, GX, GY),
        P(GX, GY),
        P(GX, GY),
        P(GX, GY),
        P(),
        P(GX, GY),
        P(GX, GY),
        P(GX, GY),
        P(GX, GY),
        P(GX, GY),
    )
    return jax.shard_map(
        shards,
        mesh=torus,
        in_specs=placed,
        out_specs=(P(None, GX, GY), P(None, GX, GY)),
        check_vma=False,
    )
```
